32 devices in a mesh: groups: 2 (over x), dp: 16 (over z, y, core).
Axes of the slice: x: 2, y: 2, z: 4, core: 2. Of those that a mesh axis runs over, the one named last changes fastest.
Arguments:
- tokens: bfloat16 [24576, 1024], P(('groups', 'dp')), parts along dimension 0, may hold values from -6 to 6
- token_mask: int32 [32, 768], P(('groups', 'dp')), parts along dimension 0, may hold values 0 or 1
- span_ids: int32 [32, 768], P(('groups', 'dp')), parts along dimension 0, may hold values from 0 to 191, never falling along the last dimension, each value on 1 to 8 neighbouring positions
- norm_gain: float32 [1024], replicated, may hold values from 0.1 to 1.9
- norm_shift: float32 [1024], replicated, may hold values from -3 to 3
- w_up: bfloat16 [1024, 4096], P(None, 'dp'), may hold values from -0.1875 to 0.1875
- b_up: float32 [4096], replicated, may hold values from -3 to 3
- w_down: bfloat16 [4096, 1024], P(None, 'dp'), may hold values from -0.09375 to 0.09375
Outputs:
- whitened: float32 [6144, 1024], P(('groups', 'dp')), parts along dimension 0
The draws below stay inside these ranges and needn't reach their ends.
There are 2 independent parts, one for each index of `groups`. The reference program is written for one: setup_inputs(seed, part) draws one part's arguments, and reference() takes and returns one part's arrays. A program takes and returns all parts, laid end to end along the dimension named above; an argument that names none is the same for every part. Nothing has to cross between parts.
Inputs may be any that keep to these rules, and one draw needn't show every extreme that they name: `span_ids`: in each row the span numbers never fall, every span 0 to 191 holds 1 to 8 tokens, and one holds exactly 8.
All inputs are finite; a program needn't handle non-finite values. No bound on the sum of `token_mask` on one device may be relied on, other than what follows from the above.
Results may differ from the reference program's by a relative error of at most 0.0095.
Values may be sent and summed in bfloat16 or wider, within the bound.
A program may use at most 128 MiB of HBM per device.

```python
import math
import jax
import jax.numpy as jnp
import numpy as np
from jax import lax

D = 1024
FF = 4096
TOK_DEV = 768
MOST = 8
SEG_DEV = 192
TOKENS = 12288
ROWS = 3072
N_DP = 16


def with_ends(entries, key, least, largest):
    extent = entries.shape
    spot = [jax.random.randint(jax.random.fold_in(key, axis), (), 0, extent[axis]) for axis in range(len(extent))]
    entries = entries.at[tuple(spot)].set(least)
    longest = extent.index(max(extent))
    spot[longest] = (spot[longest] + 1) % extent[longest]
    return entries.at[tuple(spot)].set(largest)


def shard_levels(key, shape, split, least, high):
    level = 1.0
    for position, blocks in split:
        draws = jax.random.uniform(jax.random.fold_in(jax.random.fold_in(key, 6), position), (blocks,), jnp.float32, least / len(split), high / len(split))
        level = level * jnp.repeat(jnp.exp(draws), shape[position] // blocks).reshape((-1,) + (1,) * (len(shape) - 1 - position))
    return level


def profile(amount, total, reach, lean):
    weights = [(1 << 20) // math.isqrt(standing ** lean) + 1 for standing in range(2, amount + 1)]
    spare, holding = total - reach - (amount - 1), [1] * (amount - 1)
    while spare > 0:
        free = [i for i in range(amount - 1) if holding[i] < reach]
        mass, left = sum([weights[i] for i in free]), spare
        for i in free:
            extra = min(reach - holding[i], max(1, left * weights[i] // mass), spare)
            holding[i] = holding[i] + extra
            spare = spare - extra
    return np.array([reach] + holding)


def uneven_parts(rng, count, total, reach, lean):
    if count == 2:
        one = jax.random.randint(rng, (), max(1, total - reach), min(reach, total - 1) + 1)
        return jnp.stack([one, total - one])
    sizes = jnp.asarray(profile(count, total, reach, lean), jnp.int32)
    pairs = (count - 1) // 2
    giver, receiver = sizes[1:1 + 2 * pairs:2], sizes[2:2 + 2 * pairs:2]
    margin = jnp.minimum(giver - 1, reach - receiver)
    shifted = jax.random.randint(jax.random.fold_in(rng, 1), (pairs,), 0, 1 << 20) % (margin + 1)
    sizes = sizes.at[1:1 + 2 * pairs:2].set(giver - shifted).at[2:2 + 2 * pairs:2].set(receiver + shifted)
    return sizes[jax.random.permutation(jax.random.fold_in(rng, 2), count)]


def normal_values(stream_key, shape, scale, limit, split=(), kind=jnp.bfloat16):
    factor_of = shard_levels(stream_key, shape, split, -0.22, 0.18) if split else 1.0
    drawn = jax.random.normal(stream_key, shape, jnp.float32) * scale * factor_of
    return jnp.minimum(jnp.maximum(drawn, -limit), limit).astype(kind)


def setup_inputs(seed: int = 0, part: int = 0) -> dict:
    keys = jax.random.split(jax.random.key(seed), 9)
    own_keys = jax.random.split(jax.random.fold_in(keys[8], part), 9)
    return {
        "tokens": normal_values(own_keys[0], (TOKENS, D), 1.0, 6.0, ((0, 16),)),
        "token_mask": with_ends((jax.random.randint(own_keys[1], (N_DP, TOK_DEV), 0, 8) < 7).astype(jnp.int32), jax.random.fold_in(own_keys[1], 1), 0, 1),
        "span_ids": jax.vmap(lambda own: jnp.searchsorted(jnp.cumsum(uneven_parts(own, SEG_DEV, TOK_DEV, MOST, 0)), jnp.arange(TOK_DEV), side="right"))(jax.random.split(own_keys[2], N_DP)).reshape((N_DP, TOK_DEV)).astype(jnp.int32),
        "norm_gain": jnp.clip(1.0 + 0.18 * jax.random.normal(keys[3], (D,), jnp.float32), 0.1, 1.9),
        "norm_shift": normal_values(keys[4], (D,), 0.5, 3.0, (), jnp.float32),
        "w_up": normal_values(keys[5], (D, FF), D ** -0.5, 0.1875, ((1, 16),)),
        "b_up": normal_values(keys[6], (FF,), 0.5, 3.0, (), jnp.float32),
        "w_down": normal_values(keys[7], (FF, D), FF ** -0.5, 0.09375, ((1, 16),)),
    }


def shard_pass(tokens_shard, mask_row, span_row, norm_gain, norm_shift, w_up, b_up, w_down):
    values = tokens_shard.astype(jnp.float32)
    center = lax.optimization_barrier(jnp.mean(values, axis=1, keepdims=True))
    spread = lax.optimization_barrier(jnp.mean((values - center) ** 2, axis=1, keepdims=True))
    normed = ((values - center) * lax.rsqrt(spread + 1e-05) * norm_gain + norm_shift).astype(jnp.bfloat16)
    before = jnp.dot(normed.astype(jnp.float32), w_up.astype(jnp.float32), preferred_element_type=jnp.float32) + b_up
    hidden = jax.nn.gelu(before, approximate=False).astype(jnp.bfloat16)
    block_out = (values + jnp.dot(hidden.astype(jnp.float32), w_down.astype(jnp.float32), preferred_element_type=jnp.float32)).astype(jnp.bfloat16)
    labels = jnp.arange(SEG_DEV, dtype=jnp.int32)[:, None]
    select = (span_row[None, :] == labels) & (mask_row[None, :] == 1)
    sums = jnp.dot(select.astype(jnp.bfloat16).astype(jnp.float32), block_out.astype(jnp.float32), preferred_element_type=jnp.float32)
    counts = lax.optimization_barrier(jnp.sum(select.astype(jnp.float32), axis=1))
    return (sums / jnp.maximum(counts, 1.0)[:, None]).astype(jnp.bfloat16)

def reference(tokens, token_mask, span_ids, norm_gain, norm_shift, w_up, b_up, w_down):
    shards = tokens.reshape(N_DP, TOK_DEV, D)

    def one_shard(items):
        return shard_pass(items[0], items[1], items[2], norm_gain, norm_shift, w_up, b_up, w_down)
    pooled = lax.map(one_shard, (shards, token_mask, span_ids)).reshape(ROWS, D)
    gram = jnp.dot(pooled.T.astype(jnp.float32), pooled.astype(jnp.float32), preferred_element_type=jnp.float32)
    lower = jnp.linalg.cholesky(gram)
    solved = jax.scipy.linalg.solve_triangular(lower, pooled.astype(jnp.float32).T, lower=True)
    return math.sqrt(ROWS) * solved.T
```

```python
import functools
import math

import jax
import jax.numpy as jnp
from jax import lax
from jax.experimental import pallas as pl
from jax.experimental.pallas import tpu as pltpu
from jax.sharding import PartitionSpec as P

SEG_DEV = 192
BLOCK = 128
HIGHEST = lax.Precision.HIGHEST


def inverse_block(src, dst):
    lane = lax.broadcasted_iota(jnp.int32, (8, BLOCK), 1)
    sub = lax.broadcasted_iota(jnp.int32, (8, BLOCK), 0)
    groups = BLOCK // 8
    held = [src[8 * q : 8 * q + 8, :BLOCK] for q in range(groups)]

    def column(block, c):
        return jnp.broadcast_to(block[:, c : c + 1], (8, BLOCK))

    def row(block, r):
        return jnp.broadcast_to(block[r : r + 1, :], (8, BLOCK))

    for p in range(groups):
        at = 8 * p
        inside = (lane >= at) & (lane < at + 8)
        raw = held[p]
        cols = [column(raw, at + c) for c in range(8)]
        work = jnp.where(inside, jnp.where(lane - at == sub, 1.0, 0.0), raw)
        done = jnp.zeros((8, BLOCK), jnp.float32)
        for j in range(8):
            here = sub == j
            pivot = row(cols[j], j)
            inv = 1.0 / pivot
            done = jnp.where(here, work * lax.rsqrt(pivot), done)
            scaled = row(work, j) * inv
            work = jnp.where(here, scaled, work - cols[j] * scaled)
            for c in range(j + 1, 8):
                scaled = row(cols[c], j) * inv
                cols[c] = jnp.where(here, scaled, cols[c] - cols[j] * scaled)
        dst[at : at + 8, :] = jnp.where(lane <= at + sub, done, 0.0)
        rows = [row(work, c) for c in range(8)]
        for q in range(p + 1, groups):
            total = jnp.where(inside, 0.0, held[q])
            for c in range(8):
                total = total - column(held[q], at + c) * rows[c]
            held[q] = total


def whiten_kernel(scale, first_ref, cross_ref, last_ref, rows_ref, out_ref, a, panel, inv):
    half = first_ref.shape[0]
    n = 2 * half
    extra = rows_ref.shape[1]
    a[:half, :half] = first_ref[...]
    a[:half, half:n] = cross_ref[...]
    a[half:, :half] = jnp.zeros((half, half), jnp.float32)
    a[half:, half:n] = last_ref[...]
    a[:, n:] = jnp.zeros((n, a.shape[1] - n), jnp.float32)
    a[:, n : n + extra] = rows_ref[...]
    blocks = n // BLOCK

    def step(k, carry):
        lo = pl.multiple_of(k * BLOCK, BLOCK)
        panel[:, :BLOCK] = a[pl.ds(lo, BLOCK), pl.ds(lo, BLOCK)]
        inverse_block(panel, inv)
        panel[...] = jnp.dot(
            inv[...], a[pl.ds(lo, BLOCK), :], preferred_element_type=jnp.float32, precision=HIGHEST
        )
        out_ref[pl.ds(lo, BLOCK), :] = panel[:, n : n + extra] * scale

        for first in range(0, blocks, 2):
            start = first * BLOCK

            def trail(i, carry, start=start):
                hi = pl.multiple_of(i * BLOCK, BLOCK)
                left = panel[:, pl.ds(hi, BLOCK)].T
                a[pl.ds(hi, BLOCK), start:] -= jnp.dot(
                    left, panel[:, start:], preferred_element_type=jnp.float32, precision=HIGHEST
                )
                return carry

            lax.fori_loop(jnp.maximum(k + 1, first), min(first + 2, blocks), trail, 0)
        return carry

    lax.fori_loop(0, blocks, step, 0)


def whiten(gram, rows_t, scale):
    n, extra = rows_t.shape
    wide = n + (extra + BLOCK - 1) // BLOCK * BLOCK
    return pl.pallas_call(
        functools.partial(whiten_kernel, scale),
        out_shape=jax.ShapeDtypeStruct((n, extra), jnp.float32),
        in_specs=[pl.BlockSpec(memory_space=pltpu.VMEM)] * 4,
        out_specs=pl.BlockSpec(memory_space=pltpu.VMEM),
        scratch_shapes=[
            pltpu.VMEM((n, wide), jnp.float32),
            pltpu.VMEM((BLOCK, wide), jnp.float32),
            pltpu.VMEM((BLOCK, BLOCK), jnp.float32),
        ],
        compiler_params=pltpu.CompilerParams(vmem_limit_bytes=32 << 20),
    )(*gram, rows_t)


def ring_kernel(chips, count, fused, *refs):
    if fused:
        normed, bias, up, down, hidden, down_out, up_out = refs[:7]
        ins, outs, refs = (up, down), (up_out, down_out), refs[7:]
    else:
        ins, outs, refs = refs[:count], refs[count : 2 * count], refs[2 * count :]
    ring_send, ring_recv, core_send, core_recv, own_sem = refs
    me = lax.axis_index("dp")
    core, chip = lax.rem(me, 2), me // 2
    half = chips // 2
    odd = lax.rem(chip, 2)
    place = (1 - odd) * (chip // 2) + odd * (chips - 1 - chip // 2)
    turn = 1 - 2 * core
    partner = me + turn

    def device(q):
        q = lax.rem(q + 2 * chips, chips)
        back = q // half
        return 2 * ((1 - back) * 2 * q + back * (2 * (chips - 1 - q) + 1)) + core

    ahead, behind = device(place + turn), device(place - turn)
    barrier = pltpu.get_barrier_semaphore()
    for other in (ahead, behind, partner):
        pl.semaphore_signal(
            barrier, inc=1, device_id={"dp": other}, device_id_type=pl.DeviceIdType.MESH
        )
    pl.semaphore_wait(barrier, 3)

    steps = (half, chips - 1 - half)
    started, across = [], []

    def send(a, source, slot, way, step):
        copy = pltpu.make_async_remote_copy(
            src_ref=source,
            dst_ref=outs[a].at[slot],
            send_sem=ring_send.at[a, way, step],
            recv_sem=ring_recv.at[a, way, step],
            device_id={"dp": (ahead, behind)[way]},
            device_id_type=pl.DeviceIdType.MESH,
        )
        copy.start()
        started.append(copy)
        return copy

    def share(a, source, slot, index):
        copy = pltpu.make_async_remote_copy(
            src_ref=source,
            dst_ref=outs[a].at[slot],
            send_sem=core_send.at[a, index],
            recv_sem=core_recv.at[a, index],
            device_id={"dp": partner},
            device_id_type=pl.DeviceIdType.MESH,
        )
        copy.start()
        if fused and a == 0:
            first[index] = copy
        else:
            across.append(copy)

    def compute(slot, block):
        size = block.shape[0]
        columns = pl.ds(pl.multiple_of(slot * size, BLOCK), size)
        tile = normed.shape[0] // 3

        def part(t, carry):
            at = pl.ds(pl.multiple_of(t * tile, tile), tile)
            before = lax.dot_general(
                normed[at, :],
                block[...],
                (((1,), (1,)), ((), ())),
                preferred_element_type=jnp.float32,
            )
            before = before + bias[slot]
            hidden[at, columns] = (
                0.5 * before * (1.0 + lax.erf(before * math.sqrt(0.5)))
            ).astype(hidden.dtype)
            return carry

        lax.fori_loop(0, 3, part, 0)

    first = {}

    def partner_block(index, step, way):
        first[index].wait_recv()
        slot = partner
        if index:
            slot = device(place + (1 + step) * turn * (1 - 2 * way)) + turn
        compute(slot, outs[0].at[slot])

    flying, local = {}, []
    for a in range(count):
        for way in range(2):
            flying[a, way] = send(a, ins[a], me, way, 0)
        share(a, ins[a], me, 0)
        if not (fused and a == 0):
            local.append(pltpu.make_async_copy(ins[a], outs[a].at[me], own_sem.at[a]))
            local[-1].start()
    if fused:
        compute(me, ins[0])
    for step in range(half):
        landed = []
        if fused:
            if step == 0:
                partner_block(0, 0, 0)
            for way in range(2):
                if 0 < step <= steps[way]:
                    partner_block(way * half + step, step - 1, way)
        for a in range(count):
            for way in range(2):
                if step >= steps[way]:
                    continue
                flying[a, way].wait_recv()
                slot = device(place - (1 + step) * turn * (1 - 2 * way))
                block = outs[a].at[slot]
                if step + 1 < steps[way]:
                    flying[a, way] = send(a, block, slot, way, step + 1)
                share(a, block, slot, 1 + way * half + step)
                if fused and a == 0:
                    landed.append((slot, block))
        for slot, block in landed:
            compute(slot, block)
    if fused:
        for way in range(2):
            if steps[way] == half:
                partner_block(way * half + half, half - 1, way)
        for copy in first.values():
            copy.wait_send()
    for copy in local:
        copy.wait()
    for copy in started:
        copy.wait_send()
    for copy in across:
        copy.wait()


def ring_gather(blocks, collective_id):
    devices = lax.axis_size("dp")
    chips, count = devices // 2, len(blocks)
    dma = pltpu.SemaphoreType.DMA
    return pl.pallas_call(
        functools.partial(ring_kernel, chips, count, False),
        out_shape=[jax.ShapeDtypeStruct((devices,) + b.shape, b.dtype) for b in blocks],
        in_specs=[pl.BlockSpec(memory_space=pl.ANY)] * count,
        out_specs=[pl.BlockSpec(memory_space=pl.ANY)] * count,
        scratch_shapes=[
            dma((count, 2, chips // 2)),
            dma((count, 2, chips // 2)),
            dma((count, chips)),
            dma((count, chips)),
            dma((count,)),
        ],
        compiler_params=pltpu.CompilerParams(collective_id=collective_id, has_side_effects=True),
    )(*blocks)


def ring_up(normed, bias, up, down, collective_id):
    devices = lax.axis_size("dp")
    chips = devices // 2
    dma = pltpu.SemaphoreType.DMA
    whole = pl.BlockSpec(memory_space=pltpu.VMEM)
    apart = pl.BlockSpec(memory_space=pl.ANY)
    return pl.pallas_call(
        functools.partial(ring_kernel, chips, 2, True),
        out_shape=[
            jax.ShapeDtypeStruct((normed.shape[0], devices * up.shape[0]), normed.dtype),
            jax.ShapeDtypeStruct((devices,) + down.shape, down.dtype),
        ],
        in_specs=[whole, whole, whole, apart],
        out_specs=[whole, apart],
        scratch_shapes=[
            pltpu.VMEM((devices,) + up.shape, up.dtype),
            dma((2, 2, chips // 2)),
            dma((2, 2, chips // 2)),
            dma((2, chips)),
            dma((2, chips)),
            dma((2,)),
        ],
        compiler_params=pltpu.CompilerParams(
            collective_id=collective_id, has_side_effects=True, vmem_limit_bytes=40 << 20
        ),
    )(normed, bias.reshape(devices, 1, -1), up, down)


def spread(block, r):
    return jnp.broadcast_to(block[r : r + 1, :], (8, BLOCK))


def strip_factor(a, dst, base, groups):
    lane = lax.broadcasted_iota(jnp.int32, (8, BLOCK), 1)
    sub = lax.broadcasted_iota(jnp.int32, (8, BLOCK), 0)
    h = [a[base + 8 * q : base + 8 * q + 8, :] for q in range(groups)]

    def fetch(p):
        return {
            (c, q): jnp.broadcast_to(
                h[q][:, base + 8 * p + c : base + 8 * p + c + 1], (8, BLOCK)
            )
            for q in range(p, groups)
            for c in range(8)
        }

    cols = fetch(0)
    for p in range(groups):
        more = p + 1 < groups
        following = fetch(p + 1) if more else {}
        at = base + 8 * p
        inside = (lane >= at) & (lane < at + 8)
        work = jnp.where(inside, jnp.where(lane - at == sub, 1.0, 0.0), h[p])
        for q in range(p + 1, groups):
            h[q] = jnp.where(inside, 0.0, h[q])
        pivots = jnp.zeros((8, BLOCK), jnp.float32)
        for j in range(8):
            pivot = spread(cols[j, p], j)
            inv = 1.0 / pivot
            pivots = jnp.where(sub == j, pivot, pivots)
            for c in range(j + 1, 8):
                m = spread(cols[j, p], c) * inv
                for q in range(p, groups):
                    cols[c, q] = cols[c, q] - cols[j, q] * m
            if more:
                for c in range(8):
                    m = spread(cols[j, p + 1], c) * inv
                    for q in range(p + 1, groups):
                        following[c, q] = following[c, q] - cols[j, q] * m
            scaled = spread(work, j) * inv
            if j < 7:
                work = work - jnp.where(sub > j, cols[j, p], 0.0) * scaled
            for q in range(p + 1, groups):
                h[q] = h[q] - cols[j, q] * scaled
        dst[at : at + 8, :] = work * lax.rsqrt(pivots)
        cols = following


def over_rows(left, right, precision=None):
    return lax.dot_general(
        left,
        right,
        (((0,), (0,)), ((), ())),
        preferred_element_type=jnp.float32,
        precision=precision,
    )


def inverse_factor(a, dst):
    size = 32
    for base in range(0, BLOCK, size):
        strip_factor(a, dst, base, size // 8)
        lo = base + size
        if lo < BLOCK:
            rows = dst[base:lo, :]
            r = lax.broadcasted_iota(jnp.int32, (size, BLOCK), 0) + base
            c = lax.broadcasted_iota(jnp.int32, (size, BLOCK), 1)
            drop = over_rows(rows, jnp.where((c > r) & (c < lo), 0.0, rows), HIGHEST)
            c = lax.broadcasted_iota(jnp.int32, (BLOCK - lo, BLOCK), 1)
            a[lo:, :] = jnp.where((c >= base) & (c < lo), 0.0, a[lo:, :]) - drop[lo:, :]
    r = lax.broadcasted_iota(jnp.int32, (BLOCK, BLOCK), 0)
    c = lax.broadcasted_iota(jnp.int32, (BLOCK, BLOCK), 1)
    dst[...] = jnp.where(c <= r, dst[...], 0.0)


def split(x):
    high = x.astype(jnp.bfloat16)
    return high, (x - high.astype(jnp.float32)).astype(jnp.bfloat16)


def whiten_ring_kernel(
    chips, scale, own, out, land, linv, column, a, w, ring_send, ring_recv, core_send, core_recv
):
    me = lax.axis_index("dp")
    core, chip = lax.rem(me, 2), me // 2
    half = chips // 2
    odd = lax.rem(chip, 2)
    place = (1 - odd) * (chip // 2) + odd * (chips - 1 - chip // 2)
    turn = 1 - 2 * core
    partner = me + turn
    steps = (half, chips - 1 - half)
    chunks = own.shape[1] // BLOCK
    rows = own.shape[0]
    total = 2 * chips * rows

    def device(q):
        q = lax.rem(q + 2 * chips, chips)
        back = q // half
        return 2 * ((1 - back) * 2 * q + back * (2 * (chips - 1 - q) + 1)) + core

    beside = (device(place + turn), device(place - turn))
    barrier = pltpu.get_barrier_semaphore()
    for other in (*beside, partner):
        pl.semaphore_signal(
            barrier, inc=1, device_id={"dp": other}, device_id_type=pl.DeviceIdType.MESH
        )

    def came(way, hop):
        return device(place - (1 + hop) * turn * (1 - 2 * way))

    def ring(c, way, hop):
        slot = me if hop == 0 else came(way, hop - 1)
        return pltpu.make_async_remote_copy(
            src_ref=land.at[c, slot],
            dst_ref=land.at[c, slot],
            send_sem=ring_send.at[c, way, hop],
            recv_sem=ring_recv.at[c, way, hop],
            device_id={"dp": beside[way]},
            device_id_type=pl.DeviceIdType.MESH,
        )

    def share(c, index, slot):
        return pltpu.make_async_remote_copy(
            src_ref=land.at[c, slot],
            dst_ref=land.at[c, slot],
            send_sem=core_send.at[c, index],
            recv_sem=core_recv.at[c, index],
            device_id={"dp": partner},
            device_id_type=pl.DeviceIdType.MESH,
        )

    def begin(c):
        for way in range(2):
            ring(c, way, 0).start()
        share(c, 0, me).start()

    def event(c, hop):
        for way in range(2):
            if hop < steps[way]:
                ring(c, way, hop).wait_recv()
                if hop + 1 < steps[way]:
                    ring(c, way, hop + 1).start()
                share(c, 1 + way * half + hop, came(way, hop)).start()

    def guarded(c, what, *rest):
        if isinstance(c, int):
            if c < chunks:
                what(c, *rest)
        else:
            pl.when(c < chunks)(lambda: what(c, *rest))

    def even_poll(c):
        guarded(c - 1, event, 2)
        guarded(c, event, 0)

    def odd_poll(c):
        guarded(c - 1, event, 3)
        guarded(c, event, 1)
        guarded(c + 1, begin)

    for c in range(chunks):
        land[c, me] = own[:, c * BLOCK : (c + 1) * BLOCK]
    pl.semaphore_wait(barrier, 3)
    begin(0)
    event(0, 0)
    event(0, 1)
    begin(1)
    even_poll(1)
    odd_poll(1)

    def gathered(c):
        return land[c].reshape(total, BLOCK)

    def before(k):
        n = k * BLOCK
        for m in range(k):
            column[m * BLOCK : (m + 1) * BLOCK, :] = over_rows(gathered(m), gathered(k))
        a[...] = over_rows(gathered(k), gathered(k))
        if k:
            column[:n, :] = jnp.dot(
                linv[:n, :n],
                column[:n, :],
                preferred_element_type=jnp.float32,
                precision=HIGHEST,
            )
            a[...] -= over_rows(column[:n, :], column[:n, :], HIGHEST)

    def after(k):
        n = k * BLOCK
        linv[n : n + BLOCK, n : n + BLOCK] = w[...]
        if k:
            linv[n : n + BLOCK, :n] = -jnp.dot(
                w[...],
                over_rows(column[:n, :], linv[:n, :n], HIGHEST),
                preferred_element_type=jnp.float32,
                precision=HIGHEST,
            )
        for m in range(k + 1, chunks):
            linv[n : n + BLOCK, m * BLOCK : (m + 1) * BLOCK] = jnp.zeros(
                (BLOCK, BLOCK), jnp.float32
            )
        n += BLOCK
        both = 0.0
        for part in split(linv[n - BLOCK : n, :n]):
            both += lax.dot_general(
                own[:, :n],
                part,
                (((1,), (1,)), ((), ())),
                preferred_element_type=jnp.float32,
            )
        out[:, n - BLOCK : n] = both * scale

    def step(k, carry):
        for index in range(chips):
            share(k, index, me).wait_recv()
        for i in range(chunks):
            pl.when(k == i)(functools.partial(before, i))
        even_poll(k + 2)
        inverse_factor(a, w)
        odd_poll(k + 2)
        for i in range(chunks):
            pl.when(k == i)(functools.partial(after, i))
        return carry

    lax.fori_loop(0, chunks, step, 0)

    def finish(c, carry):
        for way in range(2):
            for hop in range(steps[way]):
                ring(c, way, hop).wait_send()
        for index in range(chips):
            share(c, index, me).wait_send()
        return carry

    lax.fori_loop(0, chunks, finish, 0)


def whiten_ring(pooled, collective_id):
    devices = lax.axis_size("dp")
    chips = devices // 2
    rows, width = pooled.shape
    chunks = width // BLOCK
    dma = pltpu.SemaphoreType.DMA
    whole = pl.BlockSpec(memory_space=pltpu.VMEM)
    return pl.pallas_call(
        functools.partial(whiten_ring_kernel, chips, math.sqrt(rows * devices)),
        out_shape=jax.ShapeDtypeStruct((rows, width), jnp.float32),
        in_specs=[whole],
        out_specs=whole,
        scratch_shapes=[
            pltpu.VMEM((chunks, devices, rows, BLOCK), pooled.dtype),
            pltpu.VMEM((width, width), jnp.float32),
            pltpu.VMEM((width, BLOCK), jnp.float32),
            pltpu.VMEM((BLOCK, BLOCK), jnp.float32),
            pltpu.VMEM((BLOCK, BLOCK), jnp.float32),
            dma((chunks, 2, chips // 2)),
            dma((chunks, 2, chips // 2)),
            dma((chunks, chips)),
            dma((chunks, chips)),
        ],
        compiler_params=pltpu.CompilerParams(
            collective_id=collective_id, has_side_effects=True, vmem_limit_bytes=40 << 20
        ),
    )(pooled)


def on_device(tokens, token_mask, span_ids, norm_gain, norm_shift, w_up, b_up, w_down):
    values = tokens.astype(jnp.float32)
    center = jnp.mean(values, axis=1, keepdims=True)
    spread = jnp.mean((values - center) ** 2, axis=1, keepdims=True)
    normed = ((values - center) * lax.rsqrt(spread + 1e-05) * norm_gain + norm_shift).astype(
        jnp.bfloat16
    )
    width, hidden_size = tokens.shape[1], b_up.shape[0]
    over_last = (((1,), (1,)), ((), ()))
    if w_up.shape[1] % BLOCK == 0:
        hidden, down_full = ring_up(normed, b_up, w_up.T, w_down.T, 0)
    else:
        up_full, down_full = ring_gather((w_up.T, w_down.T), 0)
        up_full = up_full.reshape(hidden_size, width)
        before = (
            lax.dot_general(normed, up_full, over_last, preferred_element_type=jnp.float32) + b_up
        )
        hidden = jax.nn.gelu(before, approximate=False).astype(jnp.bfloat16)
    down_full = down_full.reshape(width, hidden_size)
    projected = lax.dot_general(
        hidden, down_full, over_last, preferred_element_type=jnp.float32
    )
    block_out = (values + projected).astype(jnp.bfloat16)
    labels = jnp.arange(SEG_DEV, dtype=jnp.int32)[:, None]
    select = (span_ids[0][None, :] == labels) & (token_mask[0][None, :] == 1)
    sums = jnp.dot(select.astype(jnp.bfloat16), block_out, preferred_element_type=jnp.float32)
    counts = jnp.sum(select.astype(jnp.float32), axis=1)
    pooled = (sums / jnp.maximum(counts, 1.0)[:, None]).astype(jnp.bfloat16)
    if lax.axis_size("dp") == 16:
        return whiten_ring(pooled, 1)
    middle = width // 2
    left, right = (
        half.reshape(-1, middle)
        for half in ring_gather((pooled[:, :middle], pooled[:, middle:]), 1)
    )
    gram = [
        lax.dot_general(one, two, (((0,), (0,)), ((), ())), preferred_element_type=jnp.float32)
        for one, two in ((left, left), (left, right), (right, right))
    ]
    total_rows = SEG_DEV * lax.axis_size("dp")
    return whiten(gram, pooled.astype(jnp.float32).T, math.sqrt(total_rows)).T


def solution(mesh):
    in_specs = (
        P(("groups", "dp"), None),
        P(("groups", "dp"), None),
        P(("groups", "dp"), None),
        P(),
        P(),
        P(None, "dp"),
        P(),
        P(None, "dp"),
    )
    out_specs = P(("groups", "dp"), None)
    return jax.shard_map(
        on_device, mesh=mesh, in_specs=in_specs, out_specs=out_specs, check_vma=False
    )
```

```python
import functools
import math

import jax
import jax.numpy as jnp
from jax import lax
from jax.experimental import pallas as pl
from jax.experimental.pallas import tpu as pltpu
from jax.sharding import PartitionSpec as P

SEG_DEV = 192
BLOCK = 128
HIGHEST = lax.Precision.HIGHEST


def inverse_block(src, dst):
    lane = lax.broadcasted_iota(jnp.int32, (8, BLOCK), 1)
    sub = lax.broadcasted_iota(jnp.int32, (8, BLOCK), 0)
    groups = BLOCK // 8
    held = [src[8 * q : 8 * q + 8, :BLOCK] for q in range(groups)]

    def column(block, c):
        return jnp.broadcast_to(block[:, c : c + 1], (8, BLOCK))

    def row(block, r):
        return jnp.broadcast_to(block[r : r + 1, :], (8, BLOCK))

    for p in range(groups):
        at = 8 * p
        inside = (lane >= at) & (lane < at + 8)
        raw = held[p]
        cols = [column(raw, at + c) for c in range(8)]
        work = jnp.where(inside, jnp.where(lane - at == sub, 1.0, 0.0), raw)
        done = jnp.zeros((8, BLOCK), jnp.float32)
        for j in range(8):
            here = sub == j
            pivot = row(cols[j], j)
            inv = 1.0 / pivot
            done = jnp.where(here, work * lax.rsqrt(pivot), done)
            scaled = row(work, j) * inv
            work = jnp.where(here, scaled, work - cols[j] * scaled)
            for c in range(j + 1, 8):
                scaled = row(cols[c], j) * inv
                cols[c] = jnp.where(here, scaled, cols[c] - cols[j] * scaled)
        dst[at : at + 8, :] = jnp.where(lane <= at + sub, done, 0.0)
        rows = [row(work, c) for c in range(8)]
        for q in range(p + 1, groups):
            total = jnp.where(inside, 0.0, held[q])
            for c in range(8):
                total = total - column(held[q], at + c) * rows[c]
            held[q] = total


def whiten_kernel(scale, first_ref, cross_ref, last_ref, rows_ref, out_ref, a, panel, inv):
    half = first_ref.shape[0]
    n = 2 * half
    extra = rows_ref.shape[1]
    a[:half, :half] = first_ref[...]
    a[:half, half:n] = cross_ref[...]
    a[half:, :half] = jnp.zeros((half, half), jnp.float32)
    a[half:, half:n] = last_ref[...]
    a[:, n:] = jnp.zeros((n, a.shape[1] - n), jnp.float32)
    a[:, n : n + extra] = rows_ref[...]
    blocks = n // BLOCK

    def step(k, carry):
        lo = pl.multiple_of(k * BLOCK, BLOCK)
        panel[:, :BLOCK] = a[pl.ds(lo, BLOCK), pl.ds(lo, BLOCK)]
        inverse_block(panel, inv)
        panel[...] = jnp.dot(
            inv[...], a[pl.ds(lo, BLOCK), :], preferred_element_type=jnp.float32, precision=HIGHEST
        )
        out_ref[pl.ds(lo, BLOCK), :] = panel[:, n : n + extra] * scale

        for first in range(0, blocks, 2):
            start = first * BLOCK

            def trail(i, carry, start=start):
                hi = pl.multiple_of(i * BLOCK, BLOCK)
                left = panel[:, pl.ds(hi, BLOCK)].T
                a[pl.ds(hi, BLOCK), start:] -= jnp.dot(
                    left, panel[:, start:], preferred_element_type=jnp.float32, precision=HIGHEST
                )
                return carry

            lax.fori_loop(jnp.maximum(k + 1, first), min(first + 2, blocks), trail, 0)
        return carry

    lax.fori_loop(0, blocks, step, 0)


def whiten(gram, rows_t, scale):
    n, extra = rows_t.shape
    wide = n + (extra + BLOCK - 1) // BLOCK * BLOCK
    return pl.pallas_call(
        functools.partial(whiten_kernel, scale),
        out_shape=jax.ShapeDtypeStruct((n, extra), jnp.float32),
        in_specs=[pl.BlockSpec(memory_space=pltpu.VMEM)] * 4,
        out_specs=pl.BlockSpec(memory_space=pltpu.VMEM),
        scratch_shapes=[
            pltpu.VMEM((n, wide), jnp.float32),
            pltpu.VMEM((BLOCK, wide), jnp.float32),
            pltpu.VMEM((BLOCK, BLOCK), jnp.float32),
        ],
        compiler_params=pltpu.CompilerParams(vmem_limit_bytes=32 << 20),
    )(*gram, rows_t)


def ring_kernel(chips, count, fused, *refs):
    if fused:
        normed, bias, up, down, hidden, down_out, up_out = refs[:7]
        ins, outs, refs = (up, down), (up_out, down_out), refs[7:]
    else:
        ins, outs, refs = refs[:count], refs[count : 2 * count], refs[2 * count :]
    ring_send, ring_recv, core_send, core_recv, own_sem = refs
    me = lax.axis_index("dp")
    core, chip = lax.rem(me, 2), me // 2
    half = chips // 2
    odd = lax.rem(chip, 2)
    place = (1 - odd) * (chip // 2) + odd * (chips - 1 - chip // 2)
    turn = 1 - 2 * core
    partner = me + turn

    def device(q):
        q = lax.rem(q + 2 * chips, chips)
        back = q // half
        return 2 * ((1 - back) * 2 * q + back * (2 * (chips - 1 - q) + 1)) + core

    ahead, behind = device(place + turn), device(place - turn)
    barrier = pltpu.get_barrier_semaphore()
    for other in (ahead, behind, partner):
        pl.semaphore_signal(
            barrier, inc=1, device_id={"dp": other}, device_id_type=pl.DeviceIdType.MESH
        )
    pl.semaphore_wait(barrier, 3)

    steps = (half, chips - 1 - half)
    started, across = [], []

    def send(a, source, slot, way, step):
        copy = pltpu.make_async_remote_copy(
            src_ref=source,
            dst_ref=outs[a].at[slot],
            send_sem=ring_send.at[a, way, step],
            recv_sem=ring_recv.at[a, way, step],
            device_id={"dp": (ahead, behind)[way]},
            device_id_type=pl.DeviceIdType.MESH,
        )
        copy.start()
        started.append(copy)
        return copy

    def share(a, source, slot, index):
        copy = pltpu.make_async_remote_copy(
            src_ref=source,
            dst_ref=outs[a].at[slot],
            send_sem=core_send.at[a, index],
            recv_sem=core_recv.at[a, index],
            device_id={"dp": partner},
            device_id_type=pl.DeviceIdType.MESH,
        )
        copy.start()
        if fused and a == 0:
            first[index] = copy
        else:
            across.append(copy)

    def compute(slot, block):
        size = block.shape[0]
        columns = pl.ds(pl.multiple_of(slot * size, BLOCK), size)
        tile = normed.shape[0] // 3

        def part(t, carry):
            at = pl.ds(pl.multiple_of(t * tile, tile), tile)
            before = lax.dot_general(
                normed[at, :],
                block[...],
                (((1,), (1,)), ((), ())),
                preferred_element_type=jnp.float32,
            )
            before = before + bias[slot]
            hidden[at, columns] = (
                0.5 * before * (1.0 + lax.erf(before * math.sqrt(0.5)))
            ).astype(hidden.dtype)
            return carry

        lax.fori_loop(0, 3, part, 0)

    first = {}

    def partner_block(index, step, way):
        first[index].wait_recv()
        slot = partner
        if index:
            slot = device(place + (1 + step) * turn * (1 - 2 * way)) + turn
        compute(slot, outs[0].at[slot])

    flying, local = {}, []
    for a in range(count):
        for way in range(2):
            flying[a, way] = send(a, ins[a], me, way, 0)
        share(a, ins[a], me, 0)
        if not (fused and a == 0):
            local.append(pltpu.make_async_copy(ins[a], outs[a].at[me], own_sem.at[a]))
            local[-1].start()
    if fused:
        compute(me, ins[0])
    for step in range(half):
        landed = []
        if fused:
            if step == 0:
                partner_block(0, 0, 0)
            for way in range(2):
                if 0 < step <= steps[way]:
                    partner_block(way * half + step, step - 1, way)
        for a in range(count):
            for way in range(2):
                if step >= steps[way]:
                    continue
                flying[a, way].wait_recv()
                slot = device(place - (1 + step) * turn * (1 - 2 * way))
                block = outs[a].at[slot]
                if step + 1 < steps[way]:
                    flying[a, way] = send(a, block, slot, way, step + 1)
                share(a, block, slot, 1 + way * half + step)
                if fused and a == 0:
                    landed.append((slot, block))
        for slot, block in landed:
            compute(slot, block)
    if fused:
        for way in range(2):
            if steps[way] == half:
                partner_block(way * half + half, half - 1, way)
        for copy in first.values():
            copy.wait_send()
    for copy in local:
        copy.wait()
    for copy in started:
        copy.wait_send()
    for copy in across:
        copy.wait()


def ring_gather(blocks, collective_id):
    devices = lax.axis_size("dp")
    chips, count = devices // 2, len(blocks)
    dma = pltpu.SemaphoreType.DMA
    return pl.pallas_call(
        functools.partial(ring_kernel, chips, count, False),
        out_shape=[jax.ShapeDtypeStruct((devices,) + b.shape, b.dtype) for b in blocks],
        in_specs=[pl.BlockSpec(memory_space=pl.ANY)] * count,
        out_specs=[pl.BlockSpec(memory_space=pl.ANY)] * count,
        scratch_shapes=[
            dma((count, 2, chips // 2)),
            dma((count, 2, chips // 2)),
            dma((count, chips)),
            dma((count, chips)),
            dma((count,)),
        ],
        compiler_params=pltpu.CompilerParams(collective_id=collective_id, has_side_effects=True),
    )(*blocks)


def ring_up(normed, bias, up, down, collective_id):
    devices = lax.axis_size("dp")
    chips = devices // 2
    dma = pltpu.SemaphoreType.DMA
    whole = pl.BlockSpec(memory_space=pltpu.VMEM)
    apart = pl.BlockSpec(memory_space=pl.ANY)
    return pl.pallas_call(
        functools.partial(ring_kernel, chips, 2, True),
        out_shape=[
            jax.ShapeDtypeStruct((normed.shape[0], devices * up.shape[0]), normed.dtype),
            jax.ShapeDtypeStruct((devices,) + down.shape, down.dtype),
        ],
        in_specs=[whole, whole, whole, apart],
        out_specs=[whole, apart],
        scratch_shapes=[
            pltpu.VMEM((devices,) + up.shape, up.dtype),
            dma((2, 2, chips // 2)),
            dma((2, 2, chips // 2)),
            dma((2, chips)),
            dma((2, chips)),
            dma((2,)),
        ],
        compiler_params=pltpu.CompilerParams(
            collective_id=collective_id, has_side_effects=True, vmem_limit_bytes=40 << 20
        ),
    )(normed, bias.reshape(devices, 1, -1), up, down)


def spread(block, r):
    return jnp.broadcast_to(block[r : r + 1, :], (8, BLOCK))


def strip_factor(a, dst, base, groups):
    lane = lax.broadcasted_iota(jnp.int32, (8, BLOCK), 1)
    sub = lax.broadcasted_iota(jnp.int32, (8, BLOCK), 0)
    h = [a[base + 8 * q : base + 8 * q + 8, :] for q in range(groups)]

    def fetch(p):
        return {
            (c, q): jnp.broadcast_to(
                h[q][:, base + 8 * p + c : base + 8 * p + c + 1], (8, BLOCK)
            )
            for q in range(p, groups)
            for c in range(8)
        }

    cols = fetch(0)
    for p in range(groups):
        more = p + 1 < groups
        following = fetch(p + 1) if more else {}
        at = base + 8 * p
        inside = (lane >= at) & (lane < at + 8)
        work = jnp.where(inside, jnp.where(lane - at == sub, 1.0, 0.0), h[p])
        for q in range(p + 1, groups):
            h[q] = jnp.where(inside, 0.0, h[q])
        pivots = jnp.zeros((8, BLOCK), jnp.float32)
        for j in range(8):
            pivot = spread(cols[j, p], j)
            inv = 1.0 / pivot
            pivots = jnp.where(sub == j, pivot, pivots)
            for c in range(j + 1, 8):
                m = spread(cols[j, p], c) * inv
                for q in range(p, groups):
                    cols[c, q] = cols[c, q] - cols[j, q] * m
            if more:
                for c in range(8):
                    m = spread(cols[j, p + 1], c) * inv
                    for q in range(p + 1, groups):
                        following[c, q] = following[c, q] - cols[j, q] * m
            scaled = spread(work, j) * inv
            if j < 7:
                work = work - jnp.where(sub > j, cols[j, p], 0.0) * scaled
            for q in range(p + 1, groups):
                h[q] = h[q] - cols[j, q] * scaled
        dst[at : at + 8, :] = work * lax.rsqrt(pivots)
        cols = following


def over_rows(left, right, precision=None):
    return lax.dot_general(
        left,
        right,
        (((0,), (0,)), ((), ())),
        preferred_element_type=jnp.float32,
        precision=precision,
    )


def inverse_factor(a, dst, between):
    size = 32
    for base in range(0, BLOCK, size):
        strip_factor(a, dst, base, size // 8)
        between(base // size)
        lo = base + size
        if lo < BLOCK:
            rows = dst[base:lo, :]
            r = lax.broadcasted_iota(jnp.int32, (size, BLOCK), 0) + base
            c = lax.broadcasted_iota(jnp.int32, (size, BLOCK), 1)
            drop = over_rows(rows, jnp.where((c > r) & (c < lo), 0.0, rows), HIGHEST)
            c = lax.broadcasted_iota(jnp.int32, (BLOCK - lo, BLOCK), 1)
            a[lo:, :] = jnp.where((c >= base) & (c < lo), 0.0, a[lo:, :]) - drop[lo:, :]
    r = lax.broadcasted_iota(jnp.int32, (BLOCK, BLOCK), 0)
    c = lax.broadcasted_iota(jnp.int32, (BLOCK, BLOCK), 1)
    dst[...] = jnp.where(c <= r, dst[...], 0.0)


def product(left, right):
    return jnp.dot(left, right, preferred_element_type=jnp.float32)


def split(x):
    high = x.astype(jnp.bfloat16)
    return high, (x - high.astype(jnp.float32)).astype(jnp.bfloat16)


def whiten_ring_kernel(
    scale, own, out, land, high, low, r_high, r_low, t, a, w, z_send, z_recv, y_send, y_recv, core_send, core_recv
):
    me = lax.axis_index("dp")
    core, y, z = lax.rem(me, 2), lax.rem(me // 2, 2), me // 4
    depth = land.shape[3]
    chunks = own.shape[1] // BLOCK
    rows = own.shape[0]
    total = 4 * depth * rows
    partner, across = me + 1 - 2 * core, me + 2 - 4 * y
    line = [lax.rem(z + d, depth) for d in range(1, depth)]

    barrier = pltpu.get_barrier_semaphore()
    others = [4 * other + 2 * y + core for other in line] + [partner, across]
    for other in others:
        pl.semaphore_signal(
            barrier, inc=1, device_id={"dp": other}, device_id_type=pl.DeviceIdType.MESH
        )

    def remote(ref, send_sem, recv_sem, target):
        return pltpu.make_async_remote_copy(
            src_ref=ref,
            dst_ref=ref,
            send_sem=send_sem,
            recv_sem=recv_sem,
            device_id={"dp": target},
            device_id_type=pl.DeviceIdType.MESH,
        )

    def along(c, d):
        return remote(land.at[c, y, core, z], z_send.at[c, d], z_recv.at[c, d], others[d])

    def over(c, d):
        slot = z if d == depth - 1 else lax.rem(z + depth - 1 - d, depth)
        return remote(land.at[c, y, core, slot], y_send.at[c, d], y_recv.at[c, d], across)

    def share(c, side):
        ref = land.at[c, (1 - y) if side else y, core]
        return remote(ref, core_send.at[c, side], core_recv.at[c, side], partner)

    def begin(c):
        for d in range(depth - 1):
            along(c, d).start()
        over(c, depth - 1).start()

    def first(c):
        for d in range(depth - 1):
            along(c, d).wait_recv()
            over(c, d).start()
        share(c, 0).start()

    def second(c):
        for d in range(depth):
            over(c, d).wait_recv()
        share(c, 1).start()

    def guarded(c, what):
        pl.when(c < chunks)(lambda: what(c))

    for c in range(chunks):
        land[c, y, core, z] = own[:, c * BLOCK : (c + 1) * BLOCK]
    for ref in (high, low, r_high, r_low):
        ref[...] = jnp.zeros(ref.shape, ref.dtype)
    pl.semaphore_wait(barrier, depth + 1)
    begin(0)
    begin(1)
    first(0)
    begin(2)
    first(1)
    second(0)

    def gathered(c):
        return land[c].reshape(total, BLOCK)

    def before(k):
        n = k * BLOCK
        top = [over_rows(gathered(m), gathered(k)) for m in range(k)]
        corner = over_rows(gathered(k), gathered(k))
        if k:
            c_high, c_low = split(jnp.concatenate(top, axis=0))
            r = product(high[:n, :n], c_high) + (
                product(high[:n, :n], c_low) + product(low[:n, :n], c_high)
            )
            one, two = split(r)
            r_high[:n, :] = one
            r_low[:n, :] = two
            corner -= over_rows(one, one) + (over_rows(one, two) + over_rows(two, one))
        a[...] = corner

    def between(s):
        size = t.shape[1] // 4
        at = slice(s * size, (s + 1) * size)
        t[:, at] = over_rows(r_high[...], high[:, at]) + (
            over_rows(r_high[...], low[:, at]) + over_rows(r_low[...], high[:, at])
        )

    def after(k):
        at = pl.ds(pl.multiple_of(k * BLOCK, BLOCK), BLOCK)
        w_high, w_low = split(w[...])
        t_high, t_low = split(t[...])
        left = product(w_high, t_high) + (product(w_high, t_low) + product(w_low, t_high))
        one, two = split(-left)
        high[at, :] = one
        low[at, :] = two
        high[at, at] = w_high
        low[at, at] = w_low
        both = sum(
            lax.dot_general(
                own[...],
                part,
                (((1,), (1,)), ((), ())),
                preferred_element_type=jnp.float32,
            )
            for part in (high[at, :], low[at, :])
        )
        out[:, at] = both * scale

    def step(k, carry):
        for side in range(2):
            share(k, side).wait_recv()
        guarded(k + 3, begin)
        for i in range(chunks):
            pl.when(k == i)(functools.partial(before, i))
        guarded(k + 2, first)
        inverse_factor(a, w, between)
        guarded(k + 1, second)
        after(k)
        return carry

    lax.fori_loop(0, chunks, step, 0)

    def finish(c, carry):
        for d in range(depth - 1):
            along(c, d).wait_send()
        for d in range(depth):
            over(c, d).wait_send()
        for side in range(2):
            share(c, side).wait_send()
        return carry

    lax.fori_loop(0, chunks, finish, 0)


def whiten_ring(pooled, collective_id):
    devices = lax.axis_size("dp")
    depth = devices // 4
    rows, width = pooled.shape
    chunks = width // BLOCK
    dma = pltpu.SemaphoreType.DMA
    whole = pl.BlockSpec(memory_space=pltpu.VMEM)
    return pl.pallas_call(
        functools.partial(whiten_ring_kernel, math.sqrt(rows * devices)),
        out_shape=jax.ShapeDtypeStruct((rows, width), jnp.float32),
        in_specs=[whole],
        out_specs=whole,
        scratch_shapes=[
            pltpu.VMEM((chunks, 2, 2, depth, rows, BLOCK), pooled.dtype),
            pltpu.VMEM((width, width), jnp.bfloat16),
            pltpu.VMEM((width, width), jnp.bfloat16),
            pltpu.VMEM((width, BLOCK), jnp.bfloat16),
            pltpu.VMEM((width, BLOCK), jnp.bfloat16),
            pltpu.VMEM((BLOCK, width), jnp.float32),
            pltpu.VMEM((BLOCK, BLOCK), jnp.float32),
            pltpu.VMEM((BLOCK, BLOCK), jnp.float32),
            dma((chunks, depth - 1)),
            dma((chunks, depth - 1)),
            dma((chunks, depth)),
            dma((chunks, depth)),
            dma((chunks, 2)),
            dma((chunks, 2)),
        ],
        compiler_params=pltpu.CompilerParams(
            collective_id=collective_id, has_side_effects=True, vmem_limit_bytes=40 << 20
        ),
    )(pooled)


def on_device(tokens, token_mask, span_ids, norm_gain, norm_shift, w_up, b_up, w_down):
    values = tokens.astype(jnp.float32)
    center = jnp.mean(values, axis=1, keepdims=True)
    spread = jnp.mean((values - center) ** 2, axis=1, keepdims=True)
    normed = ((values - center) * lax.rsqrt(spread + 1e-05) * norm_gain + norm_shift).astype(
        jnp.bfloat16
    )
    width, hidden_size = tokens.shape[1], b_up.shape[0]
    over_last = (((1,), (1,)), ((), ()))
    if w_up.shape[1] % BLOCK == 0:
        hidden, down_full = ring_up(normed, b_up, w_up.T, w_down.T, 0)
    else:
        up_full, down_full = ring_gather((w_up.T, w_down.T), 0)
        up_full = up_full.reshape(hidden_size, width)
        before = (
            lax.dot_general(normed, up_full, over_last, preferred_element_type=jnp.float32) + b_up
        )
        hidden = jax.nn.gelu(before, approximate=False).astype(jnp.bfloat16)
    down_full = down_full.reshape(width, hidden_size)
    projected = lax.dot_general(
        hidden, down_full, over_last, preferred_element_type=jnp.float32
    )
    block_out = (values + projected).astype(jnp.bfloat16)
    labels = jnp.arange(SEG_DEV, dtype=jnp.int32)[:, None]
    select = (span_ids[0][None, :] == labels) & (token_mask[0][None, :] == 1)
    sums = jnp.dot(select.astype(jnp.bfloat16), block_out, preferred_element_type=jnp.float32)
    counts = jnp.sum(select.astype(jnp.float32), axis=1)
    pooled = (sums / jnp.maximum(counts, 1.0)[:, None]).astype(jnp.bfloat16)
    if lax.axis_size("dp") == 16:
        return whiten_ring(pooled, 1)
    middle = width // 2
    left, right = (
        half.reshape(-1, middle)
        for half in ring_gather((pooled[:, :middle], pooled[:, middle:]), 1)
    )
    gram = [
        lax.dot_general(one, two, (((0,), (0,)), ((), ())), preferred_element_type=jnp.float32)
        for one, two in ((left, left), (left, right), (right, right))
    ]
    total_rows = SEG_DEV * lax.axis_size("dp")
    return whiten(gram, pooled.astype(jnp.float32).T, math.sqrt(total_rows)).T


def solution(mesh):
    in_specs = (
        P(("groups", "dp"), None),
        P(("groups", "dp"), None),
        P(("groups", "dp"), None),
        P(),
        P(),
        P(None, "dp"),
        P(),
        P(None, "dp"),
    )
    out_specs = P(("groups", "dp"), None)
    return jax.shard_map(
        on_device, mesh=mesh, in_specs=in_specs, out_specs=out_specs, check_vma=False
    )
```

```python
import functools
import math

import jax
import jax.numpy as jnp
from jax import lax
from jax.experimental import pallas as pl
from jax.experimental.pallas import tpu as pltpu
from jax.sharding import PartitionSpec as P

SEG_DEV = 192
BLOCK = 128
HIGHEST = lax.Precision.HIGHEST


def inverse_block(src, dst):
    lane = lax.broadcasted_iota(jnp.int32, (8, BLOCK), 1)
    sub = lax.broadcasted_iota(jnp.int32, (8, BLOCK), 0)
    groups = BLOCK // 8
    held = [src[8 * q : 8 * q + 8, :BLOCK] for q in range(groups)]

    def column(block, c):
        return jnp.broadcast_to(block[:, c : c + 1], (8, BLOCK))

    def row(block, r):
        return jnp.broadcast_to(block[r : r + 1, :], (8, BLOCK))

    for p in range(groups):
        at = 8 * p
        inside = (lane >= at) & (lane < at + 8)
        raw = held[p]
        cols = [column(raw, at + c) for c in range(8)]
        work = jnp.where(inside, jnp.where(lane - at == sub, 1.0, 0.0), raw)
        done = jnp.zeros((8, BLOCK), jnp.float32)
        for j in range(8):
            here = sub == j
            pivot = row(cols[j], j)
            inv = 1.0 / pivot
            done = jnp.where(here, work * lax.rsqrt(pivot), done)
            scaled = row(work, j) * inv
            work = jnp.where(here, scaled, work - cols[j] * scaled)
            for c in range(j + 1, 8):
                scaled = row(cols[c], j) * inv
                cols[c] = jnp.where(here, scaled, cols[c] - cols[j] * scaled)
        dst[at : at + 8, :] = jnp.where(lane <= at + sub, done, 0.0)
        rows = [row(work, c) for c in range(8)]
        for q in range(p + 1, groups):
            total = jnp.where(inside, 0.0, held[q])
            for c in range(8):
                total = total - column(held[q], at + c) * rows[c]
            held[q] = total


def whiten_kernel(scale, first_ref, cross_ref, last_ref, rows_ref, out_ref, a, panel, inv):
    half = first_ref.shape[0]
    n = 2 * half
    extra = rows_ref.shape[1]
    a[:half, :half] = first_ref[...]
    a[:half, half:n] = cross_ref[...]
    a[half:, :half] = jnp.zeros((half, half), jnp.float32)
    a[half:, half:n] = last_ref[...]
    a[:, n:] = jnp.zeros((n, a.shape[1] - n), jnp.float32)
    a[:, n : n + extra] = rows_ref[...]
    blocks = n // BLOCK

    def step(k, carry):
        lo = pl.multiple_of(k * BLOCK, BLOCK)
        panel[:, :BLOCK] = a[pl.ds(lo, BLOCK), pl.ds(lo, BLOCK)]
        inverse_block(panel, inv)
        panel[...] = jnp.dot(
            inv[...], a[pl.ds(lo, BLOCK), :], preferred_element_type=jnp.float32, precision=HIGHEST
        )
        out_ref[pl.ds(lo, BLOCK), :] = panel[:, n : n + extra] * scale

        for first in range(0, blocks, 2):
            start = first * BLOCK

            def trail(i, carry, start=start):
                hi = pl.multiple_of(i * BLOCK, BLOCK)
                left = panel[:, pl.ds(hi, BLOCK)].T
                a[pl.ds(hi, BLOCK), start:] -= jnp.dot(
                    left, panel[:, start:], preferred_element_type=jnp.float32, precision=HIGHEST
                )
                return carry

            lax.fori_loop(jnp.maximum(k + 1, first), min(first + 2, blocks), trail, 0)
        return carry

    lax.fori_loop(0, blocks, step, 0)


def whiten(gram, rows_t, scale):
    n, extra = rows_t.shape
    wide = n + (extra + BLOCK - 1) // BLOCK * BLOCK
    return pl.pallas_call(
        functools.partial(whiten_kernel, scale),
        out_shape=jax.ShapeDtypeStruct((n, extra), jnp.float32),
        in_specs=[pl.BlockSpec(memory_space=pltpu.VMEM)] * 4,
        out_specs=pl.BlockSpec(memory_space=pltpu.VMEM),
        scratch_shapes=[
            pltpu.VMEM((n, wide), jnp.float32),
            pltpu.VMEM((BLOCK, wide), jnp.float32),
            pltpu.VMEM((BLOCK, BLOCK), jnp.float32),
        ],
        compiler_params=pltpu.CompilerParams(vmem_limit_bytes=32 << 20),
    )(*gram, rows_t)


def ring_kernel(chips, count, fused, *refs):
    if fused:
        normed, bias, up, down, hidden, down_out, up_out = refs[:7]
        ins, outs, refs = (up, down), (up_out, down_out), refs[7:]
    else:
        ins, outs, refs = refs[:count], refs[count : 2 * count], refs[2 * count :]
    ring_send, ring_recv, core_send, core_recv, own_sem = refs
    me = lax.axis_index("dp")
    core, chip = lax.rem(me, 2), me // 2
    half = chips // 2
    odd = lax.rem(chip, 2)
    place = (1 - odd) * (chip // 2) + odd * (chips - 1 - chip // 2)
    turn = 1 - 2 * core
    partner = me + turn

    def device(q):
        q = lax.rem(q + 2 * chips, chips)
        back = q // half
        return 2 * ((1 - back) * 2 * q + back * (2 * (chips - 1 - q) + 1)) + core

    ahead, behind = device(place + turn), device(place - turn)
    barrier = pltpu.get_barrier_semaphore()
    for other in (ahead, behind, partner):
        pl.semaphore_signal(
            barrier, inc=1, device_id={"dp": other}, device_id_type=pl.DeviceIdType.MESH
        )
    pl.semaphore_wait(barrier, 3)

    steps = (half, chips - 1 - half)
    started, across = [], []

    def send(a, source, slot, way, step):
        copy = pltpu.make_async_remote_copy(
            src_ref=source,
            dst_ref=outs[a].at[slot],
            send_sem=ring_send.at[a, way, step],
            recv_sem=ring_recv.at[a, way, step],
            device_id={"dp": (ahead, behind)[way]},
            device_id_type=pl.DeviceIdType.MESH,
        )
        copy.start()
        started.append(copy)
        return copy

    def share(a, source, slot, index):
        copy = pltpu.make_async_remote_copy(
            src_ref=source,
            dst_ref=outs[a].at[slot],
            send_sem=core_send.at[a, index],
            recv_sem=core_recv.at[a, index],
            device_id={"dp": partner},
            device_id_type=pl.DeviceIdType.MESH,
        )
        copy.start()
        if fused and a == 0:
            first[index] = copy
        else:
            across.append(copy)

    def compute(slot, block):
        size = block.shape[0]
        columns = pl.ds(pl.multiple_of(slot * size, BLOCK), size)
        tile = normed.shape[0] // 3

        def part(t, carry):
            at = pl.ds(pl.multiple_of(t * tile, tile), tile)
            before = lax.dot_general(
                normed[at, :],
                block[...],
                (((1,), (1,)), ((), ())),
                preferred_element_type=jnp.float32,
            )
            before = before + bias[slot]
            hidden[at, columns] = (
                0.5 * before * (1.0 + lax.erf(before * math.sqrt(0.5)))
            ).astype(hidden.dtype)
            return carry

        lax.fori_loop(0, 3, part, 0)

    first = {}

    def partner_block(index, step, way):
        first[index].wait_recv()
        slot = partner
        if index:
            slot = device(place + (1 + step) * turn * (1 - 2 * way)) + turn
        compute(slot, outs[0].at[slot])

    flying, local = {}, []
    for a in range(count):
        for way in range(2):
            flying[a, way] = send(a, ins[a], me, way, 0)
        share(a, ins[a], me, 0)
        if not (fused and a == 0):
            local.append(pltpu.make_async_copy(ins[a], outs[a].at[me], own_sem.at[a]))
            local[-1].start()
    if fused:
        compute(me, ins[0])
    for step in range(half):
        landed = []
        if fused:
            if step == 0:
                partner_block(0, 0, 0)
            for way in range(2):
                if 0 < step <= steps[way]:
                    partner_block(way * half + step, step - 1, way)
        for a in range(count):
            for way in range(2):
                if step >= steps[way]:
                    continue
                flying[a, way].wait_recv()
                slot = device(place - (1 + step) * turn * (1 - 2 * way))
                block = outs[a].at[slot]
                if step + 1 < steps[way]:
                    flying[a, way] = send(a, block, slot, way, step + 1)
                share(a, block, slot, 1 + way * half + step)
                if fused and a == 0:
                    landed.append((slot, block))
        for slot, block in landed:
            compute(slot, block)
    if fused:
        for way in range(2):
            if steps[way] == half:
                partner_block(way * half + half, half - 1, way)
        for copy in first.values():
            copy.wait_send()
    for copy in local:
        copy.wait()
    for copy in started:
        copy.wait_send()
    for copy in across:
        copy.wait()


def ring_gather(blocks, collective_id):
    devices = lax.axis_size("dp")
    chips, count = devices // 2, len(blocks)
    dma = pltpu.SemaphoreType.DMA
    return pl.pallas_call(
        functools.partial(ring_kernel, chips, count, False),
        out_shape=[jax.ShapeDtypeStruct((devices,) + b.shape, b.dtype) for b in blocks],
        in_specs=[pl.BlockSpec(memory_space=pl.ANY)] * count,
        out_specs=[pl.BlockSpec(memory_space=pl.ANY)] * count,
        scratch_shapes=[
            dma((count, 2, chips // 2)),
            dma((count, 2, chips // 2)),
            dma((count, chips)),
            dma((count, chips)),
            dma((count,)),
        ],
        compiler_params=pltpu.CompilerParams(collective_id=collective_id, has_side_effects=True),
    )(*blocks)


def ring_up(normed, bias, up, down, collective_id):
    devices = lax.axis_size("dp")
    chips = devices // 2
    dma = pltpu.SemaphoreType.DMA
    whole = pl.BlockSpec(memory_space=pltpu.VMEM)
    apart = pl.BlockSpec(memory_space=pl.ANY)
    return pl.pallas_call(
        functools.partial(ring_kernel, chips, 2, True),
        out_shape=[
            jax.ShapeDtypeStruct((normed.shape[0], devices * up.shape[0]), normed.dtype),
            jax.ShapeDtypeStruct((devices,) + down.shape, down.dtype),
        ],
        in_specs=[whole, whole, whole, apart],
        out_specs=[whole, apart],
        scratch_shapes=[
            pltpu.VMEM((devices,) + up.shape, up.dtype),
            dma((2, 2, chips // 2)),
            dma((2, 2, chips // 2)),
            dma((2, chips)),
            dma((2, chips)),
            dma((2,)),
        ],
        compiler_params=pltpu.CompilerParams(
            collective_id=collective_id, has_side_effects=True, vmem_limit_bytes=40 << 20
        ),
    )(normed, bias.reshape(devices, 1, -1), up, down)


def spread(block, r):
    return jnp.broadcast_to(block[r : r + 1, :], (8, BLOCK))


def strip_factor(a, dst, base, groups):
    lane = lax.broadcasted_iota(jnp.int32, (8, BLOCK), 1)
    sub = lax.broadcasted_iota(jnp.int32, (8, BLOCK), 0)
    h = [a[base + 8 * q : base + 8 * q + 8, :] for q in range(groups)]

    def fetch(p):
        return {
            (c, q): jnp.broadcast_to(
                h[q][:, base + 8 * p + c : base + 8 * p + c + 1], (8, BLOCK)
            )
            for q in range(p, groups)
            for c in range(8)
        }

    cols = fetch(0)
    for p in range(groups):
        more = p + 1 < groups
        following = fetch(p + 1) if more else {}
        at = base + 8 * p
        inside = (lane >= at) & (lane < at + 8)
        work = jnp.where(inside, jnp.where(lane - at == sub, 1.0, 0.0), h[p])
        for q in range(p + 1, groups):
            h[q] = jnp.where(inside, 0.0, h[q])
        pivots = jnp.zeros((8, BLOCK), jnp.float32)
        for j in range(8):
            pivot = spread(cols[j, p], j)
            inv = 1.0 / pivot
            pivots = jnp.where(sub == j, pivot, pivots)
            for c in range(j + 1, 8):
                m = spread(cols[j, p], c) * inv
                for q in range(p, groups):
                    cols[c, q] = cols[c, q] - cols[j, q] * m
            if more:
                for c in range(8):
                    m = spread(cols[j, p + 1], c) * inv
                    for q in range(p + 1, groups):
                        following[c, q] = following[c, q] - cols[j, q] * m
            scaled = spread(work, j) * inv
            if j < 7:
                work = work - jnp.where(sub > j, cols[j, p], 0.0) * scaled
            for q in range(p + 1, groups):
                h[q] = h[q] - cols[j, q] * scaled
        dst[at : at + 8, :] = work * lax.rsqrt(pivots)
        cols = following


def over_rows(left, right, precision=None):
    return lax.dot_general(
        left,
        right,
        (((0,), (0,)), ((), ())),
        preferred_element_type=jnp.float32,
        precision=precision,
    )


def inverse_factor(a, dst, between):
    size = 32
    for base in range(0, BLOCK, size):
        strip_factor(a, dst, base, size // 8)
        between(base // size)
        lo = base + size
        if lo < BLOCK:
            rows = dst[base:lo, :]
            r = lax.broadcasted_iota(jnp.int32, (size, BLOCK), 0) + base
            c = lax.broadcasted_iota(jnp.int32, (size, BLOCK), 1)
            drop = over_rows(rows, jnp.where((c > r) & (c < lo), 0.0, rows), HIGHEST)
            c = lax.broadcasted_iota(jnp.int32, (BLOCK - lo, BLOCK), 1)
            a[lo:, :] = jnp.where((c >= base) & (c < lo), 0.0, a[lo:, :]) - drop[lo:, :]
    r = lax.broadcasted_iota(jnp.int32, (BLOCK, BLOCK), 0)
    c = lax.broadcasted_iota(jnp.int32, (BLOCK, BLOCK), 1)
    dst[...] = jnp.where(c <= r, dst[...], 0.0)


def product(left, right):
    return jnp.dot(left, right, preferred_element_type=jnp.float32)


def split(x):
    high = x.astype(jnp.bfloat16)
    return high, (x - high.astype(jnp.float32)).astype(jnp.bfloat16)


def whiten_ring_kernel(
    scale, own, out, land, high, low, r_high, r_low, t, a, w, z_send, z_recv, y_send, y_recv, core_send, core_recv
):
    me = lax.axis_index("dp")
    core, y, z = lax.rem(me, 2), lax.rem(me // 2, 2), me // 4
    depth = land.shape[3]
    chunks = own.shape[1] // BLOCK
    rows = own.shape[0]
    total = 4 * depth * rows
    partner, across = me + 1 - 2 * core, me + 2 - 4 * y
    line = [lax.rem(z + d, depth) for d in range(1, depth)]

    barrier = pltpu.get_barrier_semaphore()
    others = [4 * other + 2 * y + core for other in line] + [partner, across]
    for other in others:
        pl.semaphore_signal(
            barrier, inc=1, device_id={"dp": other}, device_id_type=pl.DeviceIdType.MESH
        )

    def remote(ref, send_sem, recv_sem, target):
        return pltpu.make_async_remote_copy(
            src_ref=ref,
            dst_ref=ref,
            send_sem=send_sem,
            recv_sem=recv_sem,
            device_id={"dp": target},
            device_id_type=pl.DeviceIdType.MESH,
        )

    def along(c, d):
        return remote(land.at[c, y, core, z], z_send.at[c, d], z_recv.at[c, d], others[d])

    def over(c, d):
        slot = z if d == depth - 1 else lax.rem(z + depth - 1 - d, depth)
        return remote(land.at[c, y, core, slot], y_send.at[c, d], y_recv.at[c, d], across)

    def share(c, side):
        ref = land.at[c, (1 - y) if side else y, core]
        return remote(ref, core_send.at[c, side], core_recv.at[c, side], partner)

    def begin(c):
        for d in range(depth - 1):
            along(c, d).start()
        over(c, depth - 1).start()

    def first(c):
        for d in range(depth - 1):
            along(c, d).wait_recv()
            over(c, d).start()
        share(c, 0).start()

    def second(c):
        for d in range(depth):
            over(c, d).wait_recv()
        share(c, 1).start()

    def guarded(c, what):
        pl.when(c < chunks)(lambda: what(c))

    for c in range(chunks):
        land[c, y, core, z] = own[:, c * BLOCK : (c + 1) * BLOCK]
    for ref in (high, low, r_high, r_low):
        ref[...] = jnp.zeros(ref.shape, ref.dtype)
    pl.semaphore_wait(barrier, depth + 1)
    begin(0)
    begin(1)
    first(0)
    begin(2)
    first(1)
    second(0)

    def gathered(c):
        return land[c].reshape(total, BLOCK)

    def before(k):
        n = k * BLOCK
        top = [over_rows(gathered(m), gathered(k)) for m in range(k)]
        corner = over_rows(gathered(k), gathered(k))
        if k:
            c_high, c_low = split(jnp.concatenate(top, axis=0))
            r = product(high[:n, :n], c_high) + (
                product(high[:n, :n], c_low) + product(low[:n, :n], c_high)
            )
            one, two = split(r)
            r_high[:n, :] = one
            r_low[:n, :] = two
            corner -= over_rows(one, one) + (over_rows(one, two) + over_rows(two, one))
        a[...] = corner

    def between(s):
        size = t.shape[1] // 4
        at = slice(s * size, (s + 1) * size)
        t[:, at] = over_rows(r_high[...], high[:, at]) + (
            over_rows(r_high[...], low[:, at]) + over_rows(r_low[...], high[:, at])
        )

    def after(k):
        at = pl.ds(pl.multiple_of(k * BLOCK, BLOCK), BLOCK)
        w_high, w_low = split(w[...])
        t_high, t_low = split(t[...])
        left = product(w_high, t_high) + (product(w_high, t_low) + product(w_low, t_high))
        one, two = split(-left)
        high[at, :] = one
        low[at, :] = two
        high[at, at] = w_high
        low[at, at] = w_low
        both = sum(
            lax.dot_general(
                own[...],
                part,
                (((1,), (1,)), ((), ())),
                preferred_element_type=jnp.float32,
            )
            for part in (high[at, :], low[at, :])
        )
        out[:, at] = both * scale

    def step(k, carry):
        for side in range(2):
            share(k, side).wait_recv()
        guarded(k + 3, begin)
        for i in range(chunks):
            pl.when(k == i)(functools.partial(before, i))
        guarded(k + 2, first)
        inverse_factor(a, w, between)
        guarded(k + 1, second)
        after(k)
        return carry

    lax.fori_loop(0, chunks, step, 0)

    def finish(c, carry):
        for d in range(depth - 1):
            along(c, d).wait_send()
        for d in range(depth):
            over(c, d).wait_send()
        for side in range(2):
            share(c, side).wait_send()
        return carry

    lax.fori_loop(0, chunks, finish, 0)


def whiten_ring(pooled, collective_id):
    devices = lax.axis_size("dp")
    depth = devices // 4
    rows, width = pooled.shape
    chunks = width // BLOCK
    dma = pltpu.SemaphoreType.DMA
    whole = pl.BlockSpec(memory_space=pltpu.VMEM)
    return pl.pallas_call(
        functools.partial(whiten_ring_kernel, math.sqrt(rows * devices)),
        out_shape=jax.ShapeDtypeStruct((rows, width), jnp.float32),
        in_specs=[whole],
        out_specs=whole,
        scratch_shapes=[
            pltpu.VMEM((chunks, 2, 2, depth, rows, BLOCK), pooled.dtype),
            pltpu.VMEM((width, width), jnp.bfloat16),
            pltpu.VMEM((width, width), jnp.bfloat16),
            pltpu.VMEM((width, BLOCK), jnp.bfloat16),
            pltpu.VMEM((width, BLOCK), jnp.bfloat16),
            pltpu.VMEM((BLOCK, width), jnp.float32),
            pltpu.VMEM((BLOCK, BLOCK), jnp.float32),
            pltpu.VMEM((BLOCK, BLOCK), jnp.float32),
            dma((chunks, depth - 1)),
            dma((chunks, depth - 1)),
            dma((chunks, depth)),
            dma((chunks, depth)),
            dma((chunks, 2)),
            dma((chunks, 2)),
        ],
        compiler_params=pltpu.CompilerParams(
            collective_id=collective_id, has_side_effects=True, vmem_limit_bytes=40 << 20
        ),
    )(pooled)


def weights_kernel(
    chips, tokens, mask, spans, gain, shift, bias, up, down, pooled,
    ups, downs, normed, select, sums, inner, ring_send, ring_recv, x_send, x_recv,
    core_send, core_recv, own_sem,
):
    me, group = lax.axis_index("dp"), lax.axis_index("groups")
    core, chip = lax.rem(me, 2), me // 2
    half = chips // 2
    odd = lax.rem(chip, 2)
    place = (1 - odd) * (chip // 2) + odd * (chips - 1 - chip // 2)
    turn = 1 - 2 * core
    partner = me + turn
    steps = (half, chips - 1 - half)

    def chip_at(q):
        q = lax.rem(q + 2 * chips, chips)
        back = q // half
        return (1 - back) * 2 * q + back * (2 * (chips - 1 - q) + 1)

    beside = [{"dp": 2 * chip_at(place + d) + core} for d in (turn, -turn)]
    mate, opposite = {"dp": partner}, {"groups": 1 - group}
    barrier = pltpu.get_barrier_semaphore()
    for other in (*beside, mate, opposite):
        pl.semaphore_signal(
            barrier, inc=1, device_id=other, device_id_type=pl.DeviceIdType.MESH
        )

    units = (up.shape[0] // 16, down.shape[1] // BLOCK)
    grain = (16, BLOCK)
    parts = []
    for a in range(2):
        side = units[a] * 5 // 16
        size, head = side * grain[a], (units[a] - 2 * side) * grain[a]
        mine = pl.multiple_of(head + group * size, grain[a])
        theirs = pl.multiple_of(head + (1 - group) * size, grain[a])
        parts.append(((mine, size), (0, head), (theirs, size)))

    def view(a, ref, part):
        if part is None:
            return ref
        start, size = parts[a][part]
        return ref.at[pl.ds(start, size)] if a == 0 else ref.at[:, pl.ds(start, size)]

    ins, full = (up, down), (ups, downs)

    def remote(a, source, slot, part, sems, target):
        return pltpu.make_async_remote_copy(
            src_ref=view(a, source, part),
            dst_ref=view(a, full[a].at[slot], part),
            send_sem=sems[0],
            recv_sem=sems[1],
            device_id=target,
            device_id_type=pl.DeviceIdType.MESH,
        )

    def came(way, hop):
        return 2 * chip_at(place - (1 + hop) * turn * (1 - 2 * way)) + core

    def ring(a, way, hop, part):
        slot = me if hop == 0 else came(way, hop - 1)
        source = ins[a] if hop == 0 else full[a].at[slot]
        at = (a, way, hop, part)
        return remote(a, source, slot, part, (ring_send.at[at], ring_recv.at[at]), beside[way])

    def swap(a, way, hop):
        slot = came(way, hop)
        at = (a, way * half + hop)
        return remote(a, full[a].at[slot], slot, 0, (x_send.at[at], x_recv.at[at]), opposite)

    def share(a, way, hop, part):
        slot = came(way, hop)
        at = (a, 1 + way * half + hop, part)
        return remote(
            a, full[a].at[slot], slot, part, (core_send.at[at], core_recv.at[at]), mate
        )

    def share_own(a):
        at = (a, 0, 0)
        return remote(a, ins[a], me, None, (core_send.at[at], core_recv.at[at]), mate)

    own = [pltpu.make_async_copy(ins[a], full[a].at[me], own_sem.at[a]) for a in range(2)]
    started = []

    def go(copy):
        copy.start()
        started.append(copy)

    def ways(hop):
        return [way for way in range(2) if 0 <= hop < steps[way]]

    def pass_on(a, hop, part):
        for way in ways(hop):
            ring(a, way, hop, part).wait_recv()
            if hop + 1 < steps[way]:
                go(ring(a, way, hop + 1, part))
            if part == 0:
                go(swap(a, way, hop))
            go(share(a, way, hop, part))

    def take(a, hop):
        for way in ways(hop):
            arrived = remote(
                a, full[a].at[came(way, hop)], came(way, hop), 2,
                (x_send.at[a, way * half + hop], x_recv.at[a, way * half + hop]), opposite,
            )
            arrived.wait_recv()
            go(share(a, way, hop, 2))

    def settle(a, hop):
        for way in ways(hop):
            for part in range(3):
                share(a, way, hop, part).wait_recv()

    def around(hop):
        return [chip_at(place - (1 + hop) * turn * (1 - 2 * way)) for way in ways(hop)]

    count, width = tokens.shape
    tile = 256
    over_last = (((1,), (1,)), ((), ()))

    def expand(q):
        size = up.shape[0]

        def one(s, carry):
            slot = 2 * q + s
            weights = ups.at[slot]

            def part(i, carry):
                at = pl.ds(pl.multiple_of(i * tile, tile), tile)
                before = bias[slot] + lax.dot_general(
                    normed[at, :], weights[...], over_last, preferred_element_type=jnp.float32
                )
                hidden = 0.5 * before * (1.0 + lax.erf(before * math.sqrt(0.5)))
                inner[...] += jnp.dot(
                    select[i], hidden.astype(normed.dtype), preferred_element_type=jnp.float32
                )
                return carry

            inner[...] = jnp.zeros(inner.shape, inner.dtype)
            lax.fori_loop(0, count // tile, part, 0)
            sums[:, pl.ds(pl.multiple_of(slot * size, BLOCK), size)] = inner[...].astype(
                sums.dtype
            )
            return carry

        lax.fori_loop(0, 2, one, 0)

    def contract(q):
        weights = downs[pl.ds(2 * q, 2)].reshape(2 * down.shape[0], down.shape[1])
        at = pl.ds(pl.multiple_of(q * BLOCK, BLOCK), BLOCK)
        total = lax.dot_general(
            sums[...], weights, over_last, preferred_element_type=jnp.float32
        )
        labels = jnp.zeros((select.shape[1], 1), jnp.float32)
        for i in range(count // tile):
            rows = slice(i * tile, (i + 1) * tile)
            total += jnp.dot(select[i], tokens[rows, at], preferred_element_type=jnp.float32)
            labels += jnp.sum(select[i].astype(jnp.float32), axis=1, keepdims=True)
        pooled[:, at] = (total / jnp.maximum(labels, 1.0)).astype(pooled.dtype)

    for copy in own:
        copy.start()
    pl.semaphore_wait(barrier, 4)
    for a in range(2):
        for part in range(2):
            for way in range(2):
                go(ring(a, way, 0, part))
        go(share_own(a))

    for i in range(count // tile):
        rows = slice(i * tile, (i + 1) * tile)
        values = tokens[rows, :].astype(jnp.float32)
        center = jnp.mean(values, axis=1, keepdims=True)
        spread_of = jnp.mean((values - center) ** 2, axis=1, keepdims=True)
        normed[rows, :] = (
            (values - center) * lax.rsqrt(spread_of + 1e-05) * gain[...] + shift[...]
        ).astype(normed.dtype)
        labels = lax.broadcasted_iota(jnp.int32, (select.shape[1], tile), 0)
        select[i] = jnp.where(
            (spans[:, rows] == labels) & (mask[:, rows] == 1), 1.0, 0.0
        ).astype(select.dtype)

    for copy in own:
        copy.wait()
    for a in range(2):
        share_own(a).wait_recv()
    expand(chip)

    for hop in range(half):
        for part in range(2):
            pass_on(0, hop, part)
        for part in range(2):
            pass_on(1, hop - 1, part)
        take(0, hop - 1)
        take(1, hop - 2)
        settle(0, hop - 1)
        for q in around(hop - 1):
            expand(q)
    last = half - 1
    take(0, last)
    take(1, last - 1)
    pass_on(1, last, 0)
    settle(0, last)
    for q in around(last):
        expand(q)
    contract(chip)
    for hop in range(last):
        settle(1, hop)
        for q in around(hop):
            contract(q)
    pass_on(1, last, 1)
    take(1, last)
    settle(1, last)
    for q in around(last):
        contract(q)
    for copy in started:
        copy.wait_send()


def pooled_spans(tokens, token_mask, span_ids, norm_gain, norm_shift, up, b_up, down, collective_id):
    devices = lax.axis_size("dp")
    chips = devices // 2
    count, width = tokens.shape
    dma = pltpu.SemaphoreType.DMA
    whole = pl.BlockSpec(memory_space=pltpu.VMEM)
    apart = pl.BlockSpec(memory_space=pl.ANY)
    return pl.pallas_call(
        functools.partial(weights_kernel, chips),
        out_shape=jax.ShapeDtypeStruct((SEG_DEV, width), tokens.dtype),
        in_specs=[whole] * 6 + [apart] * 2,
        out_specs=whole,
        scratch_shapes=[
            pltpu.VMEM((devices,) + up.shape, up.dtype),
            pltpu.VMEM((devices,) + down.shape, down.dtype),
            pltpu.VMEM((count, width), tokens.dtype),
            pltpu.VMEM((count // 256, SEG_DEV, 256), tokens.dtype),
            pltpu.VMEM((SEG_DEV, b_up.shape[0]), tokens.dtype),
            pltpu.VMEM((SEG_DEV, up.shape[0]), jnp.float32),
            dma((2, 2, chips // 2, 2)),
            dma((2, 2, chips // 2, 2)),
            dma((2, chips)),
            dma((2, chips)),
            dma((2, chips, 3)),
            dma((2, chips, 3)),
            dma((2,)),
        ],
        compiler_params=pltpu.CompilerParams(
            collective_id=collective_id, has_side_effects=True, vmem_limit_bytes=48 << 20
        ),
    )(
        tokens,
        token_mask,
        span_ids,
        norm_gain.reshape(1, -1),
        norm_shift.reshape(1, -1),
        b_up.reshape(devices, 1, -1),
        up,
        down,
    )


def on_device(tokens, token_mask, span_ids, norm_gain, norm_shift, w_up, b_up, w_down):
    if lax.axis_size("dp") == 16 and lax.axis_size("groups") == 2:
        pooled = pooled_spans(
            tokens, token_mask, span_ids, norm_gain, norm_shift, w_up.T, b_up, w_down.T, 0
        )
        return whiten_ring(pooled, 1)
    values = tokens.astype(jnp.float32)
    center = jnp.mean(values, axis=1, keepdims=True)
    spread = jnp.mean((values - center) ** 2, axis=1, keepdims=True)
    normed = ((values - center) * lax.rsqrt(spread + 1e-05) * norm_gain + norm_shift).astype(
        jnp.bfloat16
    )
    width, hidden_size = tokens.shape[1], b_up.shape[0]
    over_last = (((1,), (1,)), ((), ()))
    if w_up.shape[1] % BLOCK == 0:
        hidden, down_full = ring_up(normed, b_up, w_up.T, w_down.T, 0)
    else:
        up_full, down_full = ring_gather((w_up.T, w_down.T), 0)
        up_full = up_full.reshape(hidden_size, width)
        before = (
            lax.dot_general(normed, up_full, over_last, preferred_element_type=jnp.float32) + b_up
        )
        hidden = jax.nn.gelu(before, approximate=False).astype(jnp.bfloat16)
    down_full = down_full.reshape(width, hidden_size)
    projected = lax.dot_general(
        hidden, down_full, over_last, preferred_element_type=jnp.float32
    )
    block_out = (values + projected).astype(jnp.bfloat16)
    labels = jnp.arange(SEG_DEV, dtype=jnp.int32)[:, None]
    select = (span_ids[0][None, :] == labels) & (token_mask[0][None, :] == 1)
    sums = jnp.dot(select.astype(jnp.bfloat16), block_out, preferred_element_type=jnp.float32)
    counts = jnp.sum(select.astype(jnp.float32), axis=1)
    pooled = (sums / jnp.maximum(counts, 1.0)[:, None]).astype(jnp.bfloat16)
    middle = width // 2
    left, right = (
        half.reshape(-1, middle)
        for half in ring_gather((pooled[:, :middle], pooled[:, middle:]), 1)
    )
    gram = [
        lax.dot_general(one, two, (((0,), (0,)), ((), ())), preferred_element_type=jnp.float32)
        for one, two in ((left, left), (left, right), (right, right))
    ]
    total_rows = SEG_DEV * lax.axis_size("dp")
    return whiten(gram, pooled.astype(jnp.float32).T, math.sqrt(total_rows)).T


def solution(mesh):
    in_specs = (
        P(("groups", "dp"), None),
        P(("groups", "dp"), None),
        P(("groups", "dp"), None),
        P(),
        P(),
        P(None, "dp"),
        P(),
        P(None, "dp"),
    )
    out_specs = P(("groups", "dp"), None)
    return jax.shard_map(
        on_device, mesh=mesh, in_specs=in_specs, out_specs=out_specs, check_vma=False
    )
```

```python
import functools
import math

import jax
import jax.numpy as jnp
from jax import lax
from jax.experimental import pallas as pl
from jax.experimental.pallas import tpu as pltpu
from jax.sharding import PartitionSpec as P

SEG_DEV = 192
BLOCK = 128
HIGHEST = lax.Precision.HIGHEST


def inverse_block(src, dst):
    lane = lax.broadcasted_iota(jnp.int32, (8, BLOCK), 1)
    sub = lax.broadcasted_iota(jnp.int32, (8, BLOCK), 0)
    groups = BLOCK // 8
    held = [src[8 * q : 8 * q + 8, :BLOCK] for q in range(groups)]

    def column(block, c):
        return jnp.broadcast_to(block[:, c : c + 1], (8, BLOCK))

    def row(block, r):
        return jnp.broadcast_to(block[r : r + 1, :], (8, BLOCK))

    for p in range(groups):
        at = 8 * p
        inside = (lane >= at) & (lane < at + 8)
        raw = held[p]
        cols = [column(raw, at + c) for c in range(8)]
        work = jnp.where(inside, jnp.where(lane - at == sub, 1.0, 0.0), raw)
        done = jnp.zeros((8, BLOCK), jnp.float32)
        for j in range(8):
            here = sub == j
            pivot = row(cols[j], j)
            inv = 1.0 / pivot
            done = jnp.where(here, work * lax.rsqrt(pivot), done)
            scaled = row(work, j) * inv
            work = jnp.where(here, scaled, work - cols[j] * scaled)
            for c in range(j + 1, 8):
                scaled = row(cols[c], j) * inv
                cols[c] = jnp.where(here, scaled, cols[c] - cols[j] * scaled)
        dst[at : at + 8, :] = jnp.where(lane <= at + sub, done, 0.0)
        rows = [row(work, c) for c in range(8)]
        for q in range(p + 1, groups):
            total = jnp.where(inside, 0.0, held[q])
            for c in range(8):
                total = total - column(held[q], at + c) * rows[c]
            held[q] = total


def whiten_kernel(scale, first_ref, cross_ref, last_ref, rows_ref, out_ref, a, panel, inv):
    half = first_ref.shape[0]
    n = 2 * half
    extra = rows_ref.shape[1]
    a[:half, :half] = first_ref[...]
    a[:half, half:n] = cross_ref[...]
    a[half:, :half] = jnp.zeros((half, half), jnp.float32)
    a[half:, half:n] = last_ref[...]
    a[:, n:] = jnp.zeros((n, a.shape[1] - n), jnp.float32)
    a[:, n : n + extra] = rows_ref[...]
    blocks = n // BLOCK

    def step(k, carry):
        lo = pl.multiple_of(k * BLOCK, BLOCK)
        panel[:, :BLOCK] = a[pl.ds(lo, BLOCK), pl.ds(lo, BLOCK)]
        inverse_block(panel, inv)
        panel[...] = jnp.dot(
            inv[...], a[pl.ds(lo, BLOCK), :], preferred_element_type=jnp.float32, precision=HIGHEST
        )
        out_ref[pl.ds(lo, BLOCK), :] = panel[:, n : n + extra] * scale

        for first in range(0, blocks, 2):
            start = first * BLOCK

            def trail(i, carry, start=start):
                hi = pl.multiple_of(i * BLOCK, BLOCK)
                left = panel[:, pl.ds(hi, BLOCK)].T
                a[pl.ds(hi, BLOCK), start:] -= jnp.dot(
                    left, panel[:, start:], preferred_element_type=jnp.float32, precision=HIGHEST
                )
                return carry

            lax.fori_loop(jnp.maximum(k + 1, first), min(first + 2, blocks), trail, 0)
        return carry

    lax.fori_loop(0, blocks, step, 0)


def whiten(gram, rows_t, scale):
    n, extra = rows_t.shape
    wide = n + (extra + BLOCK - 1) // BLOCK * BLOCK
    return pl.pallas_call(
        functools.partial(whiten_kernel, scale),
        out_shape=jax.ShapeDtypeStruct((n, extra), jnp.float32),
        in_specs=[pl.BlockSpec(memory_space=pltpu.VMEM)] * 4,
        out_specs=pl.BlockSpec(memory_space=pltpu.VMEM),
        scratch_shapes=[
            pltpu.VMEM((n, wide), jnp.float32),
            pltpu.VMEM((BLOCK, wide), jnp.float32),
            pltpu.VMEM((BLOCK, BLOCK), jnp.float32),
        ],
        compiler_params=pltpu.CompilerParams(vmem_limit_bytes=32 << 20),
    )(*gram, rows_t)


def ring_kernel(chips, count, fused, *refs):
    if fused:
        normed, bias, up, down, hidden, down_out, up_out = refs[:7]
        ins, outs, refs = (up, down), (up_out, down_out), refs[7:]
    else:
        ins, outs, refs = refs[:count], refs[count : 2 * count], refs[2 * count :]
    ring_send, ring_recv, core_send, core_recv, own_sem = refs
    me = lax.axis_index("dp")
    core, chip = lax.rem(me, 2), me // 2
    half = chips // 2
    odd = lax.rem(chip, 2)
    place = (1 - odd) * (chip // 2) + odd * (chips - 1 - chip // 2)
    turn = 1 - 2 * core
    partner = me + turn

    def device(q):
        q = lax.rem(q + 2 * chips, chips)
        back = q // half
        return 2 * ((1 - back) * 2 * q + back * (2 * (chips - 1 - q) + 1)) + core

    ahead, behind = device(place + turn), device(place - turn)
    barrier = pltpu.get_barrier_semaphore()
    for other in (ahead, behind, partner):
        pl.semaphore_signal(
            barrier, inc=1, device_id={"dp": other}, device_id_type=pl.DeviceIdType.MESH
        )
    pl.semaphore_wait(barrier, 3)

    steps = (half, chips - 1 - half)
    started, across = [], []

    def send(a, source, slot, way, step):
        copy = pltpu.make_async_remote_copy(
            src_ref=source,
            dst_ref=outs[a].at[slot],
            send_sem=ring_send.at[a, way, step],
            recv_sem=ring_recv.at[a, way, step],
            device_id={"dp": (ahead, behind)[way]},
            device_id_type=pl.DeviceIdType.MESH,
        )
        copy.start()
        started.append(copy)
        return copy

    def share(a, source, slot, index):
        copy = pltpu.make_async_remote_copy(
            src_ref=source,
            dst_ref=outs[a].at[slot],
            send_sem=core_send.at[a, index],
            recv_sem=core_recv.at[a, index],
            device_id={"dp": partner},
            device_id_type=pl.DeviceIdType.MESH,
        )
        copy.start()
        if fused and a == 0:
            first[index] = copy
        else:
            across.append(copy)

    def compute(slot, block):
        size = block.shape[0]
        columns = pl.ds(pl.multiple_of(slot * size, BLOCK), size)
        tile = normed.shape[0] // 3

        def part(t, carry):
            at = pl.ds(pl.multiple_of(t * tile, tile), tile)
            before = lax.dot_general(
                normed[at, :],
                block[...],
                (((1,), (1,)), ((), ())),
                preferred_element_type=jnp.float32,
            )
            before = before + bias[slot]
            hidden[at, columns] = (
                0.5 * before * (1.0 + lax.erf(before * math.sqrt(0.5)))
            ).astype(hidden.dtype)
            return carry

        lax.fori_loop(0, 3, part, 0)

    first = {}

    def partner_block(index, step, way):
        first[index].wait_recv()
        slot = partner
        if index:
            slot = device(place + (1 + step) * turn * (1 - 2 * way)) + turn
        compute(slot, outs[0].at[slot])

    flying, local = {}, []
    for a in range(count):
        for way in range(2):
            flying[a, way] = send(a, ins[a], me, way, 0)
        share(a, ins[a], me, 0)
        if not (fused and a == 0):
            local.append(pltpu.make_async_copy(ins[a], outs[a].at[me], own_sem.at[a]))
            local[-1].start()
    if fused:
        compute(me, ins[0])
    for step in range(half):
        landed = []
        if fused:
            if step == 0:
                partner_block(0, 0, 0)
            for way in range(2):
                if 0 < step <= steps[way]:
                    partner_block(way * half + step, step - 1, way)
        for a in range(count):
            for way in range(2):
                if step >= steps[way]:
                    continue
                flying[a, way].wait_recv()
                slot = device(place - (1 + step) * turn * (1 - 2 * way))
                block = outs[a].at[slot]
                if step + 1 < steps[way]:
                    flying[a, way] = send(a, block, slot, way, step + 1)
                share(a, block, slot, 1 + way * half + step)
                if fused and a == 0:
                    landed.append((slot, block))
        for slot, block in landed:
            compute(slot, block)
    if fused:
        for way in range(2):
            if steps[way] == half:
                partner_block(way * half + half, half - 1, way)
        for copy in first.values():
            copy.wait_send()
    for copy in local:
        copy.wait()
    for copy in started:
        copy.wait_send()
    for copy in across:
        copy.wait()


def ring_gather(blocks, collective_id):
    devices = lax.axis_size("dp")
    chips, count = devices // 2, len(blocks)
    dma = pltpu.SemaphoreType.DMA
    return pl.pallas_call(
        functools.partial(ring_kernel, chips, count, False),
        out_shape=[jax.ShapeDtypeStruct((devices,) + b.shape, b.dtype) for b in blocks],
        in_specs=[pl.BlockSpec(memory_space=pl.ANY)] * count,
        out_specs=[pl.BlockSpec(memory_space=pl.ANY)] * count,
        scratch_shapes=[
            dma((count, 2, chips // 2)),
            dma((count, 2, chips // 2)),
            dma((count, chips)),
            dma((count, chips)),
            dma((count,)),
        ],
        compiler_params=pltpu.CompilerParams(collective_id=collective_id, has_side_effects=True),
    )(*blocks)


def ring_up(normed, bias, up, down, collective_id):
    devices = lax.axis_size("dp")
    chips = devices // 2
    dma = pltpu.SemaphoreType.DMA
    whole = pl.BlockSpec(memory_space=pltpu.VMEM)
    apart = pl.BlockSpec(memory_space=pl.ANY)
    return pl.pallas_call(
        functools.partial(ring_kernel, chips, 2, True),
        out_shape=[
            jax.ShapeDtypeStruct((normed.shape[0], devices * up.shape[0]), normed.dtype),
            jax.ShapeDtypeStruct((devices,) + down.shape, down.dtype),
        ],
        in_specs=[whole, whole, whole, apart],
        out_specs=[whole, apart],
        scratch_shapes=[
            pltpu.VMEM((devices,) + up.shape, up.dtype),
            dma((2, 2, chips // 2)),
            dma((2, 2, chips // 2)),
            dma((2, chips)),
            dma((2, chips)),
            dma((2,)),
        ],
        compiler_params=pltpu.CompilerParams(
            collective_id=collective_id, has_side_effects=True, vmem_limit_bytes=40 << 20
        ),
    )(normed, bias.reshape(devices, 1, -1), up, down)


def spread(block, r):
    return jnp.broadcast_to(block[r : r + 1, :], (8, BLOCK))


def strip_factor(a, dst, base, groups):
    lane = lax.broadcasted_iota(jnp.int32, (8, BLOCK), 1)
    sub = lax.broadcasted_iota(jnp.int32, (8, BLOCK), 0)
    h = [a[base + 8 * q : base + 8 * q + 8, :] for q in range(groups)]

    def fetch(p):
        return {
            (c, q): jnp.broadcast_to(
                h[q][:, base + 8 * p + c : base + 8 * p + c + 1], (8, BLOCK)
            )
            for q in range(p, groups)
            for c in range(8)
        }

    cols = fetch(0)
    for p in range(groups):
        more = p + 1 < groups
        following = fetch(p + 1) if more else {}
        at = base + 8 * p
        inside = (lane >= at) & (lane < at + 8)
        work = jnp.where(inside, jnp.where(lane - at == sub, 1.0, 0.0), h[p])
        for q in range(p + 1, groups):
            h[q] = jnp.where(inside, 0.0, h[q])
        pivots = jnp.zeros((8, BLOCK), jnp.float32)
        for j in range(8):
            pivot = spread(cols[j, p], j)
            inv = 1.0 / pivot
            pivots = jnp.where(sub == j, pivot, pivots)
            for c in range(j + 1, 8):
                m = spread(cols[j, p], c) * inv
                for q in range(p, groups):
                    cols[c, q] = cols[c, q] - cols[j, q] * m
            if more:
                for c in range(8):
                    m = spread(cols[j, p + 1], c) * inv
                    for q in range(p + 1, groups):
                        following[c, q] = following[c, q] - cols[j, q] * m
            scaled = spread(work, j) * inv
            if j < 7:
                work = work - jnp.where(sub > j, cols[j, p], 0.0) * scaled
            for q in range(p + 1, groups):
                h[q] = h[q] - cols[j, q] * scaled
        dst[at : at + 8, :] = work * lax.rsqrt(pivots)
        cols = following


def over_rows(left, right, precision=None):
    return lax.dot_general(
        left,
        right,
        (((0,), (0,)), ((), ())),
        preferred_element_type=jnp.float32,
        precision=precision,
    )


def inverse_factor(a, dst, between):
    size = 32
    for base in range(0, BLOCK, size):
        strip_factor(a, dst, base, size // 8)
        between(base // size)
        lo = base + size
        if lo < BLOCK:
            rows = dst[base:lo, :]
            r = lax.broadcasted_iota(jnp.int32, (size, BLOCK), 0) + base
            c = lax.broadcasted_iota(jnp.int32, (size, BLOCK), 1)
            drop = over_rows(rows, jnp.where((c > r) & (c < lo), 0.0, rows), HIGHEST)
            c = lax.broadcasted_iota(jnp.int32, (BLOCK - lo, BLOCK), 1)
            a[lo:, :] = jnp.where((c >= base) & (c < lo), 0.0, a[lo:, :]) - drop[lo:, :]
    r = lax.broadcasted_iota(jnp.int32, (BLOCK, BLOCK), 0)
    c = lax.broadcasted_iota(jnp.int32, (BLOCK, BLOCK), 1)
    dst[...] = jnp.where(c <= r, dst[...], 0.0)


def product(left, right):
    return jnp.dot(left, right, preferred_element_type=jnp.float32)


def split(x):
    high = x.astype(jnp.bfloat16)
    return high, (x - high.astype(jnp.float32)).astype(jnp.bfloat16)


def whiten_ring_kernel(
    scale, own, out, land, high, low, r_high, r_low, t, a, w, z_send, z_recv, y_send, y_recv, core_send, core_recv
):
    me = lax.axis_index("dp")
    core, y, z = lax.rem(me, 2), lax.rem(me // 2, 2), me // 4
    depth = land.shape[3]
    chunks = own.shape[1] // BLOCK
    rows = own.shape[0]
    total = 4 * depth * rows
    partner, across = me + 1 - 2 * core, me + 2 - 4 * y
    line = [lax.rem(z + d, depth) for d in range(1, depth)]

    barrier = pltpu.get_barrier_semaphore()
    others = [4 * other + 2 * y + core for other in line] + [partner, across]
    for other in others:
        pl.semaphore_signal(
            barrier, inc=1, device_id={"dp": other}, device_id_type=pl.DeviceIdType.MESH
        )

    def remote(ref, send_sem, recv_sem, target):
        return pltpu.make_async_remote_copy(
            src_ref=ref,
            dst_ref=ref,
            send_sem=send_sem,
            recv_sem=recv_sem,
            device_id={"dp": target},
            device_id_type=pl.DeviceIdType.MESH,
        )

    def along(c, d):
        return remote(land.at[c, y, core, z], z_send.at[c, d], z_recv.at[c, d], others[d])

    def over(c, d):
        slot = z if d == depth - 1 else lax.rem(z + depth - 1 - d, depth)
        return remote(land.at[c, y, core, slot], y_send.at[c, d], y_recv.at[c, d], across)

    def share(c, side):
        ref = land.at[c, (1 - y) if side else y, core]
        return remote(ref, core_send.at[c, side], core_recv.at[c, side], partner)

    def begin(c):
        for d in range(depth - 1):
            along(c, d).start()
        over(c, depth - 1).start()

    def first(c):
        for d in range(depth - 1):
            along(c, d).wait_recv()
            over(c, d).start()
        share(c, 0).start()

    def second(c):
        for d in range(depth):
            over(c, d).wait_recv()
        share(c, 1).start()

    def guarded(c, what):
        pl.when(c < chunks)(lambda: what(c))

    for c in range(chunks):
        land[c, y, core, z] = own[:, c * BLOCK : (c + 1) * BLOCK]
    for ref in (high, low, r_high, r_low):
        ref[...] = jnp.zeros(ref.shape, ref.dtype)
    pl.semaphore_wait(barrier, depth + 1)
    begin(0)
    begin(1)
    first(0)
    begin(2)
    first(1)
    second(0)

    def gathered(c):
        return land[c].reshape(total, BLOCK)

    def before(k):
        n = k * BLOCK
        top = [over_rows(gathered(m), gathered(k)) for m in range(k)]
        corner = over_rows(gathered(k), gathered(k))
        if k:
            c_high, c_low = split(jnp.concatenate(top, axis=0))
            r = product(high[:n, :n], c_high) + (
                product(high[:n, :n], c_low) + product(low[:n, :n], c_high)
            )
            one, two = split(r)
            r_high[:n, :] = one
            r_low[:n, :] = two
            corner -= over_rows(one, one) + (over_rows(one, two) + over_rows(two, one))
        a[...] = corner

    def between(s):
        size = t.shape[1] // 4
        at = slice(s * size, (s + 1) * size)
        t[:, at] = over_rows(r_high[...], high[:, at]) + (
            over_rows(r_high[...], low[:, at]) + over_rows(r_low[...], high[:, at])
        )

    def after(k):
        at = pl.ds(pl.multiple_of(k * BLOCK, BLOCK), BLOCK)
        w_high, w_low = split(w[...])
        t_high, t_low = split(t[...])
        left = product(w_high, t_high) + (product(w_high, t_low) + product(w_low, t_high))
        one, two = split(-left)
        high[at, :] = one
        low[at, :] = two
        high[at, at] = w_high
        low[at, at] = w_low
        both = sum(
            lax.dot_general(
                own[...],
                part,
                (((1,), (1,)), ((), ())),
                preferred_element_type=jnp.float32,
            )
            for part in (high[at, :], low[at, :])
        )
        out[:, at] = both * scale

    def step(k, carry):
        for side in range(2):
            share(k, side).wait_recv()
        guarded(k + 3, begin)
        for i in range(chunks):
            pl.when(k == i)(functools.partial(before, i))
        guarded(k + 2, first)
        inverse_factor(a, w, between)
        guarded(k + 1, second)
        after(k)
        return carry

    lax.fori_loop(0, chunks, step, 0)

    def finish(c, carry):
        for d in range(depth - 1):
            along(c, d).wait_send()
        for d in range(depth):
            over(c, d).wait_send()
        for side in range(2):
            share(c, side).wait_send()
        return carry

    lax.fori_loop(0, chunks, finish, 0)


def whiten_ring(pooled, collective_id):
    devices = lax.axis_size("dp")
    depth = devices // 4
    rows, width = pooled.shape
    chunks = width // BLOCK
    dma = pltpu.SemaphoreType.DMA
    whole = pl.BlockSpec(memory_space=pltpu.VMEM)
    return pl.pallas_call(
        functools.partial(whiten_ring_kernel, math.sqrt(rows * devices)),
        out_shape=jax.ShapeDtypeStruct((rows, width), jnp.float32),
        in_specs=[whole],
        out_specs=whole,
        scratch_shapes=[
            pltpu.VMEM((chunks, 2, 2, depth, rows, BLOCK), pooled.dtype),
            pltpu.VMEM((width, width), jnp.bfloat16),
            pltpu.VMEM((width, width), jnp.bfloat16),
            pltpu.VMEM((width, BLOCK), jnp.bfloat16),
            pltpu.VMEM((width, BLOCK), jnp.bfloat16),
            pltpu.VMEM((BLOCK, width), jnp.float32),
            pltpu.VMEM((BLOCK, BLOCK), jnp.float32),
            pltpu.VMEM((BLOCK, BLOCK), jnp.float32),
            dma((chunks, depth - 1)),
            dma((chunks, depth - 1)),
            dma((chunks, depth)),
            dma((chunks, depth)),
            dma((chunks, 2)),
            dma((chunks, 2)),
        ],
        compiler_params=pltpu.CompilerParams(
            collective_id=collective_id, has_side_effects=True, vmem_limit_bytes=40 << 20
        ),
    )(pooled)


def weights_kernel(
    chips, tokens_in, mask_in, spans_in, gain_in, shift_in, bias_in, up, down, pooled,
    tokens, mask, spans, gain, shift, bias, ups, downs, normed, select, sums, inner, ring_send, ring_recv, x_send, x_recv,
    core_send, core_recv, own_sem, in_sem,
):
    me, group = lax.axis_index("dp"), lax.axis_index("groups")
    core, chip = lax.rem(me, 2), me // 2
    half = chips // 2
    odd = lax.rem(chip, 2)
    place = (1 - odd) * (chip // 2) + odd * (chips - 1 - chip // 2)
    turn = 1 - 2 * core
    partner = me + turn
    steps = (half, chips - 1 - half)

    def chip_at(q):
        q = lax.rem(q + 2 * chips, chips)
        back = q // half
        return (1 - back) * 2 * q + back * (2 * (chips - 1 - q) + 1)

    beside = [{"dp": 2 * chip_at(place + d) + core} for d in (turn, -turn)]
    mate, opposite = {"dp": partner}, {"groups": 1 - group}
    barrier = pltpu.get_barrier_semaphore()
    for other in (*beside, mate, opposite):
        pl.semaphore_signal(
            barrier, inc=1, device_id=other, device_id_type=pl.DeviceIdType.MESH
        )

    units = (up.shape[0] // 16, down.shape[1] // BLOCK)
    grain = (16, BLOCK)
    parts = []
    for a in range(2):
        side = units[a] * 5 // 16
        size, head = side * grain[a], (units[a] - 2 * side) * grain[a]
        mine = pl.multiple_of(head + group * size, grain[a])
        theirs = pl.multiple_of(head + (1 - group) * size, grain[a])
        parts.append(((mine, size), (0, head), (theirs, size)))

    def view(a, ref, part):
        if part is None:
            return ref
        start, size = parts[a][part]
        return ref.at[pl.ds(start, size)] if a == 0 else ref.at[:, pl.ds(start, size)]

    ins, full = (up, down), (ups, downs)

    def remote(a, source, slot, part, sems, target):
        return pltpu.make_async_remote_copy(
            src_ref=view(a, source, part),
            dst_ref=view(a, full[a].at[slot], part),
            send_sem=sems[0],
            recv_sem=sems[1],
            device_id=target,
            device_id_type=pl.DeviceIdType.MESH,
        )

    def came(way, hop):
        return 2 * chip_at(place - (1 + hop) * turn * (1 - 2 * way)) + core

    def ring(a, way, hop, part):
        slot = me if hop == 0 else came(way, hop - 1)
        source = ins[a] if hop == 0 else full[a].at[slot]
        at = (a, way, hop, part)
        return remote(a, source, slot, part, (ring_send.at[at], ring_recv.at[at]), beside[way])

    def swap(a, way, hop):
        slot = came(way, hop)
        at = (a, way * half + hop)
        return remote(a, full[a].at[slot], slot, 0, (x_send.at[at], x_recv.at[at]), opposite)

    def share(a, way, hop, part):
        slot = came(way, hop)
        at = (a, 1 + way * half + hop, part)
        return remote(
            a, full[a].at[slot], slot, part, (core_send.at[at], core_recv.at[at]), mate
        )

    def share_own(a):
        at = (a, 0, 0)
        return remote(a, ins[a], me, None, (core_send.at[at], core_recv.at[at]), mate)

    own = [pltpu.make_async_copy(ins[a], full[a].at[me], own_sem.at[a]) for a in range(2)]
    started = []

    def go(copy):
        copy.start()
        started.append(copy)

    def ways(hop):
        return [way for way in range(2) if 0 <= hop < steps[way]]

    def pass_on(a, hop, part):
        for way in ways(hop):
            ring(a, way, hop, part).wait_recv()
            if hop + 1 < steps[way]:
                go(ring(a, way, hop + 1, part))
            if part == 0:
                go(swap(a, way, hop))
            go(share(a, way, hop, part))

    def take(a, hop):
        for way in ways(hop):
            arrived = remote(
                a, full[a].at[came(way, hop)], came(way, hop), 2,
                (x_send.at[a, way * half + hop], x_recv.at[a, way * half + hop]), opposite,
            )
            arrived.wait_recv()
            go(share(a, way, hop, 2))

    def settle(a, hop):
        for way in ways(hop):
            for part in range(3):
                share(a, way, hop, part).wait_recv()

    def around(hop):
        return [chip_at(place - (1 + hop) * turn * (1 - 2 * way)) for way in ways(hop)]

    count, width = tokens.shape
    tile = 256
    over_last = (((1,), (1,)), ((), ()))

    def expand(q):
        size = up.shape[1]

        def one(s, carry):
            slot = 2 * q + s
            weights = ups.at[slot]

            def part(i, carry):
                at = pl.ds(pl.multiple_of(i * tile, tile), tile)
                before = bias[slot] + jnp.dot(
                    normed[at, :], weights[...], preferred_element_type=jnp.float32
                )
                hidden = 0.5 * before * (1.0 + lax.erf(before * math.sqrt(0.5)))
                inner[...] += jnp.dot(
                    select[i], hidden.astype(normed.dtype), preferred_element_type=jnp.float32
                )
                return carry

            inner[...] = jnp.zeros(inner.shape, inner.dtype)
            lax.fori_loop(0, count // tile, part, 0)
            sums[:, pl.ds(pl.multiple_of(slot * size, BLOCK), size)] = inner[...].astype(
                sums.dtype
            )
            return carry

        lax.fori_loop(0, 2, one, 0)

    def contract(q):
        weights = downs[pl.ds(2 * q, 2)].reshape(2 * down.shape[0], down.shape[1])
        at = pl.ds(pl.multiple_of(q * BLOCK, BLOCK), BLOCK)
        total = lax.dot_general(
            sums[...], weights, over_last, preferred_element_type=jnp.float32
        )
        labels = jnp.zeros((select.shape[1], 1), jnp.float32)
        for i in range(count // tile):
            rows = slice(i * tile, (i + 1) * tile)
            total += jnp.dot(select[i], tokens[rows, at], preferred_element_type=jnp.float32)
            labels += jnp.sum(select[i].astype(jnp.float32), axis=1, keepdims=True)
        pooled[:, at] = (total / jnp.maximum(labels, 1.0)).astype(pooled.dtype)

    arguments = [
        pltpu.make_async_copy(source, target, in_sem.at[i])
        for i, (source, target) in enumerate(
            (
                (tokens_in, tokens),
                (mask_in, mask),
                (spans_in, spans),
                (gain_in, gain),
                (shift_in, shift),
                (bias_in, bias),
            )
        )
    ]
    for copy in arguments:
        copy.start()
    pl.semaphore_wait(barrier, 4)
    for a in range(2):
        for part in range(2):
            for way in range(2):
                go(ring(a, way, 0, part))
        go(share_own(a))
    for copy in own:
        copy.start()
    for copy in arguments:
        copy.wait()

    for i in range(count // tile):
        rows = slice(i * tile, (i + 1) * tile)
        values = tokens[rows, :].astype(jnp.float32)
        center = jnp.mean(values, axis=1, keepdims=True)
        spread_of = jnp.mean((values - center) ** 2, axis=1, keepdims=True)
        normed[rows, :] = (
            (values - center) * lax.rsqrt(spread_of + 1e-05) * gain[...] + shift[...]
        ).astype(normed.dtype)
        labels = lax.broadcasted_iota(jnp.int32, (select.shape[1], tile), 0)
        select[i] = jnp.where(
            (spans[:, rows] == labels) & (mask[:, rows] == 1), 1.0, 0.0
        ).astype(select.dtype)

    for hop in range(half):
        for part in range(2):
            pass_on(0, hop, part)
        if hop == 0:
            for copy in own:
                copy.wait()
            share_own(0).wait_recv()
            expand(chip)
        take(1, hop - 1)
        pass_on(1, hop, 0)
        if hop + 1 < half:
            pass_on(1, hop, 1)
        take(0, hop)
        settle(0, hop)
        for q in around(hop):
            expand(q)
    last = half - 1
    share_own(1).wait_recv()
    contract(chip)
    for hop in range(last):
        settle(1, hop)
        for q in around(hop):
            contract(q)
    pass_on(1, last, 1)
    take(1, last)
    settle(1, last)
    for q in around(last):
        contract(q)
    for copy in started:
        copy.wait_send()


def pooled_spans(tokens, token_mask, span_ids, norm_gain, norm_shift, up, b_up, down, collective_id):
    devices = lax.axis_size("dp")
    chips = devices // 2
    count, width = tokens.shape
    dma = pltpu.SemaphoreType.DMA
    whole = pl.BlockSpec(memory_space=pltpu.VMEM)
    apart = pl.BlockSpec(memory_space=pl.ANY)
    return pl.pallas_call(
        functools.partial(weights_kernel, chips),
        out_shape=jax.ShapeDtypeStruct((SEG_DEV, width), tokens.dtype),
        in_specs=[apart] * 8,
        out_specs=whole,
        scratch_shapes=[
            pltpu.VMEM(tokens.shape, tokens.dtype),
            pltpu.VMEM(token_mask.shape, token_mask.dtype),
            pltpu.VMEM(span_ids.shape, span_ids.dtype),
            pltpu.VMEM((1, width), norm_gain.dtype),
            pltpu.VMEM((1, width), norm_shift.dtype),
            pltpu.VMEM((devices, 1, up.shape[1]), b_up.dtype),
            pltpu.VMEM((devices,) + up.shape, up.dtype),
            pltpu.VMEM((devices,) + down.shape, down.dtype),
            pltpu.VMEM((count, width), tokens.dtype),
            pltpu.VMEM((count // 256, SEG_DEV, 256), tokens.dtype),
            pltpu.VMEM((SEG_DEV, b_up.shape[0]), tokens.dtype),
            pltpu.VMEM((SEG_DEV, up.shape[1]), jnp.float32),
            dma((2, 2, chips // 2, 2)),
            dma((2, 2, chips // 2, 2)),
            dma((2, chips)),
            dma((2, chips)),
            dma((2, chips, 3)),
            dma((2, chips, 3)),
            dma((2,)),
            dma((6,)),
        ],
        compiler_params=pltpu.CompilerParams(
            collective_id=collective_id, has_side_effects=True, vmem_limit_bytes=60 << 20
        ),
    )(
        tokens,
        token_mask,
        span_ids,
        norm_gain.reshape(1, -1),
        norm_shift.reshape(1, -1),
        b_up.reshape(devices, 1, -1),
        up,
        down,
    )


def on_device(tokens, token_mask, span_ids, norm_gain, norm_shift, w_up, b_up, w_down):
    if lax.axis_size("dp") == 16 and lax.axis_size("groups") == 2:
        pooled = pooled_spans(
            tokens, token_mask, span_ids, norm_gain, norm_shift, w_up, b_up, w_down.T, 0
        )
        return whiten_ring(pooled, 1)
    values = tokens.astype(jnp.float32)
    center = jnp.mean(values, axis=1, keepdims=True)
    spread = jnp.mean((values - center) ** 2, axis=1, keepdims=True)
    normed = ((values - center) * lax.rsqrt(spread + 1e-05) * norm_gain + norm_shift).astype(
        jnp.bfloat16
    )
    width, hidden_size = tokens.shape[1], b_up.shape[0]
    over_last = (((1,), (1,)), ((), ()))
    if w_up.shape[1] % BLOCK == 0:
        hidden, down_full = ring_up(normed, b_up, w_up.T, w_down.T, 0)
    else:
        up_full, down_full = ring_gather((w_up.T, w_down.T), 0)
        up_full = up_full.reshape(hidden_size, width)
        before = (
            lax.dot_general(normed, up_full, over_last, preferred_element_type=jnp.float32) + b_up
        )
        hidden = jax.nn.gelu(before, approximate=False).astype(jnp.bfloat16)
    down_full = down_full.reshape(width, hidden_size)
    projected = lax.dot_general(
        hidden, down_full, over_last, preferred_element_type=jnp.float32
    )
    block_out = (values + projected).astype(jnp.bfloat16)
    labels = jnp.arange(SEG_DEV, dtype=jnp.int32)[:, None]
    select = (span_ids[0][None, :] == labels) & (token_mask[0][None, :] == 1)
    sums = jnp.dot(select.astype(jnp.bfloat16), block_out, preferred_element_type=jnp.float32)
    counts = jnp.sum(select.astype(jnp.float32), axis=1)
    pooled = (sums / jnp.maximum(counts, 1.0)[:, None]).astype(jnp.bfloat16)
    middle = width // 2
    left, right = (
        half.reshape(-1, middle)
        for half in ring_gather((pooled[:, :middle], pooled[:, middle:]), 1)
    )
    gram = [
        lax.dot_general(one, two, (((0,), (0,)), ((), ())), preferred_element_type=jnp.float32)
        for one, two in ((left, left), (left, right), (right, right))
    ]
    total_rows = SEG_DEV * lax.axis_size("dp")
    return whiten(gram, pooled.astype(jnp.float32).T, math.sqrt(total_rows)).T


def solution(mesh):
    in_specs = (
        P(("groups", "dp"), None),
        P(("groups", "dp"), None),
        P(("groups", "dp"), None),
        P(),
        P(),
        P(None, "dp"),
        P(),
        P(None, "dp"),
    )
    out_specs = P(("groups", "dp"), None)
    return jax.shard_map(
        on_device, mesh=mesh, in_specs=in_specs, out_specs=out_specs, check_vma=False
    )
```

```python
import functools
import math

import jax
import jax.numpy as jnp
from jax import lax
from jax.experimental import pallas as pl
from jax.experimental.pallas import tpu as pltpu
from jax.sharding import PartitionSpec as P

SEG_DEV = 192
BLOCK = 128
HIGHEST = lax.Precision.HIGHEST


def inverse_block(src, dst):
    lane = lax.broadcasted_iota(jnp.int32, (8, BLOCK), 1)
    sub = lax.broadcasted_iota(jnp.int32, (8, BLOCK), 0)
    groups = BLOCK // 8
    held = [src[8 * q : 8 * q + 8, :BLOCK] for q in range(groups)]

    def column(block, c):
        return jnp.broadcast_to(block[:, c : c + 1], (8, BLOCK))

    def row(block, r):
        return jnp.broadcast_to(block[r : r + 1, :], (8, BLOCK))

    for p in range(groups):
        at = 8 * p
        inside = (lane >= at) & (lane < at + 8)
        raw = held[p]
        cols = [column(raw, at + c) for c in range(8)]
        work = jnp.where(inside, jnp.where(lane - at == sub, 1.0, 0.0), raw)
        done = jnp.zeros((8, BLOCK), jnp.float32)
        for j in range(8):
            here = sub == j
            pivot = row(cols[j], j)
            inv = 1.0 / pivot
            done = jnp.where(here, work * lax.rsqrt(pivot), done)
            scaled = row(work, j) * inv
            work = jnp.where(here, scaled, work - cols[j] * scaled)
            for c in range(j + 1, 8):
                scaled = row(cols[c], j) * inv
                cols[c] = jnp.where(here, scaled, cols[c] - cols[j] * scaled)
        dst[at : at + 8, :] = jnp.where(lane <= at + sub, done, 0.0)
        rows = [row(work, c) for c in range(8)]
        for q in range(p + 1, groups):
            total = jnp.where(inside, 0.0, held[q])
            for c in range(8):
                total = total - column(held[q], at + c) * rows[c]
            held[q] = total


def whiten_kernel(scale, first_ref, cross_ref, last_ref, rows_ref, out_ref, a, panel, inv):
    half = first_ref.shape[0]
    n = 2 * half
    extra = rows_ref.shape[1]
    a[:half, :half] = first_ref[...]
    a[:half, half:n] = cross_ref[...]
    a[half:, :half] = jnp.zeros((half, half), jnp.float32)
    a[half:, half:n] = last_ref[...]
    a[:, n:] = jnp.zeros((n, a.shape[1] - n), jnp.float32)
    a[:, n : n + extra] = rows_ref[...]
    blocks = n // BLOCK

    def step(k, carry):
        lo = pl.multiple_of(k * BLOCK, BLOCK)
        panel[:, :BLOCK] = a[pl.ds(lo, BLOCK), pl.ds(lo, BLOCK)]
        inverse_block(panel, inv)
        panel[...] = jnp.dot(
            inv[...], a[pl.ds(lo, BLOCK), :], preferred_element_type=jnp.float32, precision=HIGHEST
        )
        out_ref[pl.ds(lo, BLOCK), :] = panel[:, n : n + extra] * scale

        for first in range(0, blocks, 2):
            start = first * BLOCK

            def trail(i, carry, start=start):
                hi = pl.multiple_of(i * BLOCK, BLOCK)
                left = panel[:, pl.ds(hi, BLOCK)].T
                a[pl.ds(hi, BLOCK), start:] -= jnp.dot(
                    left, panel[:, start:], preferred_element_type=jnp.float32, precision=HIGHEST
                )
                return carry

            lax.fori_loop(jnp.maximum(k + 1, first), min(first + 2, blocks), trail, 0)
        return carry

    lax.fori_loop(0, blocks, step, 0)


def whiten(gram, rows_t, scale):
    n, extra = rows_t.shape
    wide = n + (extra + BLOCK - 1) // BLOCK * BLOCK
    return pl.pallas_call(
        functools.partial(whiten_kernel, scale),
        out_shape=jax.ShapeDtypeStruct((n, extra), jnp.float32),
        in_specs=[pl.BlockSpec(memory_space=pltpu.VMEM)] * 4,
        out_specs=pl.BlockSpec(memory_space=pltpu.VMEM),
        scratch_shapes=[
            pltpu.VMEM((n, wide), jnp.float32),
            pltpu.VMEM((BLOCK, wide), jnp.float32),
            pltpu.VMEM((BLOCK, BLOCK), jnp.float32),
        ],
        compiler_params=pltpu.CompilerParams(vmem_limit_bytes=32 << 20),
    )(*gram, rows_t)


def ring_kernel(chips, count, fused, *refs):
    if fused:
        normed, bias, up, down, hidden, down_out, up_out = refs[:7]
        ins, outs, refs = (up, down), (up_out, down_out), refs[7:]
    else:
        ins, outs, refs = refs[:count], refs[count : 2 * count], refs[2 * count :]
    ring_send, ring_recv, core_send, core_recv, own_sem = refs
    me = lax.axis_index("dp")
    core, chip = lax.rem(me, 2), me // 2
    half = chips // 2
    odd = lax.rem(chip, 2)
    place = (1 - odd) * (chip // 2) + odd * (chips - 1 - chip // 2)
    turn = 1 - 2 * core
    partner = me + turn

    def device(q):
        q = lax.rem(q + 2 * chips, chips)
        back = q // half
        return 2 * ((1 - back) * 2 * q + back * (2 * (chips - 1 - q) + 1)) + core

    ahead, behind = device(place + turn), device(place - turn)
    barrier = pltpu.get_barrier_semaphore()
    for other in (ahead, behind, partner):
        pl.semaphore_signal(
            barrier, inc=1, device_id={"dp": other}, device_id_type=pl.DeviceIdType.MESH
        )
    pl.semaphore_wait(barrier, 3)

    steps = (half, chips - 1 - half)
    started, across = [], []

    def send(a, source, slot, way, step):
        copy = pltpu.make_async_remote_copy(
            src_ref=source,
            dst_ref=outs[a].at[slot],
            send_sem=ring_send.at[a, way, step],
            recv_sem=ring_recv.at[a, way, step],
            device_id={"dp": (ahead, behind)[way]},
            device_id_type=pl.DeviceIdType.MESH,
        )
        copy.start()
        started.append(copy)
        return copy

    def share(a, source, slot, index):
        copy = pltpu.make_async_remote_copy(
            src_ref=source,
            dst_ref=outs[a].at[slot],
            send_sem=core_send.at[a, index],
            recv_sem=core_recv.at[a, index],
            device_id={"dp": partner},
            device_id_type=pl.DeviceIdType.MESH,
        )
        copy.start()
        if fused and a == 0:
            first[index] = copy
        else:
            across.append(copy)

    def compute(slot, block):
        size = block.shape[0]
        columns = pl.ds(pl.multiple_of(slot * size, BLOCK), size)
        tile = normed.shape[0] // 3

        def part(t, carry):
            at = pl.ds(pl.multiple_of(t * tile, tile), tile)
            before = lax.dot_general(
                normed[at, :],
                block[...],
                (((1,), (1,)), ((), ())),
                preferred_element_type=jnp.float32,
            )
            before = before + bias[slot]
            hidden[at, columns] = (
                0.5 * before * (1.0 + lax.erf(before * math.sqrt(0.5)))
            ).astype(hidden.dtype)
            return carry

        lax.fori_loop(0, 3, part, 0)

    first = {}

    def partner_block(index, step, way):
        first[index].wait_recv()
        slot = partner
        if index:
            slot = device(place + (1 + step) * turn * (1 - 2 * way)) + turn
        compute(slot, outs[0].at[slot])

    flying, local = {}, []
    for a in range(count):
        for way in range(2):
            flying[a, way] = send(a, ins[a], me, way, 0)
        share(a, ins[a], me, 0)
        if not (fused and a == 0):
            local.append(pltpu.make_async_copy(ins[a], outs[a].at[me], own_sem.at[a]))
            local[-1].start()
    if fused:
        compute(me, ins[0])
    for step in range(half):
        landed = []
        if fused:
            if step == 0:
                partner_block(0, 0, 0)
            for way in range(2):
                if 0 < step <= steps[way]:
                    partner_block(way * half + step, step - 1, way)
        for a in range(count):
            for way in range(2):
                if step >= steps[way]:
                    continue
                flying[a, way].wait_recv()
                slot = device(place - (1 + step) * turn * (1 - 2 * way))
                block = outs[a].at[slot]
                if step + 1 < steps[way]:
                    flying[a, way] = send(a, block, slot, way, step + 1)
                share(a, block, slot, 1 + way * half + step)
                if fused and a == 0:
                    landed.append((slot, block))
        for slot, block in landed:
            compute(slot, block)
    if fused:
        for way in range(2):
            if steps[way] == half:
                partner_block(way * half + half, half - 1, way)
        for copy in first.values():
            copy.wait_send()
    for copy in local:
        copy.wait()
    for copy in started:
        copy.wait_send()
    for copy in across:
        copy.wait()


def ring_gather(blocks, collective_id):
    devices = lax.axis_size("dp")
    chips, count = devices // 2, len(blocks)
    dma = pltpu.SemaphoreType.DMA
    return pl.pallas_call(
        functools.partial(ring_kernel, chips, count, False),
        out_shape=[jax.ShapeDtypeStruct((devices,) + b.shape, b.dtype) for b in blocks],
        in_specs=[pl.BlockSpec(memory_space=pl.ANY)] * count,
        out_specs=[pl.BlockSpec(memory_space=pl.ANY)] * count,
        scratch_shapes=[
            dma((count, 2, chips // 2)),
            dma((count, 2, chips // 2)),
            dma((count, chips)),
            dma((count, chips)),
            dma((count,)),
        ],
        compiler_params=pltpu.CompilerParams(collective_id=collective_id, has_side_effects=True),
    )(*blocks)


def ring_up(normed, bias, up, down, collective_id):
    devices = lax.axis_size("dp")
    chips = devices // 2
    dma = pltpu.SemaphoreType.DMA
    whole = pl.BlockSpec(memory_space=pltpu.VMEM)
    apart = pl.BlockSpec(memory_space=pl.ANY)
    return pl.pallas_call(
        functools.partial(ring_kernel, chips, 2, True),
        out_shape=[
            jax.ShapeDtypeStruct((normed.shape[0], devices * up.shape[0]), normed.dtype),
            jax.ShapeDtypeStruct((devices,) + down.shape, down.dtype),
        ],
        in_specs=[whole, whole, whole, apart],
        out_specs=[whole, apart],
        scratch_shapes=[
            pltpu.VMEM((devices,) + up.shape, up.dtype),
            dma((2, 2, chips // 2)),
            dma((2, 2, chips // 2)),
            dma((2, chips)),
            dma((2, chips)),
            dma((2,)),
        ],
        compiler_params=pltpu.CompilerParams(
            collective_id=collective_id, has_side_effects=True, vmem_limit_bytes=40 << 20
        ),
    )(normed, bias.reshape(devices, 1, -1), up, down)


def spread(block, r):
    return jnp.broadcast_to(block[r : r + 1, :], (8, BLOCK))


def strip_factor(a, dst, base, groups):
    lane = lax.broadcasted_iota(jnp.int32, (8, BLOCK), 1)
    sub = lax.broadcasted_iota(jnp.int32, (8, BLOCK), 0)
    h = [a[base + 8 * q : base + 8 * q + 8, :] for q in range(groups)]

    def fetch(p):
        return {
            (c, q): jnp.broadcast_to(
                h[q][:, base + 8 * p + c : base + 8 * p + c + 1], (8, BLOCK)
            )
            for q in range(p, groups)
            for c in range(8)
        }

    cols = fetch(0)
    for p in range(groups):
        more = p + 1 < groups
        following = fetch(p + 1) if more else {}
        at = base + 8 * p
        inside = (lane >= at) & (lane < at + 8)
        work = jnp.where(inside, jnp.where(lane - at == sub, 1.0, 0.0), h[p])
        for q in range(p + 1, groups):
            h[q] = jnp.where(inside, 0.0, h[q])
        pivots = jnp.zeros((8, BLOCK), jnp.float32)
        for j in range(8):
            pivot = spread(cols[j, p], j)
            inv = 1.0 / pivot
            pivots = jnp.where(sub == j, pivot, pivots)
            for c in range(j + 1, 8):
                m = spread(cols[j, p], c) * inv
                for q in range(p, groups):
                    cols[c, q] = cols[c, q] - cols[j, q] * m
            if more:
                for c in range(8):
                    m = spread(cols[j, p + 1], c) * inv
                    for q in range(p + 1, groups):
                        following[c, q] = following[c, q] - cols[j, q] * m
            scaled = spread(work, j) * inv
            if j < 7:
                work = work - jnp.where(sub > j, cols[j, p], 0.0) * scaled
            for q in range(p + 1, groups):
                h[q] = h[q] - cols[j, q] * scaled
        dst[at : at + 8, :] = work * lax.rsqrt(pivots)
        cols = following


def over_rows(left, right, precision=None):
    return lax.dot_general(
        left,
        right,
        (((0,), (0,)), ((), ())),
        preferred_element_type=jnp.float32,
        precision=precision,
    )


def inverse_factor(a, dst, between):
    size = 32
    for base in range(0, BLOCK, size):
        strip_factor(a, dst, base, size // 8)
        between(base // size)
        lo = base + size
        if lo < BLOCK:
            rows = dst[base:lo, :]
            r = lax.broadcasted_iota(jnp.int32, (size, BLOCK), 0) + base
            c = lax.broadcasted_iota(jnp.int32, (size, BLOCK), 1)
            drop = over_rows(rows, jnp.where((c > r) & (c < lo), 0.0, rows), HIGHEST)
            c = lax.broadcasted_iota(jnp.int32, (BLOCK - lo, BLOCK), 1)
            a[lo:, :] = jnp.where((c >= base) & (c < lo), 0.0, a[lo:, :]) - drop[lo:, :]
    r = lax.broadcasted_iota(jnp.int32, (BLOCK, BLOCK), 0)
    c = lax.broadcasted_iota(jnp.int32, (BLOCK, BLOCK), 1)
    dst[...] = jnp.where(c <= r, dst[...], 0.0)


def product(left, right):
    return jnp.dot(left, right, preferred_element_type=jnp.float32)


def split(x):
    high = x.astype(jnp.bfloat16)
    return high, (x - high.astype(jnp.float32)).astype(jnp.bfloat16)


def whiten_ring_kernel(
    scale, own, out, land, high, low, r_high, r_low, t, a, w, z_send, z_recv, y_send, y_recv, core_send, core_recv
):
    me = lax.axis_index("dp")
    core, y, z = lax.rem(me, 2), lax.rem(me // 2, 2), me // 4
    depth = land.shape[3]
    chunks = own.shape[1] // BLOCK
    rows = own.shape[0]
    total = 4 * depth * rows
    partner, across = me + 1 - 2 * core, me + 2 - 4 * y
    line = [lax.rem(z + d, depth) for d in range(1, depth)]

    barrier = pltpu.get_barrier_semaphore()
    others = [4 * other + 2 * y + core for other in line] + [partner, across]
    for other in others:
        pl.semaphore_signal(
            barrier, inc=1, device_id={"dp": other}, device_id_type=pl.DeviceIdType.MESH
        )

    def remote(ref, send_sem, recv_sem, target):
        return pltpu.make_async_remote_copy(
            src_ref=ref,
            dst_ref=ref,
            send_sem=send_sem,
            recv_sem=recv_sem,
            device_id={"dp": target},
            device_id_type=pl.DeviceIdType.MESH,
        )

    def along(c, d):
        return remote(land.at[c, y, core, z], z_send.at[c, d], z_recv.at[c, d], others[d])

    def over(c, d):
        slot = z if d == depth - 1 else lax.rem(z + depth - 1 - d, depth)
        return remote(land.at[c, y, core, slot], y_send.at[c, d], y_recv.at[c, d], across)

    def share(c, side):
        ref = land.at[c, (1 - y) if side else y, core]
        return remote(ref, core_send.at[c, side], core_recv.at[c, side], partner)

    def begin(c):
        for d in range(depth - 1):
            along(c, d).start()
        over(c, depth - 1).start()

    def first(c):
        for d in range(depth - 1):
            along(c, d).wait_recv()
            over(c, d).start()
        share(c, 0).start()

    def second(c):
        for d in range(depth):
            over(c, d).wait_recv()
        share(c, 1).start()

    def guarded(c, what):
        pl.when(c < chunks)(lambda: what(c))

    for c in range(chunks):
        land[c, y, core, z] = own[:, c * BLOCK : (c + 1) * BLOCK]
    for ref in (high, low, r_high, r_low):
        ref[...] = jnp.zeros(ref.shape, ref.dtype)
    pl.semaphore_wait(barrier, depth + 1)
    begin(0)
    begin(1)
    first(0)
    begin(2)
    first(1)
    second(0)

    def gathered(c):
        return land[c].reshape(total, BLOCK)

    def before(k):
        n = k * BLOCK
        top = [over_rows(gathered(m), gathered(k)) for m in range(k)]
        corner = over_rows(gathered(k), gathered(k))
        if k:
            c_high, c_low = split(jnp.concatenate(top, axis=0))
            r = product(high[:n, :n], c_high) + (
                product(high[:n, :n], c_low) + product(low[:n, :n], c_high)
            )
            one, two = split(r)
            r_high[:n, :] = one
            r_low[:n, :] = two
            corner -= over_rows(one, one) + (over_rows(one, two) + over_rows(two, one))
        a[...] = corner

    def between(s):
        size = t.shape[1] // 4
        at = slice(s * size, (s + 1) * size)
        t[:, at] = over_rows(r_high[...], high[:, at]) + (
            over_rows(r_high[...], low[:, at]) + over_rows(r_low[...], high[:, at])
        )

    def after(k):
        at = pl.ds(pl.multiple_of(k * BLOCK, BLOCK), BLOCK)
        w_high, w_low = split(w[...])
        t_high, t_low = split(t[...])
        left = product(w_high, t_high) + (product(w_high, t_low) + product(w_low, t_high))
        one, two = split(-left)
        high[at, :] = one
        low[at, :] = two
        high[at, at] = w_high
        low[at, at] = w_low
        both = sum(
            lax.dot_general(
                own[...],
                part,
                (((1,), (1,)), ((), ())),
                preferred_element_type=jnp.float32,
            )
            for part in (high[at, :], low[at, :])
        )
        out[:, at] = both * scale

    def step(k, carry):
        for side in range(2):
            share(k, side).wait_recv()
        guarded(k + 3, begin)
        for i in range(chunks):
            pl.when(k == i)(functools.partial(before, i))
        guarded(k + 2, first)
        inverse_factor(a, w, between)
        guarded(k + 1, second)
        after(k)
        return carry

    lax.fori_loop(0, chunks, step, 0)

    def finish(c, carry):
        for d in range(depth - 1):
            along(c, d).wait_send()
        for d in range(depth):
            over(c, d).wait_send()
        for side in range(2):
            share(c, side).wait_send()
        return carry

    lax.fori_loop(0, chunks, finish, 0)


def whiten_ring(pooled, collective_id):
    devices = lax.axis_size("dp")
    depth = devices // 4
    rows, width = pooled.shape
    chunks = width // BLOCK
    dma = pltpu.SemaphoreType.DMA
    whole = pl.BlockSpec(memory_space=pltpu.VMEM)
    return pl.pallas_call(
        functools.partial(whiten_ring_kernel, math.sqrt(rows * devices)),
        out_shape=jax.ShapeDtypeStruct((rows, width), jnp.float32),
        in_specs=[whole],
        out_specs=whole,
        scratch_shapes=[
            pltpu.VMEM((chunks, 2, 2, depth, rows, BLOCK), pooled.dtype),
            pltpu.VMEM((width, width), jnp.bfloat16),
            pltpu.VMEM((width, width), jnp.bfloat16),
            pltpu.VMEM((width, BLOCK), jnp.bfloat16),
            pltpu.VMEM((width, BLOCK), jnp.bfloat16),
            pltpu.VMEM((BLOCK, width), jnp.float32),
            pltpu.VMEM((BLOCK, BLOCK), jnp.float32),
            pltpu.VMEM((BLOCK, BLOCK), jnp.float32),
            dma((chunks, depth - 1)),
            dma((chunks, depth - 1)),
            dma((chunks, depth)),
            dma((chunks, depth)),
            dma((chunks, 2)),
            dma((chunks, 2)),
        ],
        compiler_params=pltpu.CompilerParams(
            collective_id=collective_id, has_side_effects=True, vmem_limit_bytes=40 << 20
        ),
    )(pooled)


def weights_kernel(
    chips, tokens_in, mask_in, spans_in, gain_in, shift_in, bias_in, up, down, pooled,
    tokens, mask, spans, gain, shift, bias, ups, downs, normed, select, sums, ring_send, ring_recv, x_send, x_recv,
    core_send, core_recv, own_sem, in_sem,
):
    me, group = lax.axis_index("dp"), lax.axis_index("groups")
    core, chip = lax.rem(me, 2), me // 2
    half = chips // 2
    odd = lax.rem(chip, 2)
    place = (1 - odd) * (chip // 2) + odd * (chips - 1 - chip // 2)
    turn = 1 - 2 * core
    partner = me + turn
    steps = (half, chips - 1 - half)

    def chip_at(q):
        q = lax.rem(q + 2 * chips, chips)
        back = q // half
        return (1 - back) * 2 * q + back * (2 * (chips - 1 - q) + 1)

    beside = [{"dp": 2 * chip_at(place + d) + core} for d in (turn, -turn)]
    mate, opposite = {"dp": partner}, {"groups": 1 - group}
    barrier = pltpu.get_barrier_semaphore()
    for other in (*beside, mate, opposite):
        pl.semaphore_signal(
            barrier, inc=1, device_id=other, device_id_type=pl.DeviceIdType.MESH
        )

    units = (up.shape[0] // 16, down.shape[1] // BLOCK)
    grain = (16, BLOCK)
    parts = []
    for a in range(2):
        side = units[a] * 5 // 16
        size, head = side * grain[a], (units[a] - 2 * side) * grain[a]
        mine = pl.multiple_of(head + group * size, grain[a])
        theirs = pl.multiple_of(head + (1 - group) * size, grain[a])
        parts.append(((mine, size), (0, head), (theirs, size)))

    def view(a, ref, part):
        if part is None:
            return ref
        start, size = parts[a][part]
        return ref.at[pl.ds(start, size)] if a == 0 else ref.at[:, pl.ds(start, size)]

    ins, full = (up, down), (ups, downs)

    def remote(a, source, slot, part, sems, target):
        return pltpu.make_async_remote_copy(
            src_ref=view(a, source, part),
            dst_ref=view(a, full[a].at[slot], part),
            send_sem=sems[0],
            recv_sem=sems[1],
            device_id=target,
            device_id_type=pl.DeviceIdType.MESH,
        )

    def came(way, hop):
        return 2 * chip_at(place - (1 + hop) * turn * (1 - 2 * way)) + core

    def ring(a, way, hop, part):
        slot = me if hop == 0 else came(way, hop - 1)
        source = ins[a] if hop == 0 else full[a].at[slot]
        at = (a, way, hop, part)
        return remote(a, source, slot, part, (ring_send.at[at], ring_recv.at[at]), beside[way])

    def swap(a, way, hop):
        slot = came(way, hop)
        at = (a, way * half + hop)
        return remote(a, full[a].at[slot], slot, 0, (x_send.at[at], x_recv.at[at]), opposite)

    def share(a, way, hop, part):
        slot = came(way, hop)
        at = (a, 1 + way * half + hop, part)
        return remote(
            a, full[a].at[slot], slot, part, (core_send.at[at], core_recv.at[at]), mate
        )

    def share_own(a):
        at = (a, 0, 0)
        return remote(a, ins[a], me, None, (core_send.at[at], core_recv.at[at]), mate)

    own = [pltpu.make_async_copy(ins[a], full[a].at[me], own_sem.at[a]) for a in range(2)]
    started = []

    def go(copy):
        copy.start()
        started.append(copy)

    def ways(hop):
        return [way for way in range(2) if 0 <= hop < steps[way]]

    def pass_on(a, hop, part):
        for way in ways(hop):
            ring(a, way, hop, part).wait_recv()
            if hop + 1 < steps[way]:
                go(ring(a, way, hop + 1, part))
            if part == 0:
                go(swap(a, way, hop))
            go(share(a, way, hop, part))

    def take(a, hop):
        for way in ways(hop):
            arrived = remote(
                a, full[a].at[came(way, hop)], came(way, hop), 2,
                (x_send.at[a, way * half + hop], x_recv.at[a, way * half + hop]), opposite,
            )
            arrived.wait_recv()
            go(share(a, way, hop, 2))

    def settle(a, hop):
        for way in ways(hop):
            for part in range(3):
                share(a, way, hop, part).wait_recv()

    def around(hop):
        return [chip_at(place - (1 + hop) * turn * (1 - 2 * way)) for way in ways(hop)]

    count, width = tokens.shape
    tile = 256
    over_last = (((1,), (1,)), ((), ()))

    def expand(q):
        size = up.shape[1]

        def one(s, carry):
            slot = 2 * q + s
            weights = ups.at[slot]

            total = 0.0
            for i in range(count // tile):
                before = bias[slot] + jnp.dot(
                    normed[i * tile : (i + 1) * tile, :],
                    weights[...],
                    preferred_element_type=jnp.float32,
                )
                hidden = 0.5 * before * (1.0 + lax.erf(before * math.sqrt(0.5)))
                total += jnp.dot(
                    select[i], hidden.astype(normed.dtype), preferred_element_type=jnp.float32
                )
            sums[:, pl.ds(pl.multiple_of(slot * size, BLOCK), size)] = total.astype(
                sums.dtype
            )
            return carry

        lax.fori_loop(0, 2, one, 0)

    def contract(q):
        weights = downs[pl.ds(2 * q, 2)].reshape(2 * down.shape[0], down.shape[1])
        at = pl.ds(pl.multiple_of(q * BLOCK, BLOCK), BLOCK)
        total = lax.dot_general(
            sums[...], weights, over_last, preferred_element_type=jnp.float32
        )
        labels = jnp.zeros((select.shape[1], 1), jnp.float32)
        for i in range(count // tile):
            rows = slice(i * tile, (i + 1) * tile)
            total += jnp.dot(select[i], tokens[rows, at], preferred_element_type=jnp.float32)
            labels += jnp.sum(select[i].astype(jnp.float32), axis=1, keepdims=True)
        pooled[:, at] = (total / jnp.maximum(labels, 1.0)).astype(pooled.dtype)

    arguments = [
        pltpu.make_async_copy(source, target, in_sem.at[i])
        for i, (source, target) in enumerate(
            (
                (tokens_in, tokens),
                (mask_in, mask),
                (spans_in, spans),
                (gain_in, gain),
                (shift_in, shift),
                (bias_in, bias),
            )
        )
    ]
    for copy in arguments:
        copy.start()
    pl.semaphore_wait(barrier, 4)
    for a in range(2):
        for part in range(2):
            for way in range(2):
                go(ring(a, way, 0, part))
        go(share_own(a))
    for copy in own:
        copy.start()
    for copy in arguments:
        copy.wait()

    for i in range(count // tile):
        rows = slice(i * tile, (i + 1) * tile)
        values = tokens[rows, :].astype(jnp.float32)
        center = jnp.mean(values, axis=1, keepdims=True)
        spread_of = jnp.mean((values - center) ** 2, axis=1, keepdims=True)
        normed[rows, :] = (
            (values - center) * lax.rsqrt(spread_of + 1e-05) * gain[...] + shift[...]
        ).astype(normed.dtype)
        labels = lax.broadcasted_iota(jnp.int32, (select.shape[1], tile), 0)
        select[i] = jnp.where(
            (spans[:, rows] == labels) & (mask[:, rows] == 1), 1.0, 0.0
        ).astype(select.dtype)

    for hop in range(half):
        for part in range(2):
            pass_on(0, hop, part)
        if hop == 0:
            for copy in own:
                copy.wait()
            share_own(0).wait_recv()
            expand(chip)
        take(1, hop - 1)
        for q in around(hop - 1)[1:]:
            expand(q)
        pass_on(1, hop, 0)
        if hop + 1 < half:
            pass_on(1, hop, 1)
        take(0, hop)
        settle(0, hop)
        expand(around(hop)[0])
    last = half - 1
    share_own(1).wait_recv()
    contract(chip)
    for hop in range(last):
        settle(1, hop)
        for q in around(hop):
            contract(q)
    pass_on(1, last, 1)
    take(1, last)
    settle(1, last)
    for q in around(last):
        contract(q)
    for copy in started:
        copy.wait_send()


def pooled_spans(tokens, token_mask, span_ids, norm_gain, norm_shift, up, b_up, down, collective_id):
    devices = lax.axis_size("dp")
    chips = devices // 2
    count, width = tokens.shape
    dma = pltpu.SemaphoreType.DMA
    whole = pl.BlockSpec(memory_space=pltpu.VMEM)
    apart = pl.BlockSpec(memory_space=pl.ANY)
    return pl.pallas_call(
        functools.partial(weights_kernel, chips),
        out_shape=jax.ShapeDtypeStruct((SEG_DEV, width), tokens.dtype),
        in_specs=[apart] * 8,
        out_specs=whole,
        scratch_shapes=[
            pltpu.VMEM(tokens.shape, tokens.dtype),
            pltpu.VMEM(token_mask.shape, token_mask.dtype),
            pltpu.VMEM(span_ids.shape, span_ids.dtype),
            pltpu.VMEM((1, width), norm_gain.dtype),
            pltpu.VMEM((1, width), norm_shift.dtype),
            pltpu.VMEM((devices, 1, up.shape[1]), b_up.dtype),
            pltpu.VMEM((devices,) + up.shape, up.dtype),
            pltpu.VMEM((devices,) + down.shape, down.dtype),
            pltpu.VMEM((count, width), tokens.dtype),
            pltpu.VMEM((count // 256, SEG_DEV, 256), tokens.dtype),
            pltpu.VMEM((SEG_DEV, b_up.shape[0]), tokens.dtype),
            dma((2, 2, chips // 2, 2)),
            dma((2, 2, chips // 2, 2)),
            dma((2, chips)),
            dma((2, chips)),
            dma((2, chips, 3)),
            dma((2, chips, 3)),
            dma((2,)),
            dma((6,)),
        ],
        compiler_params=pltpu.CompilerParams(
            collective_id=collective_id, has_side_effects=True, vmem_limit_bytes=60 << 20
        ),
    )(
        tokens,
        token_mask,
        span_ids,
        norm_gain.reshape(1, -1),
        norm_shift.reshape(1, -1),
        b_up.reshape(devices, 1, -1),
        up,
        down,
    )


def on_device(tokens, token_mask, span_ids, norm_gain, norm_shift, w_up, b_up, w_down):
    if lax.axis_size("dp") == 16 and lax.axis_size("groups") == 2:
        pooled = pooled_spans(
            tokens, token_mask, span_ids, norm_gain, norm_shift, w_up, b_up, w_down.T, 0
        )
        return whiten_ring(pooled, 1)
    values = tokens.astype(jnp.float32)
    center = jnp.mean(values, axis=1, keepdims=True)
    spread = jnp.mean((values - center) ** 2, axis=1, keepdims=True)
    normed = ((values - center) * lax.rsqrt(spread + 1e-05) * norm_gain + norm_shift).astype(
        jnp.bfloat16
    )
    width, hidden_size = tokens.shape[1], b_up.shape[0]
    over_last = (((1,), (1,)), ((), ()))
    if w_up.shape[1] % BLOCK == 0:
        hidden, down_full = ring_up(normed, b_up, w_up.T, w_down.T, 0)
    else:
        up_full, down_full = ring_gather((w_up.T, w_down.T), 0)
        up_full = up_full.reshape(hidden_size, width)
        before = (
            lax.dot_general(normed, up_full, over_last, preferred_element_type=jnp.float32) + b_up
        )
        hidden = jax.nn.gelu(before, approximate=False).astype(jnp.bfloat16)
    down_full = down_full.reshape(width, hidden_size)
    projected = lax.dot_general(
        hidden, down_full, over_last, preferred_element_type=jnp.float32
    )
    block_out = (values + projected).astype(jnp.bfloat16)
    labels = jnp.arange(SEG_DEV, dtype=jnp.int32)[:, None]
    select = (span_ids[0][None, :] == labels) & (token_mask[0][None, :] == 1)
    sums = jnp.dot(select.astype(jnp.bfloat16), block_out, preferred_element_type=jnp.float32)
    counts = jnp.sum(select.astype(jnp.float32), axis=1)
    pooled = (sums / jnp.maximum(counts, 1.0)[:, None]).astype(jnp.bfloat16)
    middle = width // 2
    left, right = (
        half.reshape(-1, middle)
        for half in ring_gather((pooled[:, :middle], pooled[:, middle:]), 1)
    )
    gram = [
        lax.dot_general(one, two, (((0,), (0,)), ((), ())), preferred_element_type=jnp.float32)
        for one, two in ((left, left), (left, right), (right, right))
    ]
    total_rows = SEG_DEV * lax.axis_size("dp")
    return whiten(gram, pooled.astype(jnp.float32).T, math.sqrt(total_rows)).T


def solution(mesh):
    in_specs = (
        P(("groups", "dp"), None),
        P(("groups", "dp"), None),
        P(("groups", "dp"), None),
        P(),
        P(),
        P(None, "dp"),
        P(),
        P(None, "dp"),
    )
    out_specs = P(("groups", "dp"), None)
    return jax.shard_map(
        on_device, mesh=mesh, in_specs=in_specs, out_specs=out_specs, check_vma=False
    )
```

```python
import functools
import math

import jax
import jax.numpy as jnp
from jax import lax
from jax.experimental import pallas as pl
from jax.experimental.pallas import tpu as pltpu
from jax.sharding import PartitionSpec as P

SEG_DEV = 192
BLOCK = 128
HIGHEST = lax.Precision.HIGHEST


def inverse_block(src, dst):
    lane = lax.broadcasted_iota(jnp.int32, (8, BLOCK), 1)
    sub = lax.broadcasted_iota(jnp.int32, (8, BLOCK), 0)
    groups = BLOCK // 8
    held = [src[8 * q : 8 * q + 8, :BLOCK] for q in range(groups)]

    def column(block, c):
        return jnp.broadcast_to(block[:, c : c + 1], (8, BLOCK))

    def row(block, r):
        return jnp.broadcast_to(block[r : r + 1, :], (8, BLOCK))

    for p in range(groups):
        at = 8 * p
        inside = (lane >= at) & (lane < at + 8)
        raw = held[p]
        cols = [column(raw, at + c) for c in range(8)]
        work = jnp.where(inside, jnp.where(lane - at == sub, 1.0, 0.0), raw)
        done = jnp.zeros((8, BLOCK), jnp.float32)
        for j in range(8):
            here = sub == j
            pivot = row(cols[j], j)
            inv = 1.0 / pivot
            done = jnp.where(here, work * lax.rsqrt(pivot), done)
            scaled = row(work, j) * inv
            work = jnp.where(here, scaled, work - cols[j] * scaled)
            for c in range(j + 1, 8):
                scaled = row(cols[c], j) * inv
                cols[c] = jnp.where(here, scaled, cols[c] - cols[j] * scaled)
        dst[at : at + 8, :] = jnp.where(lane <= at + sub, done, 0.0)
        rows = [row(work, c) for c in range(8)]
        for q in range(p + 1, groups):
            total = jnp.where(inside, 0.0, held[q])
            for c in range(8):
                total = total - column(held[q], at + c) * rows[c]
            held[q] = total


def whiten_kernel(scale, first_ref, cross_ref, last_ref, rows_ref, out_ref, a, panel, inv):
    half = first_ref.shape[0]
    n = 2 * half
    extra = rows_ref.shape[1]
    a[:half, :half] = first_ref[...]
    a[:half, half:n] = cross_ref[...]
    a[half:, :half] = jnp.zeros((half, half), jnp.float32)
    a[half:, half:n] = last_ref[...]
    a[:, n:] = jnp.zeros((n, a.shape[1] - n), jnp.float32)
    a[:, n : n + extra] = rows_ref[...]
    blocks = n // BLOCK

    def step(k, carry):
        lo = pl.multiple_of(k * BLOCK, BLOCK)
        panel[:, :BLOCK] = a[pl.ds(lo, BLOCK), pl.ds(lo, BLOCK)]
        inverse_block(panel, inv)
        panel[...] = jnp.dot(
            inv[...], a[pl.ds(lo, BLOCK), :], preferred_element_type=jnp.float32, precision=HIGHEST
        )
        out_ref[pl.ds(lo, BLOCK), :] = panel[:, n : n + extra] * scale

        for first in range(0, blocks, 2):
            start = first * BLOCK

            def trail(i, carry, start=start):
                hi = pl.multiple_of(i * BLOCK, BLOCK)
                left = panel[:, pl.ds(hi, BLOCK)].T
                a[pl.ds(hi, BLOCK), start:] -= jnp.dot(
                    left, panel[:, start:], preferred_element_type=jnp.float32, precision=HIGHEST
                )
                return carry

            lax.fori_loop(jnp.maximum(k + 1, first), min(first + 2, blocks), trail, 0)
        return carry

    lax.fori_loop(0, blocks, step, 0)


def whiten(gram, rows_t, scale):
    n, extra = rows_t.shape
    wide = n + (extra + BLOCK - 1) // BLOCK * BLOCK
    return pl.pallas_call(
        functools.partial(whiten_kernel, scale),
        out_shape=jax.ShapeDtypeStruct((n, extra), jnp.float32),
        in_specs=[pl.BlockSpec(memory_space=pltpu.VMEM)] * 4,
        out_specs=pl.BlockSpec(memory_space=pltpu.VMEM),
        scratch_shapes=[
            pltpu.VMEM((n, wide), jnp.float32),
            pltpu.VMEM((BLOCK, wide), jnp.float32),
            pltpu.VMEM((BLOCK, BLOCK), jnp.float32),
        ],
        compiler_params=pltpu.CompilerParams(vmem_limit_bytes=32 << 20),
    )(*gram, rows_t)


def ring_kernel(chips, count, fused, *refs):
    if fused:
        normed, bias, up, down, hidden, down_out, up_out = refs[:7]
        ins, outs, refs = (up, down), (up_out, down_out), refs[7:]
    else:
        ins, outs, refs = refs[:count], refs[count : 2 * count], refs[2 * count :]
    ring_send, ring_recv, core_send, core_recv, own_sem = refs
    me = lax.axis_index("dp")
    core, chip = lax.rem(me, 2), me // 2
    half = chips // 2
    odd = lax.rem(chip, 2)
    place = (1 - odd) * (chip // 2) + odd * (chips - 1 - chip // 2)
    turn = 1 - 2 * core
    partner = me + turn

    def device(q):
        q = lax.rem(q + 2 * chips, chips)
        back = q // half
        return 2 * ((1 - back) * 2 * q + back * (2 * (chips - 1 - q) + 1)) + core

    ahead, behind = device(place + turn), device(place - turn)
    barrier = pltpu.get_barrier_semaphore()
    for other in (ahead, behind, partner):
        pl.semaphore_signal(
            barrier, inc=1, device_id={"dp": other}, device_id_type=pl.DeviceIdType.MESH
        )
    pl.semaphore_wait(barrier, 3)

    steps = (half, chips - 1 - half)
    started, across = [], []

    def send(a, source, slot, way, step):
        copy = pltpu.make_async_remote_copy(
            src_ref=source,
            dst_ref=outs[a].at[slot],
            send_sem=ring_send.at[a, way, step],
            recv_sem=ring_recv.at[a, way, step],
            device_id={"dp": (ahead, behind)[way]},
            device_id_type=pl.DeviceIdType.MESH,
        )
        copy.start()
        started.append(copy)
        return copy

    def share(a, source, slot, index):
        copy = pltpu.make_async_remote_copy(
            src_ref=source,
            dst_ref=outs[a].at[slot],
            send_sem=core_send.at[a, index],
            recv_sem=core_recv.at[a, index],
            device_id={"dp": partner},
            device_id_type=pl.DeviceIdType.MESH,
        )
        copy.start()
        if fused and a == 0:
            first[index] = copy
        else:
            across.append(copy)

    def compute(slot, block):
        size = block.shape[0]
        columns = pl.ds(pl.multiple_of(slot * size, BLOCK), size)
        tile = normed.shape[0] // 3

        def part(t, carry):
            at = pl.ds(pl.multiple_of(t * tile, tile), tile)
            before = lax.dot_general(
                normed[at, :],
                block[...],
                (((1,), (1,)), ((), ())),
                preferred_element_type=jnp.float32,
            )
            before = before + bias[slot]
            hidden[at, columns] = (
                0.5 * before * (1.0 + lax.erf(before * math.sqrt(0.5)))
            ).astype(hidden.dtype)
            return carry

        lax.fori_loop(0, 3, part, 0)

    first = {}

    def partner_block(index, step, way):
        first[index].wait_recv()
        slot = partner
        if index:
            slot = device(place + (1 + step) * turn * (1 - 2 * way)) + turn
        compute(slot, outs[0].at[slot])

    flying, local = {}, []
    for a in range(count):
        for way in range(2):
            flying[a, way] = send(a, ins[a], me, way, 0)
        share(a, ins[a], me, 0)
        if not (fused and a == 0):
            local.append(pltpu.make_async_copy(ins[a], outs[a].at[me], own_sem.at[a]))
            local[-1].start()
    if fused:
        compute(me, ins[0])
    for step in range(half):
        landed = []
        if fused:
            if step == 0:
                partner_block(0, 0, 0)
            for way in range(2):
                if 0 < step <= steps[way]:
                    partner_block(way * half + step, step - 1, way)
        for a in range(count):
            for way in range(2):
                if step >= steps[way]:
                    continue
                flying[a, way].wait_recv()
                slot = device(place - (1 + step) * turn * (1 - 2 * way))
                block = outs[a].at[slot]
                if step + 1 < steps[way]:
                    flying[a, way] = send(a, block, slot, way, step + 1)
                share(a, block, slot, 1 + way * half + step)
                if fused and a == 0:
                    landed.append((slot, block))
        for slot, block in landed:
            compute(slot, block)
    if fused:
        for way in range(2):
            if steps[way] == half:
                partner_block(way * half + half, half - 1, way)
        for copy in first.values():
            copy.wait_send()
    for copy in local:
        copy.wait()
    for copy in started:
        copy.wait_send()
    for copy in across:
        copy.wait()


def ring_gather(blocks, collective_id):
    devices = lax.axis_size("dp")
    chips, count = devices // 2, len(blocks)
    dma = pltpu.SemaphoreType.DMA
    return pl.pallas_call(
        functools.partial(ring_kernel, chips, count, False),
        out_shape=[jax.ShapeDtypeStruct((devices,) + b.shape, b.dtype) for b in blocks],
        in_specs=[pl.BlockSpec(memory_space=pl.ANY)] * count,
        out_specs=[pl.BlockSpec(memory_space=pl.ANY)] * count,
        scratch_shapes=[
            dma((count, 2, chips // 2)),
            dma((count, 2, chips // 2)),
            dma((count, chips)),
            dma((count, chips)),
            dma((count,)),
        ],
        compiler_params=pltpu.CompilerParams(collective_id=collective_id, has_side_effects=True),
    )(*blocks)


def ring_up(normed, bias, up, down, collective_id):
    devices = lax.axis_size("dp")
    chips = devices // 2
    dma = pltpu.SemaphoreType.DMA
    whole = pl.BlockSpec(memory_space=pltpu.VMEM)
    apart = pl.BlockSpec(memory_space=pl.ANY)
    return pl.pallas_call(
        functools.partial(ring_kernel, chips, 2, True),
        out_shape=[
            jax.ShapeDtypeStruct((normed.shape[0], devices * up.shape[0]), normed.dtype),
            jax.ShapeDtypeStruct((devices,) + down.shape, down.dtype),
        ],
        in_specs=[whole, whole, whole, apart],
        out_specs=[whole, apart],
        scratch_shapes=[
            pltpu.VMEM((devices,) + up.shape, up.dtype),
            dma((2, 2, chips // 2)),
            dma((2, 2, chips // 2)),
            dma((2, chips)),
            dma((2, chips)),
            dma((2,)),
        ],
        compiler_params=pltpu.CompilerParams(
            collective_id=collective_id, has_side_effects=True, vmem_limit_bytes=40 << 20
        ),
    )(normed, bias.reshape(devices, 1, -1), up, down)


def spread(block, r):
    return jnp.broadcast_to(block[r : r + 1, :], (8, BLOCK))


def strip_factor(a, dst, base, groups):
    lane = lax.broadcasted_iota(jnp.int32, (8, BLOCK), 1)
    sub = lax.broadcasted_iota(jnp.int32, (8, BLOCK), 0)
    h = [a[base + 8 * q : base + 8 * q + 8, :] for q in range(groups)]

    def fetch(p):
        return {
            (c, q): jnp.broadcast_to(
                h[q][:, base + 8 * p + c : base + 8 * p + c + 1], (8, BLOCK)
            )
            for q in range(p, groups)
            for c in range(8)
        }

    cols = fetch(0)
    for p in range(groups):
        more = p + 1 < groups
        following = fetch(p + 1) if more else {}
        at = base + 8 * p
        inside = (lane >= at) & (lane < at + 8)
        work = jnp.where(inside, jnp.where(lane - at == sub, 1.0, 0.0), h[p])
        for q in range(p + 1, groups):
            h[q] = jnp.where(inside, 0.0, h[q])
        pivots = jnp.zeros((8, BLOCK), jnp.float32)
        for j in range(8):
            pivot = spread(cols[j, p], j)
            inv = 1.0 / pivot
            pivots = jnp.where(sub == j, pivot, pivots)
            for c in range(j + 1, 8):
                m = spread(cols[j, p], c) * inv
                for q in range(p, groups):
                    cols[c, q] = cols[c, q] - cols[j, q] * m
            if more:
                for c in range(8):
                    m = spread(cols[j, p + 1], c) * inv
                    for q in range(p + 1, groups):
                        following[c, q] = following[c, q] - cols[j, q] * m
            scaled = spread(work, j) * inv
            if j < 7:
                work = work - jnp.where(sub > j, cols[j, p], 0.0) * scaled
            for q in range(p + 1, groups):
                h[q] = h[q] - cols[j, q] * scaled
        dst[at : at + 8, :] = work * lax.rsqrt(pivots)
        cols = following


def over_rows(left, right, precision=None):
    return lax.dot_general(
        left,
        right,
        (((0,), (0,)), ((), ())),
        preferred_element_type=jnp.float32,
        precision=precision,
    )


def inverse_factor(a, dst, between):
    size = 32
    for base in range(0, BLOCK, size):
        strip_factor(a, dst, base, size // 8)
        between(base // size)
        lo = base + size
        if lo < BLOCK:
            rows = dst[base:lo, :]
            r = lax.broadcasted_iota(jnp.int32, (size, BLOCK), 0) + base
            c = lax.broadcasted_iota(jnp.int32, (size, BLOCK), 1)
            drop = over_rows(rows, jnp.where((c > r) & (c < lo), 0.0, rows), HIGHEST)
            c = lax.broadcasted_iota(jnp.int32, (BLOCK - lo, BLOCK), 1)
            a[lo:, :] = jnp.where((c >= base) & (c < lo), 0.0, a[lo:, :]) - drop[lo:, :]
    r = lax.broadcasted_iota(jnp.int32, (BLOCK, BLOCK), 0)
    c = lax.broadcasted_iota(jnp.int32, (BLOCK, BLOCK), 1)
    dst[...] = jnp.where(c <= r, dst[...], 0.0)


def product(left, right):
    return jnp.dot(left, right, preferred_element_type=jnp.float32)


def split(x):
    high = x.astype(jnp.bfloat16)
    return high, (x - high.astype(jnp.float32)).astype(jnp.bfloat16)


def whiten_ring_kernel(
    scale, own, out, land, high, low, r_high, r_low, t, a, w, z_send, z_recv, y_send, y_recv, core_send, core_recv
):
    me = lax.axis_index("dp")
    core, y, z = lax.rem(me, 2), lax.rem(me // 2, 2), me // 4
    depth = land.shape[3]
    chunks = own.shape[1] // BLOCK
    rows = own.shape[0]
    total = 4 * depth * rows
    partner, across = me + 1 - 2 * core, me + 2 - 4 * y
    line = [lax.rem(z + d, depth) for d in range(1, depth)]

    others = [4 * other + 2 * y + core for other in line] + [partner, across]

    def remote(ref, send_sem, recv_sem, target):
        return pltpu.make_async_remote_copy(
            src_ref=ref,
            dst_ref=ref,
            send_sem=send_sem,
            recv_sem=recv_sem,
            device_id={"dp": target},
            device_id_type=pl.DeviceIdType.MESH,
        )

    def along(c, d):
        return remote(land.at[c, y, core, z], z_send.at[c, d], z_recv.at[c, d], others[d])

    def over(c, d):
        slot = z if d == depth - 1 else lax.rem(z + depth - 1 - d, depth)
        return remote(land.at[c, y, core, slot], y_send.at[c, d], y_recv.at[c, d], across)

    def share(c, side):
        ref = land.at[c, (1 - y) if side else y, core]
        return remote(ref, core_send.at[c, side], core_recv.at[c, side], partner)

    def begin(c):
        for d in range(depth - 1):
            along(c, d).start()
        over(c, depth - 1).start()

    def first(c):
        for d in range(depth - 1):
            along(c, d).wait_recv()
            over(c, d).start()
        share(c, 0).start()

    def second(c):
        for d in range(depth):
            over(c, d).wait_recv()
        share(c, 1).start()

    def guarded(c, what):
        pl.when(c < chunks)(lambda: what(c))

    for c in range(chunks):
        land[c, y, core, z] = own[:, c * BLOCK : (c + 1) * BLOCK]
    for ref in (high, low, r_high, r_low):
        ref[...] = jnp.zeros(ref.shape, ref.dtype)
    begin(0)
    begin(1)
    first(0)
    begin(2)
    first(1)
    second(0)

    def gathered(c):
        return land[c].reshape(total, BLOCK)

    def before(k):
        n = k * BLOCK
        top = [over_rows(gathered(m), gathered(k)) for m in range(k)]
        corner = over_rows(gathered(k), gathered(k))
        if k:
            c_high, c_low = split(jnp.concatenate(top, axis=0))
            r = product(high[:n, :n], c_high) + (
                product(high[:n, :n], c_low) + product(low[:n, :n], c_high)
            )
            one, two = split(r)
            r_high[:n, :] = one
            r_low[:n, :] = two
            corner -= over_rows(one, one) + (over_rows(one, two) + over_rows(two, one))
        a[...] = corner

    def between(s):
        size = t.shape[1] // 4
        at = slice(s * size, (s + 1) * size)
        t[:, at] = over_rows(r_high[...], high[:, at]) + (
            over_rows(r_high[...], low[:, at]) + over_rows(r_low[...], high[:, at])
        )

    def after(k):
        at = pl.ds(pl.multiple_of(k * BLOCK, BLOCK), BLOCK)
        w_high, w_low = split(w[...])
        t_high, t_low = split(t[...])
        left = product(w_high, t_high) + (product(w_high, t_low) + product(w_low, t_high))
        one, two = split(-left)
        high[at, :] = one
        low[at, :] = two
        high[at, at] = w_high
        low[at, at] = w_low
        both = sum(
            lax.dot_general(
                own[...],
                part,
                (((1,), (1,)), ((), ())),
                preferred_element_type=jnp.float32,
            )
            for part in (high[at, :], low[at, :])
        )
        out[:, at] = both * scale

    def step(k, carry):
        for side in range(2):
            share(k, side).wait_recv()
        guarded(k + 3, begin)
        for i in range(chunks):
            pl.when(k == i)(functools.partial(before, i))
        guarded(k + 2, first)
        inverse_factor(a, w, between)
        guarded(k + 1, second)
        after(k)
        return carry

    lax.fori_loop(0, chunks, step, 0)

    def finish(c, carry):
        for d in range(depth - 1):
            along(c, d).wait_send()
        for d in range(depth):
            over(c, d).wait_send()
        for side in range(2):
            share(c, side).wait_send()
        return carry

    lax.fori_loop(0, chunks, finish, 0)


def weights_kernel(
    chips, tokens_in, mask_in, spans_in, gain_in, shift_in, bias_in, up, down, pooled,
    tokens, mask, spans, gain, shift, bias, ups, downs, normed, select, sums, ring_send, ring_recv, x_send, x_recv,
    core_send, core_recv, own_sem, in_sem,
):
    me, group = lax.axis_index("dp"), lax.axis_index("groups")
    core, chip = lax.rem(me, 2), me // 2
    half = chips // 2
    odd = lax.rem(chip, 2)
    place = (1 - odd) * (chip // 2) + odd * (chips - 1 - chip // 2)
    turn = 1 - 2 * core
    partner = me + turn
    steps = (half, chips - 1 - half)

    def chip_at(q):
        q = lax.rem(q + 2 * chips, chips)
        back = q // half
        return (1 - back) * 2 * q + back * (2 * (chips - 1 - q) + 1)

    beside = [{"dp": 2 * chip_at(place + d) + core} for d in (turn, -turn)]
    mate, opposite = {"dp": partner}, {"groups": 1 - group}
    barrier = pltpu.get_barrier_semaphore()
    depth = chips // 2
    line = [
        {"dp": lax.rem(me + 4 * d, 4 * depth)} for d in range(1, depth)
    ]
    over = {"dp": me + 2 - 4 * odd}
    for other in (*beside, mate, opposite, *line, over):
        pl.semaphore_signal(
            barrier, inc=1, device_id=other, device_id_type=pl.DeviceIdType.MESH
        )

    units = (up.shape[0] // 16, down.shape[1] // BLOCK)
    grain = (16, BLOCK)
    parts = []
    for a in range(2):
        side = units[a] * 5 // 16
        size, head = side * grain[a], (units[a] - 2 * side) * grain[a]
        mine = pl.multiple_of(head + group * size, grain[a])
        theirs = pl.multiple_of(head + (1 - group) * size, grain[a])
        parts.append(((mine, size), (0, head), (theirs, size)))

    def view(a, ref, part):
        if part is None:
            return ref
        start, size = parts[a][part]
        return ref.at[pl.ds(start, size)] if a == 0 else ref.at[:, pl.ds(start, size)]

    ins, full = (up, down), (ups, downs)

    def remote(a, source, slot, part, sems, target):
        return pltpu.make_async_remote_copy(
            src_ref=view(a, source, part),
            dst_ref=view(a, full[a].at[slot], part),
            send_sem=sems[0],
            recv_sem=sems[1],
            device_id=target,
            device_id_type=pl.DeviceIdType.MESH,
        )

    def came(way, hop):
        return 2 * chip_at(place - (1 + hop) * turn * (1 - 2 * way)) + core

    def ring(a, way, hop, part):
        slot = me if hop == 0 else came(way, hop - 1)
        source = ins[a] if hop == 0 else full[a].at[slot]
        at = (a, way, hop, part)
        return remote(a, source, slot, part, (ring_send.at[at], ring_recv.at[at]), beside[way])

    def swap(a, way, hop):
        slot = came(way, hop)
        at = (a, way * half + hop)
        return remote(a, full[a].at[slot], slot, 0, (x_send.at[at], x_recv.at[at]), opposite)

    def share(a, way, hop, part):
        slot = came(way, hop)
        at = (a, 1 + way * half + hop, part)
        return remote(
            a, full[a].at[slot], slot, part, (core_send.at[at], core_recv.at[at]), mate
        )

    def share_own(a):
        at = (a, 0, 0)
        return remote(a, ins[a], me, None, (core_send.at[at], core_recv.at[at]), mate)

    own = [pltpu.make_async_copy(ins[a], full[a].at[me], own_sem.at[a]) for a in range(2)]
    started = []

    def go(copy):
        copy.start()
        started.append(copy)

    def ways(hop):
        return [way for way in range(2) if 0 <= hop < steps[way]]

    def pass_on(a, hop, part):
        for way in ways(hop):
            ring(a, way, hop, part).wait_recv()
            if hop + 1 < steps[way]:
                go(ring(a, way, hop + 1, part))
            if part == 0:
                go(swap(a, way, hop))
            go(share(a, way, hop, part))

    def take(a, hop):
        for way in ways(hop):
            arrived = remote(
                a, full[a].at[came(way, hop)], came(way, hop), 2,
                (x_send.at[a, way * half + hop], x_recv.at[a, way * half + hop]), opposite,
            )
            arrived.wait_recv()
            go(share(a, way, hop, 2))

    def settle(a, hop):
        for way in ways(hop):
            for part in range(3):
                share(a, way, hop, part).wait_recv()

    def around(hop):
        return [chip_at(place - (1 + hop) * turn * (1 - 2 * way)) for way in ways(hop)]

    count, width = tokens.shape
    tile = 256
    over_last = (((1,), (1,)), ((), ()))

    def expand(q):
        size = up.shape[1]

        def one(s, carry):
            slot = 2 * q + s
            weights = ups.at[slot]

            total = 0.0
            for i in range(count // tile):
                before = bias[slot] + jnp.dot(
                    normed[i * tile : (i + 1) * tile, :],
                    weights[...],
                    preferred_element_type=jnp.float32,
                )
                hidden = 0.5 * before * (1.0 + lax.erf(before * math.sqrt(0.5)))
                total += jnp.dot(
                    select[i], hidden.astype(normed.dtype), preferred_element_type=jnp.float32
                )
            sums[:, pl.ds(pl.multiple_of(slot * size, BLOCK), size)] = total.astype(
                sums.dtype
            )
            return carry

        lax.fori_loop(0, 2, one, 0)

    def contract(q):
        weights = downs[pl.ds(2 * q, 2)].reshape(2 * down.shape[0], down.shape[1])
        at = pl.ds(pl.multiple_of(q * BLOCK, BLOCK), BLOCK)
        total = lax.dot_general(
            sums[...], weights, over_last, preferred_element_type=jnp.float32
        )
        labels = jnp.zeros((select.shape[1], 1), jnp.float32)
        for i in range(count // tile):
            rows = slice(i * tile, (i + 1) * tile)
            total += jnp.dot(select[i], tokens[rows, at], preferred_element_type=jnp.float32)
            labels += jnp.sum(select[i].astype(jnp.float32), axis=1, keepdims=True)
        pooled[:, at] = (total / jnp.maximum(labels, 1.0)).astype(pooled.dtype)

    arguments = [
        pltpu.make_async_copy(source, target, in_sem.at[i])
        for i, (source, target) in enumerate(
            (
                (tokens_in, tokens),
                (mask_in, mask),
                (spans_in, spans),
                (gain_in, gain),
                (shift_in, shift),
                (bias_in, bias),
            )
        )
    ]
    for copy in arguments:
        copy.start()
    pl.semaphore_wait(barrier, 4 + depth)
    for a in range(2):
        for part in range(2):
            for way in range(2):
                go(ring(a, way, 0, part))
        go(share_own(a))
    for copy in own:
        copy.start()
    for copy in arguments:
        copy.wait()

    for i in range(count // tile):
        rows = slice(i * tile, (i + 1) * tile)
        values = tokens[rows, :].astype(jnp.float32)
        center = jnp.mean(values, axis=1, keepdims=True)
        spread_of = jnp.mean((values - center) ** 2, axis=1, keepdims=True)
        normed[rows, :] = (
            (values - center) * lax.rsqrt(spread_of + 1e-05) * gain[...] + shift[...]
        ).astype(normed.dtype)
        labels = lax.broadcasted_iota(jnp.int32, (select.shape[1], tile), 0)
        select[i] = jnp.where(
            (spans[:, rows] == labels) & (mask[:, rows] == 1), 1.0, 0.0
        ).astype(select.dtype)

    for hop in range(half):
        for part in range(2):
            pass_on(0, hop, part)
        if hop == 0:
            for copy in own:
                copy.wait()
            share_own(0).wait_recv()
            expand(chip)
        take(1, hop - 1)
        for q in around(hop - 1)[1:]:
            expand(q)
        pass_on(1, hop, 0)
        if hop + 1 < half:
            pass_on(1, hop, 1)
        take(0, hop)
        settle(0, hop)
        expand(around(hop)[0])
    last = half - 1
    share_own(1).wait_recv()
    contract(chip)
    for hop in range(last):
        settle(1, hop)
        for q in around(hop):
            contract(q)
    pass_on(1, last, 1)
    take(1, last)
    settle(1, last)
    for q in around(last):
        contract(q)
    for copy in started:
        copy.wait_send()


def whole_kernel(chips, scale, *refs):
    ins, out, pooled, first, second = refs[:8], refs[8], refs[9], refs[10:29], refs[29:]
    weights_kernel(chips, *ins, pooled, *first)
    whiten_ring_kernel(scale, pooled, out, *second)


def whitened_spans(tokens, token_mask, span_ids, norm_gain, norm_shift, up, b_up, down):
    devices = lax.axis_size("dp")
    chips, depth = devices // 2, devices // 4
    count, width = tokens.shape
    chunks = width // BLOCK
    kind = tokens.dtype
    dma = pltpu.SemaphoreType.DMA
    vmem = pltpu.VMEM
    first = [
        vmem(tokens.shape, kind),
        vmem(token_mask.shape, token_mask.dtype),
        vmem(span_ids.shape, span_ids.dtype),
        vmem((1, width), norm_gain.dtype),
        vmem((1, width), norm_shift.dtype),
        vmem((devices, 1, up.shape[1]), b_up.dtype),
        vmem((devices,) + up.shape, up.dtype),
        vmem((devices,) + down.shape, down.dtype),
        vmem((count, width), kind),
        vmem((count // 256, SEG_DEV, 256), kind),
        vmem((SEG_DEV, b_up.shape[0]), kind),
        dma((2, 2, chips // 2, 2)),
        dma((2, 2, chips // 2, 2)),
        dma((2, chips)),
        dma((2, chips)),
        dma((2, chips, 3)),
        dma((2, chips, 3)),
        dma((2,)),
        dma((6,)),
    ]
    second = [
        vmem((chunks, 2, 2, depth, SEG_DEV, BLOCK), kind),
        vmem((width, width), jnp.bfloat16),
        vmem((width, width), jnp.bfloat16),
        vmem((width, BLOCK), jnp.bfloat16),
        vmem((width, BLOCK), jnp.bfloat16),
        vmem((BLOCK, width), jnp.float32),
        vmem((BLOCK, BLOCK), jnp.float32),
        vmem((BLOCK, BLOCK), jnp.float32),
        dma((chunks, depth - 1)),
        dma((chunks, depth - 1)),
        dma((chunks, depth)),
        dma((chunks, depth)),
        dma((chunks, 2)),
        dma((chunks, 2)),
    ]
    return pl.pallas_call(
        functools.partial(whole_kernel, chips, math.sqrt(SEG_DEV * devices)),
        out_shape=jax.ShapeDtypeStruct((SEG_DEV, width), jnp.float32),
        in_specs=[pl.BlockSpec(memory_space=pl.ANY)] * 8,
        out_specs=pl.BlockSpec(memory_space=pltpu.VMEM),
        scratch_shapes=[vmem((SEG_DEV, width), kind)] + first + second,
        compiler_params=pltpu.CompilerParams(
            collective_id=0, has_side_effects=True, vmem_limit_bytes=60 << 20
        ),
    )(
        tokens,
        token_mask,
        span_ids,
        norm_gain.reshape(1, -1),
        norm_shift.reshape(1, -1),
        b_up.reshape(devices, 1, -1),
        up,
        down,
    )


def on_device(tokens, token_mask, span_ids, norm_gain, norm_shift, w_up, b_up, w_down):
    if lax.axis_size("dp") == 16 and lax.axis_size("groups") == 2:
        return whitened_spans(
            tokens, token_mask, span_ids, norm_gain, norm_shift, w_up, b_up, w_down.T
        )
    values = tokens.astype(jnp.float32)
    center = jnp.mean(values, axis=1, keepdims=True)
    spread = jnp.mean((values - center) ** 2, axis=1, keepdims=True)
    normed = ((values - center) * lax.rsqrt(spread + 1e-05) * norm_gain + norm_shift).astype(
        jnp.bfloat16
    )
    width, hidden_size = tokens.shape[1], b_up.shape[0]
    over_last = (((1,), (1,)), ((), ()))
    if w_up.shape[1] % BLOCK == 0:
        hidden, down_full = ring_up(normed, b_up, w_up.T, w_down.T, 0)
    else:
        up_full, down_full = ring_gather((w_up.T, w_down.T), 0)
        up_full = up_full.reshape(hidden_size, width)
        before = (
            lax.dot_general(normed, up_full, over_last, preferred_element_type=jnp.float32) + b_up
        )
        hidden = jax.nn.gelu(before, approximate=False).astype(jnp.bfloat16)
    down_full = down_full.reshape(width, hidden_size)
    projected = lax.dot_general(
        hidden, down_full, over_last, preferred_element_type=jnp.float32
    )
    block_out = (values + projected).astype(jnp.bfloat16)
    labels = jnp.arange(SEG_DEV, dtype=jnp.int32)[:, None]
    select = (span_ids[0][None, :] == labels) & (token_mask[0][None, :] == 1)
    sums = jnp.dot(select.astype(jnp.bfloat16), block_out, preferred_element_type=jnp.float32)
    counts = jnp.sum(select.astype(jnp.float32), axis=1)
    pooled = (sums / jnp.maximum(counts, 1.0)[:, None]).astype(jnp.bfloat16)
    middle = width // 2
    left, right = (
        half.reshape(-1, middle)
        for half in ring_gather((pooled[:, :middle], pooled[:, middle:]), 1)
    )
    gram = [
        lax.dot_general(one, two, (((0,), (0,)), ((), ())), preferred_element_type=jnp.float32)
        for one, two in ((left, left), (left, right), (right, right))
    ]
    total_rows = SEG_DEV * lax.axis_size("dp")
    return whiten(gram, pooled.astype(jnp.float32).T, math.sqrt(total_rows)).T


def solution(mesh):
    in_specs = (
        P(("groups", "dp"), None),
        P(("groups", "dp"), None),
        P(("groups", "dp"), None),
        P(),
        P(),
        P(None, "dp"),
        P(),
        P(None, "dp"),
    )
    out_specs = P(("groups", "dp"), None)
    return jax.shard_map(
        on_device, mesh=mesh, in_specs=in_specs, out_specs=out_specs, check_vma=False
    )
```

```python
import functools
import math

import jax
import jax.numpy as jnp
from jax import lax
from jax.experimental import pallas as pl
from jax.experimental.pallas import tpu as pltpu
from jax.sharding import PartitionSpec as P

SEG_DEV = 192
BLOCK = 128
HIGHEST = lax.Precision.HIGHEST


def inverse_block(src, dst):
    lane = lax.broadcasted_iota(jnp.int32, (8, BLOCK), 1)
    sub = lax.broadcasted_iota(jnp.int32, (8, BLOCK), 0)
    groups = BLOCK // 8
    held = [src[8 * q : 8 * q + 8, :BLOCK] for q in range(groups)]

    def column(block, c):
        return jnp.broadcast_to(block[:, c : c + 1], (8, BLOCK))

    def row(block, r):
        return jnp.broadcast_to(block[r : r + 1, :], (8, BLOCK))

    for p in range(groups):
        at = 8 * p
        inside = (lane >= at) & (lane < at + 8)
        raw = held[p]
        cols = [column(raw, at + c) for c in range(8)]
        work = jnp.where(inside, jnp.where(lane - at == sub, 1.0, 0.0), raw)
        done = jnp.zeros((8, BLOCK), jnp.float32)
        for j in range(8):
            here = sub == j
            pivot = row(cols[j], j)
            inv = 1.0 / pivot
            done = jnp.where(here, work * lax.rsqrt(pivot), done)
            scaled = row(work, j) * inv
            work = jnp.where(here, scaled, work - cols[j] * scaled)
            for c in range(j + 1, 8):
                scaled = row(cols[c], j) * inv
                cols[c] = jnp.where(here, scaled, cols[c] - cols[j] * scaled)
        dst[at : at + 8, :] = jnp.where(lane <= at + sub, done, 0.0)
        rows = [row(work, c) for c in range(8)]
        for q in range(p + 1, groups):
            total = jnp.where(inside, 0.0, held[q])
            for c in range(8):
                total = total - column(held[q], at + c) * rows[c]
            held[q] = total


def whiten_kernel(scale, first_ref, cross_ref, last_ref, rows_ref, out_ref, a, panel, inv):
    half = first_ref.shape[0]
    n = 2 * half
    extra = rows_ref.shape[1]
    a[:half, :half] = first_ref[...]
    a[:half, half:n] = cross_ref[...]
    a[half:, :half] = jnp.zeros((half, half), jnp.float32)
    a[half:, half:n] = last_ref[...]
    a[:, n:] = jnp.zeros((n, a.shape[1] - n), jnp.float32)
    a[:, n : n + extra] = rows_ref[...]
    blocks = n // BLOCK

    def step(k, carry):
        lo = pl.multiple_of(k * BLOCK, BLOCK)
        panel[:, :BLOCK] = a[pl.ds(lo, BLOCK), pl.ds(lo, BLOCK)]
        inverse_block(panel, inv)
        panel[...] = jnp.dot(
            inv[...], a[pl.ds(lo, BLOCK), :], preferred_element_type=jnp.float32, precision=HIGHEST
        )
        out_ref[pl.ds(lo, BLOCK), :] = panel[:, n : n + extra] * scale

        for first in range(0, blocks, 2):
            start = first * BLOCK

            def trail(i, carry, start=start):
                hi = pl.multiple_of(i * BLOCK, BLOCK)
                left = panel[:, pl.ds(hi, BLOCK)].T
                a[pl.ds(hi, BLOCK), start:] -= jnp.dot(
                    left, panel[:, start:], preferred_element_type=jnp.float32, precision=HIGHEST
                )
                return carry

            lax.fori_loop(jnp.maximum(k + 1, first), min(first + 2, blocks), trail, 0)
        return carry

    lax.fori_loop(0, blocks, step, 0)


def whiten(gram, rows_t, scale):
    n, extra = rows_t.shape
    wide = n + (extra + BLOCK - 1) // BLOCK * BLOCK
    return pl.pallas_call(
        functools.partial(whiten_kernel, scale),
        out_shape=jax.ShapeDtypeStruct((n, extra), jnp.float32),
        in_specs=[pl.BlockSpec(memory_space=pltpu.VMEM)] * 4,
        out_specs=pl.BlockSpec(memory_space=pltpu.VMEM),
        scratch_shapes=[
            pltpu.VMEM((n, wide), jnp.float32),
            pltpu.VMEM((BLOCK, wide), jnp.float32),
            pltpu.VMEM((BLOCK, BLOCK), jnp.float32),
        ],
        compiler_params=pltpu.CompilerParams(vmem_limit_bytes=32 << 20),
    )(*gram, rows_t)


def ring_kernel(chips, count, fused, *refs):
    if fused:
        normed, bias, up, down, hidden, down_out, up_out = refs[:7]
        ins, outs, refs = (up, down), (up_out, down_out), refs[7:]
    else:
        ins, outs, refs = refs[:count], refs[count : 2 * count], refs[2 * count :]
    ring_send, ring_recv, core_send, core_recv, own_sem = refs
    me = lax.axis_index("dp")
    core, chip = lax.rem(me, 2), me // 2
    half = chips // 2
    odd = lax.rem(chip, 2)
    place = (1 - odd) * (chip // 2) + odd * (chips - 1 - chip // 2)
    turn = 1 - 2 * core
    partner = me + turn

    def device(q):
        q = lax.rem(q + 2 * chips, chips)
        back = q // half
        return 2 * ((1 - back) * 2 * q + back * (2 * (chips - 1 - q) + 1)) + core

    ahead, behind = device(place + turn), device(place - turn)
    barrier = pltpu.get_barrier_semaphore()
    for other in (ahead, behind, partner):
        pl.semaphore_signal(
            barrier, inc=1, device_id={"dp": other}, device_id_type=pl.DeviceIdType.MESH
        )
    pl.semaphore_wait(barrier, 3)

    steps = (half, chips - 1 - half)
    started, across = [], []

    def send(a, source, slot, way, step):
        copy = pltpu.make_async_remote_copy(
            src_ref=source,
            dst_ref=outs[a].at[slot],
            send_sem=ring_send.at[a, way, step],
            recv_sem=ring_recv.at[a, way, step],
            device_id={"dp": (ahead, behind)[way]},
            device_id_type=pl.DeviceIdType.MESH,
        )
        copy.start()
        started.append(copy)
        return copy

    def share(a, source, slot, index):
        copy = pltpu.make_async_remote_copy(
            src_ref=source,
            dst_ref=outs[a].at[slot],
            send_sem=core_send.at[a, index],
            recv_sem=core_recv.at[a, index],
            device_id={"dp": partner},
            device_id_type=pl.DeviceIdType.MESH,
        )
        copy.start()
        if fused and a == 0:
            first[index] = copy
        else:
            across.append(copy)

    def compute(slot, block):
        size = block.shape[0]
        columns = pl.ds(pl.multiple_of(slot * size, BLOCK), size)
        tile = normed.shape[0] // 3

        def part(t, carry):
            at = pl.ds(pl.multiple_of(t * tile, tile), tile)
            before = lax.dot_general(
                normed[at, :],
                block[...],
                (((1,), (1,)), ((), ())),
                preferred_element_type=jnp.float32,
            )
            before = before + bias[slot]
            hidden[at, columns] = (
                0.5 * before * (1.0 + lax.erf(before * math.sqrt(0.5)))
            ).astype(hidden.dtype)
            return carry

        lax.fori_loop(0, 3, part, 0)

    first = {}

    def partner_block(index, step, way):
        first[index].wait_recv()
        slot = partner
        if index:
            slot = device(place + (1 + step) * turn * (1 - 2 * way)) + turn
        compute(slot, outs[0].at[slot])

    flying, local = {}, []
    for a in range(count):
        for way in range(2):
            flying[a, way] = send(a, ins[a], me, way, 0)
        share(a, ins[a], me, 0)
        if not (fused and a == 0):
            local.append(pltpu.make_async_copy(ins[a], outs[a].at[me], own_sem.at[a]))
            local[-1].start()
    if fused:
        compute(me, ins[0])
    for step in range(half):
        landed = []
        if fused:
            if step == 0:
                partner_block(0, 0, 0)
            for way in range(2):
                if 0 < step <= steps[way]:
                    partner_block(way * half + step, step - 1, way)
        for a in range(count):
            for way in range(2):
                if step >= steps[way]:
                    continue
                flying[a, way].wait_recv()
                slot = device(place - (1 + step) * turn * (1 - 2 * way))
                block = outs[a].at[slot]
                if step + 1 < steps[way]:
                    flying[a, way] = send(a, block, slot, way, step + 1)
                share(a, block, slot, 1 + way * half + step)
                if fused and a == 0:
                    landed.append((slot, block))
        for slot, block in landed:
            compute(slot, block)
    if fused:
        for way in range(2):
            if steps[way] == half:
                partner_block(way * half + half, half - 1, way)
        for copy in first.values():
            copy.wait_send()
    for copy in local:
        copy.wait()
    for copy in started:
        copy.wait_send()
    for copy in across:
        copy.wait()


def ring_gather(blocks, collective_id):
    devices = lax.axis_size("dp")
    chips, count = devices // 2, len(blocks)
    dma = pltpu.SemaphoreType.DMA
    return pl.pallas_call(
        functools.partial(ring_kernel, chips, count, False),
        out_shape=[jax.ShapeDtypeStruct((devices,) + b.shape, b.dtype) for b in blocks],
        in_specs=[pl.BlockSpec(memory_space=pl.ANY)] * count,
        out_specs=[pl.BlockSpec(memory_space=pl.ANY)] * count,
        scratch_shapes=[
            dma((count, 2, chips // 2)),
            dma((count, 2, chips // 2)),
            dma((count, chips)),
            dma((count, chips)),
            dma((count,)),
        ],
        compiler_params=pltpu.CompilerParams(collective_id=collective_id, has_side_effects=True),
    )(*blocks)


def ring_up(normed, bias, up, down, collective_id):
    devices = lax.axis_size("dp")
    chips = devices // 2
    dma = pltpu.SemaphoreType.DMA
    whole = pl.BlockSpec(memory_space=pltpu.VMEM)
    apart = pl.BlockSpec(memory_space=pl.ANY)
    return pl.pallas_call(
        functools.partial(ring_kernel, chips, 2, True),
        out_shape=[
            jax.ShapeDtypeStruct((normed.shape[0], devices * up.shape[0]), normed.dtype),
            jax.ShapeDtypeStruct((devices,) + down.shape, down.dtype),
        ],
        in_specs=[whole, whole, whole, apart],
        out_specs=[whole, apart],
        scratch_shapes=[
            pltpu.VMEM((devices,) + up.shape, up.dtype),
            dma((2, 2, chips // 2)),
            dma((2, 2, chips // 2)),
            dma((2, chips)),
            dma((2, chips)),
            dma((2,)),
        ],
        compiler_params=pltpu.CompilerParams(
            collective_id=collective_id, has_side_effects=True, vmem_limit_bytes=40 << 20
        ),
    )(normed, bias.reshape(devices, 1, -1), up, down)


def spread(block, r):
    return jnp.broadcast_to(block[r : r + 1, :], (8, BLOCK))


def strip_factor(a, dst, base, groups):
    lane = lax.broadcasted_iota(jnp.int32, (8, BLOCK), 1)
    sub = lax.broadcasted_iota(jnp.int32, (8, BLOCK), 0)
    h = [a[base + 8 * q : base + 8 * q + 8, :] for q in range(groups)]

    def fetch(p):
        return {
            (c, q): jnp.broadcast_to(
                h[q][:, base + 8 * p + c : base + 8 * p + c + 1], (8, BLOCK)
            )
            for q in range(p, groups)
            for c in range(8)
        }

    cols = fetch(0)
    for p in range(groups):
        more = p + 1 < groups
        following = fetch(p + 1) if more else {}
        at = base + 8 * p
        inside = (lane >= at) & (lane < at + 8)
        work = jnp.where(inside, jnp.where(lane - at == sub, 1.0, 0.0), h[p])
        for q in range(p + 1, groups):
            h[q] = jnp.where(inside, 0.0, h[q])
        pivots = jnp.zeros((8, BLOCK), jnp.float32)
        for j in range(8):
            pivot = spread(cols[j, p], j)
            inv = 1.0 / pivot
            pivots = jnp.where(sub == j, pivot, pivots)
            for c in range(j + 1, 8):
                m = spread(cols[j, p], c) * inv
                for q in range(p, groups):
                    cols[c, q] = cols[c, q] - cols[j, q] * m
            if more:
                for c in range(8):
                    m = spread(cols[j, p + 1], c) * inv
                    for q in range(p + 1, groups):
                        following[c, q] = following[c, q] - cols[j, q] * m
            scaled = spread(work, j) * inv
            if j < 7:
                work = work - jnp.where(sub > j, cols[j, p], 0.0) * scaled
            for q in range(p + 1, groups):
                h[q] = h[q] - cols[j, q] * scaled
        dst[at : at + 8, :] = work * lax.rsqrt(pivots)
        cols = following


def over_rows(left, right, precision=None):
    return lax.dot_general(
        left,
        right,
        (((0,), (0,)), ((), ())),
        preferred_element_type=jnp.float32,
        precision=precision,
    )


def inverse_factor(a, dst, between):
    size = 32
    for base in range(0, BLOCK, size):
        strip_factor(a, dst, base, size // 8)
        between(base // size)
        lo = base + size
        if lo < BLOCK:
            rows = dst[base:lo, :]
            r = lax.broadcasted_iota(jnp.int32, (size, BLOCK), 0) + base
            c = lax.broadcasted_iota(jnp.int32, (size, BLOCK), 1)
            drop = over_rows(rows, jnp.where((c > r) & (c < lo), 0.0, rows), HIGHEST)
            c = lax.broadcasted_iota(jnp.int32, (BLOCK - lo, BLOCK), 1)
            a[lo:, :] = jnp.where((c >= base) & (c < lo), 0.0, a[lo:, :]) - drop[lo:, :]
    r = lax.broadcasted_iota(jnp.int32, (BLOCK, BLOCK), 0)
    c = lax.broadcasted_iota(jnp.int32, (BLOCK, BLOCK), 1)
    dst[...] = jnp.where(c <= r, dst[...], 0.0)


def product(left, right):
    return jnp.dot(left, right, preferred_element_type=jnp.float32)


def split(x):
    high = x.astype(jnp.bfloat16)
    return high, (x - high.astype(jnp.float32)).astype(jnp.bfloat16)


def whiten_ring_kernel(
    scale, own, out, land, high, low, r_high, r_low, t, a, w, z_send, z_recv, y_send, y_recv, core_send, core_recv
):
    me = lax.axis_index("dp")
    core, y, z = lax.rem(me, 2), lax.rem(me // 2, 2), me // 4
    depth = land.shape[3]
    chunks = own.shape[1] // BLOCK
    rows = own.shape[0]
    total = 4 * depth * rows
    partner, across = me + 1 - 2 * core, me + 2 - 4 * y
    line = [lax.rem(z + d, depth) for d in range(1, depth)]

    others = [4 * other + 2 * y + core for other in line] + [partner, across]

    def remote(ref, send_sem, recv_sem, target):
        return pltpu.make_async_remote_copy(
            src_ref=ref,
            dst_ref=ref,
            send_sem=send_sem,
            recv_sem=recv_sem,
            device_id={"dp": target},
            device_id_type=pl.DeviceIdType.MESH,
        )

    def along(c, d):
        return remote(land.at[c, y, core, z], z_send.at[c, d], z_recv.at[c, d], others[d])

    def over(c, d):
        slot = z if d == depth - 1 else lax.rem(z + depth - 1 - d, depth)
        return remote(land.at[c, y, core, slot], y_send.at[c, d], y_recv.at[c, d], across)

    def share(c, side):
        ref = land.at[c, (1 - y) if side else y, core]
        return remote(ref, core_send.at[c, side], core_recv.at[c, side], partner)

    def begin(c):
        for d in range(depth - 1):
            along(c, d).start()
        over(c, depth - 1).start()

    def first(c):
        for d in range(depth - 1):
            along(c, d).wait_recv()
            over(c, d).start()
        share(c, 0).start()

    def second(c):
        for d in range(depth):
            over(c, d).wait_recv()
        share(c, 1).start()

    def guarded(c, what):
        pl.when(c < chunks)(lambda: what(c))

    for c in range(chunks):
        land[c, y, core, z] = own[:, c * BLOCK : (c + 1) * BLOCK]
    begin(0)
    begin(1)
    for ref in (high, low, r_high, r_low):
        ref[...] = jnp.zeros(ref.shape, ref.dtype)
    first(0)
    begin(2)
    first(1)
    second(0)

    def gathered(c):
        return land[c].reshape(total, BLOCK)

    def before(k):
        n = k * BLOCK
        top = [over_rows(gathered(m), gathered(k)) for m in range(k)]
        corner = over_rows(gathered(k), gathered(k))
        if k:
            c_high, c_low = split(jnp.concatenate(top, axis=0))
            r = product(high[:n, :n], c_high) + (
                product(high[:n, :n], c_low) + product(low[:n, :n], c_high)
            )
            one, two = split(r)
            r_high[:n, :] = one
            r_low[:n, :] = two
            corner -= over_rows(one, one) + (over_rows(one, two) + over_rows(two, one))
        a[...] = corner

    def between(s):
        size = t.shape[1] // 4
        at = slice(s * size, (s + 1) * size)
        t[:, at] = over_rows(r_high[...], high[:, at]) + (
            over_rows(r_high[...], low[:, at]) + over_rows(r_low[...], high[:, at])
        )

    def after(k):
        at = pl.ds(pl.multiple_of(k * BLOCK, BLOCK), BLOCK)
        w_high, w_low = split(w[...])
        t_high, t_low = split(t[...])
        left = product(w_high, t_high) + (product(w_high, t_low) + product(w_low, t_high))
        one, two = split(-left)
        high[at, :] = one
        low[at, :] = two
        high[at, at] = w_high
        low[at, at] = w_low
        both = sum(
            lax.dot_general(
                own[...],
                part,
                (((1,), (1,)), ((), ())),
                preferred_element_type=jnp.float32,
            )
            for part in (high[at, :], low[at, :])
        )
        out[:, at] = both * scale

    def step(k, carry):
        for side in range(2):
            share(k, side).wait_recv()
        guarded(k + 3, begin)
        for i in range(chunks):
            pl.when(k == i)(functools.partial(before, i))
        guarded(k + 2, first)
        inverse_factor(a, w, between)
        guarded(k + 1, second)
        after(k)
        return carry

    lax.fori_loop(0, chunks, step, 0)

    def finish(c, carry):
        for d in range(depth - 1):
            along(c, d).wait_send()
        for d in range(depth):
            over(c, d).wait_send()
        for side in range(2):
            share(c, side).wait_send()
        return carry

    lax.fori_loop(0, chunks, finish, 0)


def weights_kernel(
    chips, tokens_in, mask_in, spans_in, gain_in, shift_in, bias_in, up, down, pooled,
    tokens, mask, spans, gain, shift, bias, ups, downs, normed, select, sums, ring_send, ring_recv, x_send, x_recv,
    core_send, core_recv, own_sem, in_sem,
):
    me, group = lax.axis_index("dp"), lax.axis_index("groups")
    core, chip = lax.rem(me, 2), me // 2
    half = chips // 2
    odd = lax.rem(chip, 2)
    place = (1 - odd) * (chip // 2) + odd * (chips - 1 - chip // 2)
    turn = 1 - 2 * core
    partner = me + turn
    steps = (half, chips - 1 - half)

    def chip_at(q):
        q = lax.rem(q + 2 * chips, chips)
        back = q // half
        return (1 - back) * 2 * q + back * (2 * (chips - 1 - q) + 1)

    beside = [{"dp": 2 * chip_at(place + d) + core} for d in (turn, -turn)]
    mate, opposite = {"dp": partner}, {"groups": 1 - group}
    barrier = pltpu.get_barrier_semaphore()
    depth = chips // 2
    line = [
        {"dp": lax.rem(me + 4 * d, 4 * depth)} for d in range(1, depth)
    ]
    over = {"dp": me + 2 - 4 * odd}
    for other in (*beside, mate, opposite, *line, over):
        pl.semaphore_signal(
            barrier, inc=1, device_id=other, device_id_type=pl.DeviceIdType.MESH
        )

    units = (up.shape[0] // 16, down.shape[1] // BLOCK)
    grain = (16, BLOCK)
    parts = []
    for a in range(2):
        side = units[a] * 5 // 16
        size, head = side * grain[a], (units[a] - 2 * side) * grain[a]
        mine = pl.multiple_of(head + group * size, grain[a])
        theirs = pl.multiple_of(head + (1 - group) * size, grain[a])
        parts.append(((mine, size), (0, head), (theirs, size)))

    def view(a, ref, part):
        if part is None:
            return ref
        start, size = parts[a][part]
        return ref.at[pl.ds(start, size)] if a == 0 else ref.at[:, pl.ds(start, size)]

    ins, full = (up, down), (ups, downs)

    def remote(a, source, slot, part, sems, target):
        return pltpu.make_async_remote_copy(
            src_ref=view(a, source, part),
            dst_ref=view(a, full[a].at[slot], part),
            send_sem=sems[0],
            recv_sem=sems[1],
            device_id=target,
            device_id_type=pl.DeviceIdType.MESH,
        )

    def came(way, hop):
        return 2 * chip_at(place - (1 + hop) * turn * (1 - 2 * way)) + core

    def ring(a, way, hop, part):
        slot = me if hop == 0 else came(way, hop - 1)
        source = ins[a] if hop == 0 else full[a].at[slot]
        at = (a, way, hop, part)
        return remote(a, source, slot, part, (ring_send.at[at], ring_recv.at[at]), beside[way])

    def swap(a, way, hop):
        slot = came(way, hop)
        at = (a, way * half + hop)
        return remote(a, full[a].at[slot], slot, 0, (x_send.at[at], x_recv.at[at]), opposite)

    def share(a, way, hop, part):
        slot = came(way, hop)
        at = (a, 1 + way * half + hop, part)
        return remote(
            a, full[a].at[slot], slot, part, (core_send.at[at], core_recv.at[at]), mate
        )

    def share_own(a):
        at = (a, 0, 0)
        return remote(a, ins[a], me, None, (core_send.at[at], core_recv.at[at]), mate)

    own = [pltpu.make_async_copy(ins[a], full[a].at[me], own_sem.at[a]) for a in range(2)]
    started = []

    def go(copy):
        copy.start()
        started.append(copy)

    def ways(hop):
        return [way for way in range(2) if 0 <= hop < steps[way]]

    def pass_on(a, hop, part):
        for way in ways(hop):
            ring(a, way, hop, part).wait_recv()
            if hop + 1 < steps[way]:
                go(ring(a, way, hop + 1, part))
            if part == 0:
                go(swap(a, way, hop))
            go(share(a, way, hop, part))

    def take(a, hop):
        for way in ways(hop):
            arrived = remote(
                a, full[a].at[came(way, hop)], came(way, hop), 2,
                (x_send.at[a, way * half + hop], x_recv.at[a, way * half + hop]), opposite,
            )
            arrived.wait_recv()
            go(share(a, way, hop, 2))

    def settle(a, hop):
        for way in ways(hop):
            for part in range(3):
                share(a, way, hop, part).wait_recv()

    def around(hop):
        return [chip_at(place - (1 + hop) * turn * (1 - 2 * way)) for way in ways(hop)]

    count, width = tokens.shape
    tile = 256
    over_last = (((1,), (1,)), ((), ()))

    def expand(q):
        size = up.shape[1]

        def one(s, carry):
            slot = 2 * q + s
            weights = ups.at[slot]

            total = 0.0
            for i in range(count // tile):
                before = bias[slot] + jnp.dot(
                    normed[i * tile : (i + 1) * tile, :],
                    weights[...],
                    preferred_element_type=jnp.float32,
                )
                hidden = 0.5 * before * (1.0 + lax.erf(before * math.sqrt(0.5)))
                total += jnp.dot(
                    select[i], hidden.astype(normed.dtype), preferred_element_type=jnp.float32
                )
            sums[:, pl.ds(pl.multiple_of(slot * size, BLOCK), size)] = total.astype(
                sums.dtype
            )
            return carry

        lax.fori_loop(0, 2, one, 0)

    def contract(q):
        weights = downs[pl.ds(2 * q, 2)].reshape(2 * down.shape[0], down.shape[1])
        at = pl.ds(pl.multiple_of(q * BLOCK, BLOCK), BLOCK)
        total = lax.dot_general(
            sums[...], weights, over_last, preferred_element_type=jnp.float32
        )
        labels = jnp.zeros((select.shape[1], 1), jnp.float32)
        for i in range(count // tile):
            rows = slice(i * tile, (i + 1) * tile)
            total += jnp.dot(select[i], tokens[rows, at], preferred_element_type=jnp.float32)
            labels += jnp.sum(select[i].astype(jnp.float32), axis=1, keepdims=True)
        pooled[:, at] = (total / jnp.maximum(labels, 1.0)).astype(pooled.dtype)

    arguments = [
        pltpu.make_async_copy(source, target, in_sem.at[i])
        for i, (source, target) in enumerate(
            (
                (tokens_in, tokens),
                (mask_in, mask),
                (spans_in, spans),
                (gain_in, gain),
                (shift_in, shift),
                (bias_in, bias),
            )
        )
    ]
    for copy in arguments:
        copy.start()
    pl.semaphore_wait(barrier, 4 + depth)
    for a in range(2):
        for part in range(2):
            for way in range(2):
                go(ring(a, way, 0, part))
        go(share_own(a))
    for copy in own:
        copy.start()
    for copy in arguments:
        copy.wait()

    for i in range(count // tile):
        rows = slice(i * tile, (i + 1) * tile)
        values = tokens[rows, :].astype(jnp.float32)
        center = jnp.mean(values, axis=1, keepdims=True)
        spread_of = jnp.mean((values - center) ** 2, axis=1, keepdims=True)
        normed[rows, :] = (
            (values - center) * lax.rsqrt(spread_of + 1e-05) * gain[...] + shift[...]
        ).astype(normed.dtype)
        labels = lax.broadcasted_iota(jnp.int32, (select.shape[1], tile), 0)
        select[i] = jnp.where(
            (spans[:, rows] == labels) & (mask[:, rows] == 1), 1.0, 0.0
        ).astype(select.dtype)

    for hop in range(half):
        for part in range(2):
            pass_on(0, hop, part)
        if hop == 0:
            for copy in own:
                copy.wait()
            share_own(0).wait_recv()
            expand(chip)
        take(1, hop - 1)
        for q in around(hop - 1)[1:]:
            expand(q)
        pass_on(1, hop, 0)
        if hop + 1 < half:
            pass_on(1, hop, 1)
        take(0, hop)
        settle(0, hop)
        expand(around(hop)[0])
    last = half - 1
    share_own(1).wait_recv()
    contract(chip)
    for hop in range(last):
        settle(1, hop)
        for q in around(hop):
            contract(q)
    pass_on(1, last, 1)
    take(1, last)
    settle(1, last)
    for q in around(last):
        contract(q)
    for copy in started:
        copy.wait_send()


def whole_kernel(chips, scale, *refs):
    ins, out, pooled, first, second = refs[:8], refs[8], refs[9], refs[10:29], refs[29:]
    weights_kernel(chips, *ins, pooled, *first)
    whiten_ring_kernel(scale, pooled, out, *second)


def whitened_spans(tokens, token_mask, span_ids, norm_gain, norm_shift, up, b_up, down):
    devices = lax.axis_size("dp")
    chips, depth = devices // 2, devices // 4
    count, width = tokens.shape
    chunks = width // BLOCK
    kind = tokens.dtype
    dma = pltpu.SemaphoreType.DMA
    vmem = pltpu.VMEM
    first = [
        vmem(tokens.shape, kind),
        vmem(token_mask.shape, token_mask.dtype),
        vmem(span_ids.shape, span_ids.dtype),
        vmem((1, width), norm_gain.dtype),
        vmem((1, width), norm_shift.dtype),
        vmem((devices, 1, up.shape[1]), b_up.dtype),
        vmem((devices,) + up.shape, up.dtype),
        vmem((devices,) + down.shape, down.dtype),
        vmem((count, width), kind),
        vmem((count // 256, SEG_DEV, 256), kind),
        vmem((SEG_DEV, b_up.shape[0]), kind),
        dma((2, 2, chips // 2, 2)),
        dma((2, 2, chips // 2, 2)),
        dma((2, chips)),
        dma((2, chips)),
        dma((2, chips, 3)),
        dma((2, chips, 3)),
        dma((2,)),
        dma((6,)),
    ]
    second = [
        vmem((chunks, 2, 2, depth, SEG_DEV, BLOCK), kind),
        vmem((width, width), jnp.bfloat16),
        vmem((width, width), jnp.bfloat16),
        vmem((width, BLOCK), jnp.bfloat16),
        vmem((width, BLOCK), jnp.bfloat16),
        vmem((BLOCK, width), jnp.float32),
        vmem((BLOCK, BLOCK), jnp.float32),
        vmem((BLOCK, BLOCK), jnp.float32),
        dma((chunks, depth - 1)),
        dma((chunks, depth - 1)),
        dma((chunks, depth)),
        dma((chunks, depth)),
        dma((chunks, 2)),
        dma((chunks, 2)),
    ]
    return pl.pallas_call(
        functools.partial(whole_kernel, chips, math.sqrt(SEG_DEV * devices)),
        out_shape=jax.ShapeDtypeStruct((SEG_DEV, width), jnp.float32),
        in_specs=[pl.BlockSpec(memory_space=pl.ANY)] * 8,
        out_specs=pl.BlockSpec(memory_space=pltpu.VMEM),
        scratch_shapes=[vmem((SEG_DEV, width), kind)] + first + second,
        compiler_params=pltpu.CompilerParams(
            collective_id=0, has_side_effects=True, vmem_limit_bytes=60 << 20
        ),
    )(
        tokens,
        token_mask,
        span_ids,
        norm_gain.reshape(1, -1),
        norm_shift.reshape(1, -1),
        b_up.reshape(devices, 1, -1),
        up,
        down,
    )


def on_device(tokens, token_mask, span_ids, norm_gain, norm_shift, w_up, b_up, w_down):
    if lax.axis_size("dp") == 16 and lax.axis_size("groups") == 2:
        return whitened_spans(
            tokens, token_mask, span_ids, norm_gain, norm_shift, w_up, b_up, w_down.T
        )
    values = tokens.astype(jnp.float32)
    center = jnp.mean(values, axis=1, keepdims=True)
    spread = jnp.mean((values - center) ** 2, axis=1, keepdims=True)
    normed = ((values - center) * lax.rsqrt(spread + 1e-05) * norm_gain + norm_shift).astype(
        jnp.bfloat16
    )
    width, hidden_size = tokens.shape[1], b_up.shape[0]
    over_last = (((1,), (1,)), ((), ()))
    if w_up.shape[1] % BLOCK == 0:
        hidden, down_full = ring_up(normed, b_up, w_up.T, w_down.T, 0)
    else:
        up_full, down_full = ring_gather((w_up.T, w_down.T), 0)
        up_full = up_full.reshape(hidden_size, width)
        before = (
            lax.dot_general(normed, up_full, over_last, preferred_element_type=jnp.float32) + b_up
        )
        hidden = jax.nn.gelu(before, approximate=False).astype(jnp.bfloat16)
    down_full = down_full.reshape(width, hidden_size)
    projected = lax.dot_general(
        hidden, down_full, over_last, preferred_element_type=jnp.float32
    )
    block_out = (values + projected).astype(jnp.bfloat16)
    labels = jnp.arange(SEG_DEV, dtype=jnp.int32)[:, None]
    select = (span_ids[0][None, :] == labels) & (token_mask[0][None, :] == 1)
    sums = jnp.dot(select.astype(jnp.bfloat16), block_out, preferred_element_type=jnp.float32)
    counts = jnp.sum(select.astype(jnp.float32), axis=1)
    pooled = (sums / jnp.maximum(counts, 1.0)[:, None]).astype(jnp.bfloat16)
    middle = width // 2
    left, right = (
        half.reshape(-1, middle)
        for half in ring_gather((pooled[:, :middle], pooled[:, middle:]), 1)
    )
    gram = [
        lax.dot_general(one, two, (((0,), (0,)), ((), ())), preferred_element_type=jnp.float32)
        for one, two in ((left, left), (left, right), (right, right))
    ]
    total_rows = SEG_DEV * lax.axis_size("dp")
    return whiten(gram, pooled.astype(jnp.float32).T, math.sqrt(total_rows)).T


def solution(mesh):
    in_specs = (
        P(("groups", "dp"), None),
        P(("groups", "dp"), None),
        P(("groups", "dp"), None),
        P(),
        P(),
        P(None, "dp"),
        P(),
        P(None, "dp"),
    )
    out_specs = P(("groups", "dp"), None)
    return jax.shard_map(
        on_device, mesh=mesh, in_specs=in_specs, out_specs=out_specs, check_vma=False
    )
```

```python
import functools
import math

import jax
import jax.numpy as jnp
from jax import lax
from jax.experimental import pallas as pl
from jax.experimental.pallas import tpu as pltpu
from jax.sharding import PartitionSpec as P

SEG_DEV = 192
BLOCK = 128
HIGHEST = lax.Precision.HIGHEST


def inverse_block(src, dst):
    lane = lax.broadcasted_iota(jnp.int32, (8, BLOCK), 1)
    sub = lax.broadcasted_iota(jnp.int32, (8, BLOCK), 0)
    groups = BLOCK // 8
    held = [src[8 * q : 8 * q + 8, :BLOCK] for q in range(groups)]

    def column(block, c):
        return jnp.broadcast_to(block[:, c : c + 1], (8, BLOCK))

    def row(block, r):
        return jnp.broadcast_to(block[r : r + 1, :], (8, BLOCK))

    for p in range(groups):
        at = 8 * p
        inside = (lane >= at) & (lane < at + 8)
        raw = held[p]
        cols = [column(raw, at + c) for c in range(8)]
        work = jnp.where(inside, jnp.where(lane - at == sub, 1.0, 0.0), raw)
        done = jnp.zeros((8, BLOCK), jnp.float32)
        for j in range(8):
            here = sub == j
            pivot = row(cols[j], j)
            inv = 1.0 / pivot
            done = jnp.where(here, work * lax.rsqrt(pivot), done)
            scaled = row(work, j) * inv
            work = jnp.where(here, scaled, work - cols[j] * scaled)
            for c in range(j + 1, 8):
                scaled = row(cols[c], j) * inv
                cols[c] = jnp.where(here, scaled, cols[c] - cols[j] * scaled)
        dst[at : at + 8, :] = jnp.where(lane <= at + sub, done, 0.0)
        rows = [row(work, c) for c in range(8)]
        for q in range(p + 1, groups):
            total = jnp.where(inside, 0.0, held[q])
            for c in range(8):
                total = total - column(held[q], at + c) * rows[c]
            held[q] = total


def whiten_kernel(scale, first_ref, cross_ref, last_ref, rows_ref, out_ref, a, panel, inv):
    half = first_ref.shape[0]
    n = 2 * half
    extra = rows_ref.shape[1]
    a[:half, :half] = first_ref[...]
    a[:half, half:n] = cross_ref[...]
    a[half:, :half] = jnp.zeros((half, half), jnp.float32)
    a[half:, half:n] = last_ref[...]
    a[:, n:] = jnp.zeros((n, a.shape[1] - n), jnp.float32)
    a[:, n : n + extra] = rows_ref[...]
    blocks = n // BLOCK

    def step(k, carry):
        lo = pl.multiple_of(k * BLOCK, BLOCK)
        panel[:, :BLOCK] = a[pl.ds(lo, BLOCK), pl.ds(lo, BLOCK)]
        inverse_block(panel, inv)
        panel[...] = jnp.dot(
            inv[...], a[pl.ds(lo, BLOCK), :], preferred_element_type=jnp.float32, precision=HIGHEST
        )
        out_ref[pl.ds(lo, BLOCK), :] = panel[:, n : n + extra] * scale

        for first in range(0, blocks, 2):
            start = first * BLOCK

            def trail(i, carry, start=start):
                hi = pl.multiple_of(i * BLOCK, BLOCK)
                left = panel[:, pl.ds(hi, BLOCK)].T
                a[pl.ds(hi, BLOCK), start:] -= jnp.dot(
                    left, panel[:, start:], preferred_element_type=jnp.float32, precision=HIGHEST
                )
                return carry

            lax.fori_loop(jnp.maximum(k + 1, first), min(first + 2, blocks), trail, 0)
        return carry

    lax.fori_loop(0, blocks, step, 0)


def whiten(gram, rows_t, scale):
    n, extra = rows_t.shape
    wide = n + (extra + BLOCK - 1) // BLOCK * BLOCK
    return pl.pallas_call(
        functools.partial(whiten_kernel, scale),
        out_shape=jax.ShapeDtypeStruct((n, extra), jnp.float32),
        in_specs=[pl.BlockSpec(memory_space=pltpu.VMEM)] * 4,
        out_specs=pl.BlockSpec(memory_space=pltpu.VMEM),
        scratch_shapes=[
            pltpu.VMEM((n, wide), jnp.float32),
            pltpu.VMEM((BLOCK, wide), jnp.float32),
            pltpu.VMEM((BLOCK, BLOCK), jnp.float32),
        ],
        compiler_params=pltpu.CompilerParams(vmem_limit_bytes=32 << 20),
    )(*gram, rows_t)


def ring_kernel(chips, count, fused, *refs):
    if fused:
        normed, bias, up, down, hidden, down_out, up_out = refs[:7]
        ins, outs, refs = (up, down), (up_out, down_out), refs[7:]
    else:
        ins, outs, refs = refs[:count], refs[count : 2 * count], refs[2 * count :]
    ring_send, ring_recv, core_send, core_recv, own_sem = refs
    me = lax.axis_index("dp")
    core, chip = lax.rem(me, 2), me // 2
    half = chips // 2
    odd = lax.rem(chip, 2)
    place = (1 - odd) * (chip // 2) + odd * (chips - 1 - chip // 2)
    turn = 1 - 2 * core
    partner = me + turn

    def device(q):
        q = lax.rem(q + 2 * chips, chips)
        back = q // half
        return 2 * ((1 - back) * 2 * q + back * (2 * (chips - 1 - q) + 1)) + core

    ahead, behind = device(place + turn), device(place - turn)
    barrier = pltpu.get_barrier_semaphore()
    for other in (ahead, behind, partner):
        pl.semaphore_signal(
            barrier, inc=1, device_id={"dp": other}, device_id_type=pl.DeviceIdType.MESH
        )
    pl.semaphore_wait(barrier, 3)

    steps = (half, chips - 1 - half)
    started, across = [], []

    def send(a, source, slot, way, step):
        copy = pltpu.make_async_remote_copy(
            src_ref=source,
            dst_ref=outs[a].at[slot],
            send_sem=ring_send.at[a, way, step],
            recv_sem=ring_recv.at[a, way, step],
            device_id={"dp": (ahead, behind)[way]},
            device_id_type=pl.DeviceIdType.MESH,
        )
        copy.start()
        started.append(copy)
        return copy

    def share(a, source, slot, index):
        copy = pltpu.make_async_remote_copy(
            src_ref=source,
            dst_ref=outs[a].at[slot],
            send_sem=core_send.at[a, index],
            recv_sem=core_recv.at[a, index],
            device_id={"dp": partner},
            device_id_type=pl.DeviceIdType.MESH,
        )
        copy.start()
        if fused and a == 0:
            first[index] = copy
        else:
            across.append(copy)

    def compute(slot, block):
        size = block.shape[0]
        columns = pl.ds(pl.multiple_of(slot * size, BLOCK), size)
        tile = normed.shape[0] // 3

        def part(t, carry):
            at = pl.ds(pl.multiple_of(t * tile, tile), tile)
            before = lax.dot_general(
                normed[at, :],
                block[...],
                (((1,), (1,)), ((), ())),
                preferred_element_type=jnp.float32,
            )
            before = before + bias[slot]
            hidden[at, columns] = (
                0.5 * before * (1.0 + lax.erf(before * math.sqrt(0.5)))
            ).astype(hidden.dtype)
            return carry

        lax.fori_loop(0, 3, part, 0)

    first = {}

    def partner_block(index, step, way):
        first[index].wait_recv()
        slot = partner
        if index:
            slot = device(place + (1 + step) * turn * (1 - 2 * way)) + turn
        compute(slot, outs[0].at[slot])

    flying, local = {}, []
    for a in range(count):
        for way in range(2):
            flying[a, way] = send(a, ins[a], me, way, 0)
        share(a, ins[a], me, 0)
        if not (fused and a == 0):
            local.append(pltpu.make_async_copy(ins[a], outs[a].at[me], own_sem.at[a]))
            local[-1].start()
    if fused:
        compute(me, ins[0])
    for step in range(half):
        landed = []
        if fused:
            if step == 0:
                partner_block(0, 0, 0)
            for way in range(2):
                if 0 < step <= steps[way]:
                    partner_block(way * half + step, step - 1, way)
        for a in range(count):
            for way in range(2):
                if step >= steps[way]:
                    continue
                flying[a, way].wait_recv()
                slot = device(place - (1 + step) * turn * (1 - 2 * way))
                block = outs[a].at[slot]
                if step + 1 < steps[way]:
                    flying[a, way] = send(a, block, slot, way, step + 1)
                share(a, block, slot, 1 + way * half + step)
                if fused and a == 0:
                    landed.append((slot, block))
        for slot, block in landed:
            compute(slot, block)
    if fused:
        for way in range(2):
            if steps[way] == half:
                partner_block(way * half + half, half - 1, way)
        for copy in first.values():
            copy.wait_send()
    for copy in local:
        copy.wait()
    for copy in started:
        copy.wait_send()
    for copy in across:
        copy.wait()


def ring_gather(blocks, collective_id):
    devices = lax.axis_size("dp")
    chips, count = devices // 2, len(blocks)
    dma = pltpu.SemaphoreType.DMA
    return pl.pallas_call(
        functools.partial(ring_kernel, chips, count, False),
        out_shape=[jax.ShapeDtypeStruct((devices,) + b.shape, b.dtype) for b in blocks],
        in_specs=[pl.BlockSpec(memory_space=pl.ANY)] * count,
        out_specs=[pl.BlockSpec(memory_space=pl.ANY)] * count,
        scratch_shapes=[
            dma((count, 2, chips // 2)),
            dma((count, 2, chips // 2)),
            dma((count, chips)),
            dma((count, chips)),
            dma((count,)),
        ],
        compiler_params=pltpu.CompilerParams(collective_id=collective_id, has_side_effects=True),
    )(*blocks)


def ring_up(normed, bias, up, down, collective_id):
    devices = lax.axis_size("dp")
    chips = devices // 2
    dma = pltpu.SemaphoreType.DMA
    whole = pl.BlockSpec(memory_space=pltpu.VMEM)
    apart = pl.BlockSpec(memory_space=pl.ANY)
    return pl.pallas_call(
        functools.partial(ring_kernel, chips, 2, True),
        out_shape=[
            jax.ShapeDtypeStruct((normed.shape[0], devices * up.shape[0]), normed.dtype),
            jax.ShapeDtypeStruct((devices,) + down.shape, down.dtype),
        ],
        in_specs=[whole, whole, whole, apart],
        out_specs=[whole, apart],
        scratch_shapes=[
            pltpu.VMEM((devices,) + up.shape, up.dtype),
            dma((2, 2, chips // 2)),
            dma((2, 2, chips // 2)),
            dma((2, chips)),
            dma((2, chips)),
            dma((2,)),
        ],
        compiler_params=pltpu.CompilerParams(
            collective_id=collective_id, has_side_effects=True, vmem_limit_bytes=40 << 20
        ),
    )(normed, bias.reshape(devices, 1, -1), up, down)


def spread(block, r):
    return jnp.broadcast_to(block[r : r + 1, :], (8, BLOCK))


def strip_factor(a, dst, base, groups):
    lane = lax.broadcasted_iota(jnp.int32, (8, BLOCK), 1)
    sub = lax.broadcasted_iota(jnp.int32, (8, BLOCK), 0)
    h = [a[base + 8 * q : base + 8 * q + 8, :] for q in range(groups)]

    def fetch(p):
        return {
            (c, q): jnp.broadcast_to(
                h[q][:, base + 8 * p + c : base + 8 * p + c + 1], (8, BLOCK)
            )
            for q in range(p, groups)
            for c in range(8)
        }

    cols = fetch(0)
    for p in range(groups):
        more = p + 1 < groups
        following = fetch(p + 1) if more else {}
        at = base + 8 * p
        inside = (lane >= at) & (lane < at + 8)
        work = jnp.where(inside, jnp.where(lane - at == sub, 1.0, 0.0), h[p])
        for q in range(p + 1, groups):
            h[q] = jnp.where(inside, 0.0, h[q])
        pivots = jnp.zeros((8, BLOCK), jnp.float32)
        for j in range(8):
            pivot = spread(cols[j, p], j)
            inv = 1.0 / pivot
            pivots = jnp.where(sub == j, pivot, pivots)
            for c in range(j + 1, 8):
                m = spread(cols[j, p], c) * inv
                for q in range(p, groups):
                    cols[c, q] = cols[c, q] - cols[j, q] * m
            if more:
                for c in range(8):
                    m = spread(cols[j, p + 1], c) * inv
                    for q in range(p + 1, groups):
                        following[c, q] = following[c, q] - cols[j, q] * m
            scaled = spread(work, j) * inv
            if j < 7:
                work = work - jnp.where(sub > j, cols[j, p], 0.0) * scaled
            for q in range(p + 1, groups):
                h[q] = h[q] - cols[j, q] * scaled
        dst[at : at + 8, :] = work * lax.rsqrt(pivots)
        cols = following


def over_rows(left, right, precision=None):
    return lax.dot_general(
        left,
        right,
        (((0,), (0,)), ((), ())),
        preferred_element_type=jnp.float32,
        precision=precision,
    )


def inverse_factor(a, dst, between):
    size = 32
    for base in range(0, BLOCK, size):
        strip_factor(a, dst, base, size // 8)
        between(base // size)
        lo = base + size
        if lo < BLOCK:
            rows = dst[base:lo, :]
            r = lax.broadcasted_iota(jnp.int32, (size, BLOCK), 0) + base
            c = lax.broadcasted_iota(jnp.int32, (size, BLOCK), 1)
            one, two = split(rows)
            high, low = split(jnp.where((c > r) & (c < lo), 0.0, rows))
            drop = over_rows(one, high) + (over_rows(one, low) + over_rows(two, high))
            c = lax.broadcasted_iota(jnp.int32, (BLOCK - lo, BLOCK), 1)
            a[lo:, :] = jnp.where((c >= base) & (c < lo), 0.0, a[lo:, :]) - drop[lo:, :]
    r = lax.broadcasted_iota(jnp.int32, (BLOCK, BLOCK), 0)
    c = lax.broadcasted_iota(jnp.int32, (BLOCK, BLOCK), 1)
    dst[...] = jnp.where(c <= r, dst[...], 0.0)


def product(left, right):
    return jnp.dot(left, right, preferred_element_type=jnp.float32)


def split(x):
    high = x.astype(jnp.bfloat16)
    return high, (x - high.astype(jnp.float32)).astype(jnp.bfloat16)


def whiten_ring_kernel(
    scale, own, out, land, high, low, r_high, r_low, t, a, w, z_send, z_recv, y_send, y_recv, core_send, core_recv
):
    me = lax.axis_index("dp")
    core, y, z = lax.rem(me, 2), lax.rem(me // 2, 2), me // 4
    depth = land.shape[3]
    chunks = own.shape[1] // BLOCK
    rows = own.shape[0]
    total = 4 * depth * rows
    partner, across = me + 1 - 2 * core, me + 2 - 4 * y
    line = [lax.rem(z + d, depth) for d in range(1, depth)]

    others = [4 * other + 2 * y + core for other in line] + [partner, across]

    def remote(ref, send_sem, recv_sem, target):
        return pltpu.make_async_remote_copy(
            src_ref=ref,
            dst_ref=ref,
            send_sem=send_sem,
            recv_sem=recv_sem,
            device_id={"dp": target},
            device_id_type=pl.DeviceIdType.MESH,
        )

    def along(c, d):
        return remote(land.at[c, y, core, z], z_send.at[c, d], z_recv.at[c, d], others[d])

    def over(c, d):
        slot = z if d == depth - 1 else lax.rem(z + depth - 1 - d, depth)
        return remote(land.at[c, y, core, slot], y_send.at[c, d], y_recv.at[c, d], across)

    def share(c, side):
        ref = land.at[c, (1 - y) if side else y, core]
        return remote(ref, core_send.at[c, side], core_recv.at[c, side], partner)

    def begin(c):
        for d in range(depth - 1):
            along(c, d).start()
        over(c, depth - 1).start()

    def first(c):
        for d in range(depth - 1):
            along(c, d).wait_recv()
            over(c, d).start()
        share(c, 0).start()

    def second(c):
        for d in range(depth):
            over(c, d).wait_recv()
        share(c, 1).start()

    def guarded(c, what):
        pl.when(c < chunks)(lambda: what(c))

    for c in range(chunks):
        land[c, y, core, z] = own[:, c * BLOCK : (c + 1) * BLOCK]
    begin(0)
    begin(1)
    for ref in (high, low, r_high, r_low):
        ref[...] = jnp.zeros(ref.shape, ref.dtype)
    first(0)
    begin(2)
    first(1)
    second(0)

    def gathered(c):
        return land[c].reshape(total, BLOCK)

    def before(k):
        n = k * BLOCK
        top = [over_rows(gathered(m), gathered(k)) for m in range(k)]
        corner = over_rows(gathered(k), gathered(k))
        if k:
            c_high, c_low = split(jnp.concatenate(top, axis=0))
            r = product(high[:n, :n], c_high) + (
                product(high[:n, :n], c_low) + product(low[:n, :n], c_high)
            )
            one, two = split(r)
            r_high[:n, :] = one
            r_low[:n, :] = two
            corner -= over_rows(one, one) + (over_rows(one, two) + over_rows(two, one))
        a[...] = corner

    def between(s):
        size = t.shape[1] // 4
        at = slice(s * size, (s + 1) * size)
        t[:, at] = over_rows(r_high[...], high[:, at]) + (
            over_rows(r_high[...], low[:, at]) + over_rows(r_low[...], high[:, at])
        )

    def after(k):
        at = pl.ds(pl.multiple_of(k * BLOCK, BLOCK), BLOCK)
        w_high, w_low = split(w[...])
        t_high, t_low = split(t[...])
        left = product(w_high, t_high) + (product(w_high, t_low) + product(w_low, t_high))
        one, two = split(-left)
        high[at, :] = one
        low[at, :] = two
        high[at, at] = w_high
        low[at, at] = w_low
        both = sum(
            lax.dot_general(
                own[...],
                part,
                (((1,), (1,)), ((), ())),
                preferred_element_type=jnp.float32,
            )
            for part in (high[at, :], low[at, :])
        )
        out[:, at] = both * scale

    def step(k, carry):
        for side in range(2):
            share(k, side).wait_recv()
        guarded(k + 3, begin)
        for i in range(chunks):
            pl.when(k == i)(functools.partial(before, i))
        guarded(k + 2, first)
        inverse_factor(a, w, between)
        guarded(k + 1, second)
        after(k)
        return carry

    lax.fori_loop(0, chunks, step, 0)

    def finish(c, carry):
        for d in range(depth - 1):
            along(c, d).wait_send()
        for d in range(depth):
            over(c, d).wait_send()
        for side in range(2):
            share(c, side).wait_send()
        return carry

    lax.fori_loop(0, chunks, finish, 0)


def weights_kernel(
    chips, tokens_in, mask_in, spans_in, gain_in, shift_in, bias_in, up, down, pooled,
    tokens, mask, spans, gain, shift, bias, ups, downs, normed, select, sums, ring_send, ring_recv, x_send, x_recv,
    core_send, core_recv, own_sem, in_sem,
):
    me, group = lax.axis_index("dp"), lax.axis_index("groups")
    core, chip = lax.rem(me, 2), me // 2
    half = chips // 2
    odd = lax.rem(chip, 2)
    place = (1 - odd) * (chip // 2) + odd * (chips - 1 - chip // 2)
    turn = 1 - 2 * core
    partner = me + turn
    steps = (half, chips - 1 - half)

    def chip_at(q):
        q = lax.rem(q + 2 * chips, chips)
        back = q // half
        return (1 - back) * 2 * q + back * (2 * (chips - 1 - q) + 1)

    beside = [{"dp": 2 * chip_at(place + d) + core} for d in (turn, -turn)]
    mate, opposite = {"dp": partner}, {"groups": 1 - group}
    barrier = pltpu.get_barrier_semaphore()
    depth = chips // 2
    line = [
        {"dp": lax.rem(me + 4 * d, 4 * depth)} for d in range(1, depth)
    ]
    over = {"dp": me + 2 - 4 * odd}
    for other in (*beside, mate, opposite, *line, over):
        pl.semaphore_signal(
            barrier, inc=1, device_id=other, device_id_type=pl.DeviceIdType.MESH
        )

    units = (up.shape[0] // 16, down.shape[1] // BLOCK)
    grain = (16, BLOCK)
    parts = []
    for a in range(2):
        side = units[a] * 5 // 16
        size, head = side * grain[a], (units[a] - 2 * side) * grain[a]
        mine = pl.multiple_of(head + group * size, grain[a])
        theirs = pl.multiple_of(head + (1 - group) * size, grain[a])
        parts.append(((mine, size), (0, head), (theirs, size)))

    def view(a, ref, part):
        if part is None:
            return ref
        start, size = parts[a][part]
        return ref.at[pl.ds(start, size)] if a == 0 else ref.at[:, pl.ds(start, size)]

    ins, full = (up, down), (ups, downs)

    def remote(a, source, slot, part, sems, target):
        return pltpu.make_async_remote_copy(
            src_ref=view(a, source, part),
            dst_ref=view(a, full[a].at[slot], part),
            send_sem=sems[0],
            recv_sem=sems[1],
            device_id=target,
            device_id_type=pl.DeviceIdType.MESH,
        )

    def came(way, hop):
        return 2 * chip_at(place - (1 + hop) * turn * (1 - 2 * way)) + core

    def ring(a, way, hop, part):
        slot = me if hop == 0 else came(way, hop - 1)
        source = ins[a] if hop == 0 else full[a].at[slot]
        at = (a, way, hop, part)
        return remote(a, source, slot, part, (ring_send.at[at], ring_recv.at[at]), beside[way])

    def swap(a, way, hop):
        slot = came(way, hop)
        at = (a, way * half + hop)
        return remote(a, full[a].at[slot], slot, 0, (x_send.at[at], x_recv.at[at]), opposite)

    def share(a, way, hop, part):
        slot = came(way, hop)
        at = (a, 1 + way * half + hop, part)
        return remote(
            a, full[a].at[slot], slot, part, (core_send.at[at], core_recv.at[at]), mate
        )

    def share_own(a):
        at = (a, 0, 0)
        return remote(a, ins[a], me, None, (core_send.at[at], core_recv.at[at]), mate)

    own = [pltpu.make_async_copy(ins[a], full[a].at[me], own_sem.at[a]) for a in range(2)]
    started = []

    def go(copy):
        copy.start()
        started.append(copy)

    def ways(hop):
        return [way for way in range(2) if 0 <= hop < steps[way]]

    def pass_on(a, hop, part):
        for way in ways(hop):
            ring(a, way, hop, part).wait_recv()
            if hop + 1 < steps[way]:
                go(ring(a, way, hop + 1, part))
            if part == 0:
                go(swap(a, way, hop))
            go(share(a, way, hop, part))

    def take(a, hop):
        for way in ways(hop):
            arrived = remote(
                a, full[a].at[came(way, hop)], came(way, hop), 2,
                (x_send.at[a, way * half + hop], x_recv.at[a, way * half + hop]), opposite,
            )
            arrived.wait_recv()
            go(share(a, way, hop, 2))

    def settle(a, hop):
        for way in ways(hop):
            for part in range(3):
                share(a, way, hop, part).wait_recv()

    def around(hop):
        return [chip_at(place - (1 + hop) * turn * (1 - 2 * way)) for way in ways(hop)]

    count, width = tokens.shape
    tile = 256
    over_last = (((1,), (1,)), ((), ()))

    def expand(q):
        size = up.shape[1]

        def one(s, carry):
            slot = 2 * q + s
            weights = ups.at[slot]

            total = 0.0
            for i in range(count // tile):
                before = bias[slot] + jnp.dot(
                    normed[i * tile : (i + 1) * tile, :],
                    weights[...],
                    preferred_element_type=jnp.float32,
                )
                hidden = 0.5 * before * (1.0 + lax.erf(before * math.sqrt(0.5)))
                total += jnp.dot(
                    select[i], hidden.astype(normed.dtype), preferred_element_type=jnp.float32
                )
            sums[:, pl.ds(pl.multiple_of(slot * size, BLOCK), size)] = total.astype(
                sums.dtype
            )
            return carry

        lax.fori_loop(0, 2, one, 0)

    def contract(q):
        weights = downs[pl.ds(2 * q, 2)].reshape(2 * down.shape[0], down.shape[1])
        at = pl.ds(pl.multiple_of(q * BLOCK, BLOCK), BLOCK)
        total = lax.dot_general(
            sums[...], weights, over_last, preferred_element_type=jnp.float32
        )
        labels = jnp.zeros((select.shape[1], 1), jnp.float32)
        for i in range(count // tile):
            rows = slice(i * tile, (i + 1) * tile)
            total += jnp.dot(select[i], tokens[rows, at], preferred_element_type=jnp.float32)
            labels += jnp.sum(select[i].astype(jnp.float32), axis=1, keepdims=True)
        pooled[:, at] = (total / jnp.maximum(labels, 1.0)).astype(pooled.dtype)

    arguments = [
        pltpu.make_async_copy(source, target, in_sem.at[i])
        for i, (source, target) in enumerate(
            (
                (tokens_in, tokens),
                (mask_in, mask),
                (spans_in, spans),
                (gain_in, gain),
                (shift_in, shift),
                (bias_in, bias),
            )
        )
    ]
    for copy in arguments:
        copy.start()
    pl.semaphore_wait(barrier, 4 + depth)
    for a in range(2):
        for part in range(2):
            for way in range(2):
                go(ring(a, way, 0, part))
        go(share_own(a))
    for copy in own:
        copy.start()
    for copy in arguments:
        copy.wait()

    for i in range(count // tile):
        rows = slice(i * tile, (i + 1) * tile)
        values = tokens[rows, :].astype(jnp.float32)
        center = jnp.mean(values, axis=1, keepdims=True)
        spread_of = jnp.mean((values - center) ** 2, axis=1, keepdims=True)
        normed[rows, :] = (
            (values - center) * lax.rsqrt(spread_of + 1e-05) * gain[...] + shift[...]
        ).astype(normed.dtype)
        labels = lax.broadcasted_iota(jnp.int32, (select.shape[1], tile), 0)
        select[i] = jnp.where(
            (spans[:, rows] == labels) & (mask[:, rows] == 1), 1.0, 0.0
        ).astype(select.dtype)

    for hop in range(half):
        for part in range(2):
            pass_on(0, hop, part)
        if hop == 0:
            for copy in own:
                copy.wait()
            share_own(0).wait_recv()
            expand(chip)
        take(1, hop - 1)
        for q in around(hop - 1)[1:]:
            expand(q)
        pass_on(1, hop, 0)
        if hop + 1 < half:
            pass_on(1, hop, 1)
        take(0, hop)
        settle(0, hop)
        expand(around(hop)[0])
    last = half - 1
    share_own(1).wait_recv()
    contract(chip)
    for hop in range(last):
        settle(1, hop)
        for q in around(hop):
            contract(q)
    pass_on(1, last, 1)
    take(1, last)
    settle(1, last)
    for q in around(last):
        contract(q)
    for copy in started:
        copy.wait_send()


def whole_kernel(chips, scale, *refs):
    ins, out, pooled, first, second = refs[:8], refs[8], refs[9], refs[10:29], refs[29:]
    weights_kernel(chips, *ins, pooled, *first)
    whiten_ring_kernel(scale, pooled, out, *second)


def whitened_spans(tokens, token_mask, span_ids, norm_gain, norm_shift, up, b_up, down):
    devices = lax.axis_size("dp")
    chips, depth = devices // 2, devices // 4
    count, width = tokens.shape
    chunks = width // BLOCK
    kind = tokens.dtype
    dma = pltpu.SemaphoreType.DMA
    vmem = pltpu.VMEM
    first = [
        vmem(tokens.shape, kind),
        vmem(token_mask.shape, token_mask.dtype),
        vmem(span_ids.shape, span_ids.dtype),
        vmem((1, width), norm_gain.dtype),
        vmem((1, width), norm_shift.dtype),
        vmem((devices, 1, up.shape[1]), b_up.dtype),
        vmem((devices,) + up.shape, up.dtype),
        vmem((devices,) + down.shape, down.dtype),
        vmem((count, width), kind),
        vmem((count // 256, SEG_DEV, 256), kind),
        vmem((SEG_DEV, b_up.shape[0]), kind),
        dma((2, 2, chips // 2, 2)),
        dma((2, 2, chips // 2, 2)),
        dma((2, chips)),
        dma((2, chips)),
        dma((2, chips, 3)),
        dma((2, chips, 3)),
        dma((2,)),
        dma((6,)),
    ]
    second = [
        vmem((chunks, 2, 2, depth, SEG_DEV, BLOCK), kind),
        vmem((width, width), jnp.bfloat16),
        vmem((width, width), jnp.bfloat16),
        vmem((width, BLOCK), jnp.bfloat16),
        vmem((width, BLOCK), jnp.bfloat16),
        vmem((BLOCK, width), jnp.float32),
        vmem((BLOCK, BLOCK), jnp.float32),
        vmem((BLOCK, BLOCK), jnp.float32),
        dma((chunks, depth - 1)),
        dma((chunks, depth - 1)),
        dma((chunks, depth)),
        dma((chunks, depth)),
        dma((chunks, 2)),
        dma((chunks, 2)),
    ]
    return pl.pallas_call(
        functools.partial(whole_kernel, chips, math.sqrt(SEG_DEV * devices)),
        out_shape=jax.ShapeDtypeStruct((SEG_DEV, width), jnp.float32),
        in_specs=[pl.BlockSpec(memory_space=pl.ANY)] * 8,
        out_specs=pl.BlockSpec(memory_space=pltpu.VMEM),
        scratch_shapes=[vmem((SEG_DEV, width), kind)] + first + second,
        compiler_params=pltpu.CompilerParams(
            collective_id=0, has_side_effects=True, vmem_limit_bytes=60 << 20
        ),
    )(
        tokens,
        token_mask,
        span_ids,
        norm_gain.reshape(1, -1),
        norm_shift.reshape(1, -1),
        b_up.reshape(devices, 1, -1),
        up,
        down,
    )


def on_device(tokens, token_mask, span_ids, norm_gain, norm_shift, w_up, b_up, w_down):
    if lax.axis_size("dp") == 16 and lax.axis_size("groups") == 2:
        return whitened_spans(
            tokens, token_mask, span_ids, norm_gain, norm_shift, w_up, b_up, w_down.T
        )
    values = tokens.astype(jnp.float32)
    center = jnp.mean(values, axis=1, keepdims=True)
    spread = jnp.mean((values - center) ** 2, axis=1, keepdims=True)
    normed = ((values - center) * lax.rsqrt(spread + 1e-05) * norm_gain + norm_shift).astype(
        jnp.bfloat16
    )
    width, hidden_size = tokens.shape[1], b_up.shape[0]
    over_last = (((1,), (1,)), ((), ()))
    if w_up.shape[1] % BLOCK == 0:
        hidden, down_full = ring_up(normed, b_up, w_up.T, w_down.T, 0)
    else:
        up_full, down_full = ring_gather((w_up.T, w_down.T), 0)
        up_full = up_full.reshape(hidden_size, width)
        before = (
            lax.dot_general(normed, up_full, over_last, preferred_element_type=jnp.float32) + b_up
        )
        hidden = jax.nn.gelu(before, approximate=False).astype(jnp.bfloat16)
    down_full = down_full.reshape(width, hidden_size)
    projected = lax.dot_general(
        hidden, down_full, over_last, preferred_element_type=jnp.float32
    )
    block_out = (values + projected).astype(jnp.bfloat16)
    labels = jnp.arange(SEG_DEV, dtype=jnp.int32)[:, None]
    select = (span_ids[0][None, :] == labels) & (token_mask[0][None, :] == 1)
    sums = jnp.dot(select.astype(jnp.bfloat16), block_out, preferred_element_type=jnp.float32)
    counts = jnp.sum(select.astype(jnp.float32), axis=1)
    pooled = (sums / jnp.maximum(counts, 1.0)[:, None]).astype(jnp.bfloat16)
    middle = width // 2
    left, right = (
        half.reshape(-1, middle)
        for half in ring_gather((pooled[:, :middle], pooled[:, middle:]), 1)
    )
    gram = [
        lax.dot_general(one, two, (((0,), (0,)), ((), ())), preferred_element_type=jnp.float32)
        for one, two in ((left, left), (left, right), (right, right))
    ]
    total_rows = SEG_DEV * lax.axis_size("dp")
    return whiten(gram, pooled.astype(jnp.float32).T, math.sqrt(total_rows)).T


def solution(mesh):
    in_specs = (
        P(("groups", "dp"), None),
        P(("groups", "dp"), None),
        P(("groups", "dp"), None),
        P(),
        P(),
        P(None, "dp"),
        P(),
        P(None, "dp"),
    )
    out_specs = P(("groups", "dp"), None)
    return jax.shard_map(
        on_device, mesh=mesh, in_specs=in_specs, out_specs=out_specs, check_vma=False
    )
```
